32 devices in a mesh: runs: 2 (over y), gx: 4 (over z), gy: 2 (over core), gz: 2 (over x).
Axes of the slice: x: 2, y: 2, z: 4, core: 2. Of those that a mesh axis runs over, the one named last changes fastest.
Arguments:
- labels: int32 [24, 128, 1024], P(('runs', 'gz'), 'gx', 'gy'), parts along dimension 0, may hold values from 0 to 3
- background: bfloat16 [24, 128, 1024], P(('runs', 'gz'), 'gx', 'gy'), parts along dimension 0, may hold values from -3 to 3
- contrasts: float32 [8], P('runs'), parts along dimension 0, may hold values from -1 to 1
- kernels: bfloat16 [24, 15, 15], P(('runs', 'gz')), parts along dimension 0, may hold values from -0.125 to 0.125
- observed: float32 [6, 128, 1024], P('runs', 'gx', 'gy'), parts along dimension 0, may hold values from -6 to 6
Outputs:
- residual: float32 [6, 128, 1024], P('runs', ('gx', 'gz'), 'gy'), parts along dimension 0
- gradient: float32 [24, 128, 1024], P(('runs', 'gz'), 'gx', 'gy'), parts along dimension 0
The draws below stay inside these ranges and needn't reach their ends.
There are 2 independent parts, one for each index of `runs`. The reference program is written for one: setup_inputs(seed, part) draws one part's arguments, and reference() takes and returns one part's arrays. A program takes and returns all parts, laid end to end along the dimension named above; each array names one. Nothing has to cross between parts.
All inputs are finite; a program needn't handle non-finite values.
Results may differ from the reference program's by a relative error of at most 0.0058.
Values may be sent and summed in bfloat16 or wider, within the bound.
No kernel may reach another device: no remote copies, remote signals or barrier semaphores. Data moves between devices by JAX's collectives and lax.ppermute only.
A program may use at most 64 MiB of HBM per device.

```python
import jax
import jax.numpy as jnp
from jax import lax

SPAN = 15
RADIUS = 7
NLAB = 4
ITERS = 2
LAYERS = 12
NX = 128
NY = 1024


def touch_ends(result, own_key, least, top_value):
    dims = result.shape
    spot = [jax.random.randint(jax.random.fold_in(own_key, axis), (), 0, dims[axis]) for axis in range(len(dims))]
    result = result.at[tuple(spot)].set(least)
    longest = dims.index(max(dims))
    spot[longest] = (spot[longest] + 1) % dims[longest]
    return result.at[tuple(spot)].set(top_value)


def levels(rng, extent, split, smallest, top_value):
    def one(dim, blocks):
        heights = jax.random.uniform(jax.random.fold_in(jax.random.fold_in(rng, 6), dim), (blocks,), jnp.float32, smallest / len(split), top_value / len(split))
        return jnp.repeat(jnp.exp(heights), extent[dim] // blocks).reshape((-1,) + (1,) * (len(extent) - dim - 1))

    loudness = one(*split[0])
    for cut in split[1:]:
        loudness = loudness * one(*cut)
    return loudness


def noise(key, dims, spread, reach, cuts=(), kind=jnp.bfloat16):
    entries = spread * jax.random.normal(key, dims, jnp.float32)
    if cuts:
        entries = entries * levels(key, dims, cuts, -0.22, 0.18)
    return jnp.clip(entries, -reach, reach).astype(kind)


def setup_inputs(seed: int = 0, part: int = 0) -> dict:
    streams_of = jax.random.split(jax.random.key(seed), 6)
    part_splits = jax.random.split(jax.random.fold_in(streams_of[5], part), 6)
    labels = touch_ends(jax.random.randint(part_splits[0], (LAYERS, NX, NY), 0, NLAB), jax.random.fold_in(part_splits[0], 1), 0, NLAB - 1).astype(jnp.int32)
    background = noise(part_splits[1], (LAYERS, NX, NY), 0.5, 3.0, ((0, 2), (1, 4), (2, 2)))
    contrasts = jnp.clip(jax.random.uniform(part_splits[2], (NLAB,), jnp.float32, -1.0, 1.0), -1.0, 1.0)
    kernels = noise(part_splits[3], (LAYERS, SPAN, SPAN), (SPAN * SPAN * LAYERS) ** -0.5, 0.125, ((0, 2),))
    observed = noise(part_splits[4], (3, NX, NY), 1.0, 6.0, ((1, 4), (2, 2)), jnp.float32)
    return dict(labels=labels, background=background, contrasts=contrasts, kernels=kernels, observed=observed)


descent = 0.01


def rolled(values, step_x, step_y):
    return jnp.roll(values, (-step_x, -step_y), axis=(-2, -1))


def tensor_parts(values):
    along_x = rolled(values, 1, 0) + rolled(values, -1, 0) - 2.0 * values
    along_y = rolled(values, 0, 1) + rolled(values, 0, -1) - 2.0 * values
    mixed = 0.25 * (rolled(values, 1, 1) - rolled(values, 1, -1) - rolled(values, -1, 1) + rolled(values, -1, -1))
    return along_x, along_y, mixed


def adjoint_sum(misfit):
    return tensor_parts(misfit[0])[0] + tensor_parts(misfit[1])[1] + tensor_parts(misfit[2])[2]


def reference(labels, background, contrasts, kernels, observed):
    density = jnp.take(contrasts, labels, axis=0) + background.astype(jnp.float32)
    placed = jnp.zeros((LAYERS, NX, NY), jnp.float32)
    placed = placed.at[:, :SPAN, :SPAN].set(kernels[:, ::-1, ::-1].astype(jnp.float32))
    placed = jnp.roll(placed, (-RADIUS, -RADIUS), axis=(1, 2))
    spectra = jnp.fft.rfft2(placed)
    residual = observed
    gradient = density
    for iteration in range(ITERS):
        rounded = lax.optimization_barrier(density.astype(jnp.bfloat16)).astype(jnp.float32)
        surface = jnp.fft.irfft2(jnp.sum(jnp.fft.rfft2(rounded) * spectra, axis=0), s=(NX, NY))
        residual = jnp.stack(tensor_parts(surface)) - observed
        adjoint_field = lax.optimization_barrier(adjoint_sum(residual).astype(jnp.bfloat16)).astype(jnp.float32)
        gradient = jnp.fft.irfft2(jnp.fft.rfft2(adjoint_field)[None] * jnp.conj(spectra), s=(NX, NY))
        density = density - descent * gradient
    return residual, gradient
```

```python
import functools

import jax
import jax.numpy as jnp
from jax import lax
from jax.experimental import pallas as pl
from jax.experimental.pallas import tpu as pltpu
from jax.sharding import PartitionSpec as P


descent = 0.01
ITERS = 2
PART = 48
FULL = 64
SHIFTS = 16
WIDE = 256

f32 = jnp.float32
bf16 = jnp.bfloat16


def iota(shape, dim):
    return lax.broadcasted_iota(jnp.int32, shape, dim)


def up_rows(v):
    return pltpu.roll(v, v.shape[0] - 1, 0)


def down_rows(v):
    return pltpu.roll(v, 1, 0)


def right(v):
    return pltpu.roll(v, v.shape[1] - 1, 1)


def left(v):
    return pltpu.roll(v, 1, 1)


def tensor_fields(s):
    above, below = up_rows(s), down_rows(s)
    along_x = above + below - 2.0 * s
    along_y = right(s) + left(s) - 2.0 * s
    diff = above - below
    mixed = 0.25 * (right(diff) - left(diff))
    return along_x, along_y, mixed


def adjoint_of(r0, r1, r2):
    cross = 0.25 * (right(r2) - left(r2))
    return (
        up_rows(r0 + cross)
        + down_rows(r0 - cross)
        - 2.0 * r0
        + right(r1)
        + left(r1)
        - 2.0 * r1
    )


def edge_message(field):
    width = field.shape[1]
    lane = iota((field.shape[0], 128), 1)
    first = field[:, :128]
    last = field[:, width - 256 : width - 128]
    side = pltpu.roll(field[:, width - 128 :], 64, 1)
    return jnp.where(lane < 32, first, jnp.where(lane < 96, side, last))


def add_edges(field, message):
    width = field.shape[1]
    lane = iota(message.shape, 1)
    swapped = pltpu.roll(message, 64, 1)
    zero = jnp.zeros_like(message)
    first = field[:, :128] + jnp.where(lane < 32, swapped, zero)
    last = field[:, width - 256 : width - 128] + jnp.where(lane >= 96, swapped, zero)
    side = field[:, width - 128 :] + jnp.where((lane < 32) | (lane >= 96), message, zero)
    return jnp.concatenate([first, field[:, 128 : width - 256], last, side], axis=1)


def build_bands(k_ref, base_ref, rows_ref, bands_ref):
    layers, span, _ = k_ref.shape
    base = jnp.zeros((span, WIDE), f32)
    for l in range(layers):
        place = jnp.where(
            iota((span, WIDE), 1) == l * 32 + iota((span, WIDE), 0), 1.0, 0.0
        )
        base = base + lax.dot_general(
            k_ref[l],
            place.astype(bf16),
            (((0,), (0,)), ((), ())),
            preferred_element_type=f32,
        )
    base_ref[...] = base
    for j in range(span):
        rows_ref[j * 8 : j * 8 + 8, :] = jnp.broadcast_to(base_ref[j : j + 1, :], (8, WIDE))
    rows = rows_ref[...]
    sub = iota(rows.shape, 0) & 7
    for bit in (1, 2, 4):
        rows = jnp.where((sub & bit) != 0, pltpu.roll(rows, bit, 1), rows)
    lane = iota(rows.shape, 1)
    for g in range(PART // 8):
        tap = (lane & 31) - (sub + 8 * g) + 15
        keep = (tap >= 0) & (tap < span) & (lane < layers * 32)
        moved = jnp.where(keep, pltpu.roll(rows, (8 * g - 15) % WIDE, 1), 0.0)
        for j in range(span):
            bands_ref[j * PART + 8 * g : j * PART + 8 * g + 8, :] = moved[8 * j : 8 * j + 8]


def scatter_surface(bands, rounded, prod_ref, span, radius):
    cells_y = rounded.shape[1]
    prod_ref[...] = jnp.dot(bands, rounded, preferred_element_type=f32)
    total = jnp.zeros((PART, cells_y + 128), f32)
    side = jnp.zeros((PART, 128), f32)
    for j in range(span):
        piece = jnp.concatenate([prod_ref[j * PART : (j + 1) * PART, :], side], axis=1)
        shift = (radius - j) % (cells_y + 128)
        total = total + (pltpu.roll(piece, shift, 1) if shift else piece)
    return total


def first_kernel(
    labels_ref, background_ref, contrasts_ref, k_ref, observed_ref,
    part_ref, edge_ref, q_ref, density_ref, bands_ref,
    base_ref, rows_ref, wide_ref, prod_ref, obs_ref,
):
    layers, cells_x, cells_y = labels_ref.shape
    span = k_ref.shape[1]
    build_bands(k_ref, base_ref, rows_ref, wide_ref)
    bands = wide_ref[...].astype(bf16)
    bands_ref[...] = bands
    classes = contrasts_ref.shape[0]
    for l in range(layers):
        label = labels_ref[l]
        value = jnp.full(label.shape, contrasts_ref[0], f32)
        for c in range(1, classes):
            value = jnp.where(label == c, contrasts_ref[c], value)
        density_ref[l * cells_x : (l + 1) * cells_x, :] = value + background_ref[l].astype(f32)
    rounded = density_ref[...].astype(bf16)
    bands_x = bands[:, : layers * cells_x]
    part = scatter_surface(bands_x, rounded, prod_ref, span, (span - 1) // 2)
    part_ref[...] = part
    edge_ref[:PART, :] = edge_message(part)
    obs_ref[...] = jnp.zeros(obs_ref.shape, f32)
    for k in range(3):
        obs_ref[k, 8 : 8 + cells_x, :cells_y] = observed_ref[k]
    q = adjoint_of(obs_ref[0], obs_ref[1], obs_ref[2])
    q_ref[...] = q
    edge_ref[PART:, :] = edge_message(q)


def transpose_kernel(bands_ref, out_ref):
    out_ref[...] = bands_ref[...].astype(f32).T.astype(bf16)


def edges_kernel(part_ref, edge_ref, out_ref):
    out_ref[...] = add_edges(part_ref[...], edge_ref[: part_ref.shape[0], :])


def rows_kernel(part_ref, other_ref, q_ref, edge_ref, sum_ref, up_ref, down_ref, q_out_ref):
    sum_ref[...] = part_ref[...] + other_ref[...]
    up_ref[:16, :] = sum_ref[1:17, :]
    down_ref[:16, :] = sum_ref[31:47, :]
    if q_ref is not None:
        q_out_ref[...] = add_edges(q_ref[...], edge_ref[PART:, :])
        up_ref[16:24, :] = q_out_ref[7:15, :]
        down_ref[16:24, :] = q_out_ref[33:41, :]


def full_surface(sum_ref, above_ref, below_ref, full_ref):
    zero = jnp.zeros((8, full_ref.shape[1]), f32)
    full_ref[:8, :] = zero
    full_ref[8:56, :] = sum_ref[...]
    full_ref[56:, :] = zero
    full_ref[7:23, :] = full_ref[7:23, :] + above_ref[:16, :]
    full_ref[41:57, :] = full_ref[41:57, :] + below_ref[:16, :]
    return full_ref[...]


def gradient_of(adjoint, turned, stack_ref, span, radius):
    cells_y = stack_ref.shape[1]
    for j in range(span):
        shift = (j - radius) % adjoint.shape[1]
        moved = pltpu.roll(adjoint, shift, 1) if shift else adjoint
        stack_ref[j * PART : (j + 1) * PART, :] = moved[:, :cells_y].astype(bf16)
    return jnp.dot(turned, stack_ref[...], preferred_element_type=f32)


def middle_kernel(
    sum_ref, above_ref, below_ref, q_ref, density_ref, bands_ref, turned_ref,
    part_ref, edge_ref, q_out_ref,
    full_ref, stack_ref, prod_ref, *, span,
):
    radius = (span - 1) // 2
    lanes = density_ref.shape[0]
    q_out_ref[...] = q_ref[...]
    q_out_ref[1:9, :] = q_out_ref[1:9, :] + above_ref[16:24, :]
    q_out_ref[39:47, :] = q_out_ref[39:47, :] + below_ref[16:24, :]
    s = full_surface(sum_ref, above_ref, below_ref, full_ref)
    adjoint = adjoint_of(*tensor_fields(s))[8:56] - q_out_ref[...]
    adjoint = adjoint.astype(bf16).astype(f32)
    gradient = gradient_of(adjoint, turned_ref[:lanes, :], stack_ref, span, radius)
    density = density_ref[...] - descent * gradient
    part = scatter_surface(
        bands_ref[:, :lanes], density.astype(bf16), prod_ref, span, radius
    )
    part_ref[...] = part
    edge_ref[...] = edge_message(part)


def last_kernel(
    start_ref, sum_ref, above_ref, below_ref, q_ref, turned_ref, observed_ref,
    residual_ref, gradient_ref,
    full_ref, stack_ref, misfit_ref, *, span,
):
    radius = (span - 1) // 2
    layers, cells_x, cells_y = gradient_ref.shape
    s = full_surface(sum_ref, above_ref, below_ref, full_ref)
    fields = tensor_fields(s)
    adjoint = adjoint_of(*fields)[8:56] - q_ref[...]
    adjoint = adjoint.astype(bf16).astype(f32)
    share = residual_ref.shape[1]
    for k in range(3):
        misfit_ref[k] = fields[k][16 : 16 + cells_x, :cells_y] - observed_ref[k]
    for start in range(0, cells_x, share):

        @pl.when(start_ref[0] == start)
        def _():
            residual_ref[...] = misfit_ref[:, start : start + share, :]

    gradient = gradient_of(adjoint, turned_ref[: layers * cells_x, :], stack_ref, span, radius)
    for l in range(layers):
        gradient_ref[l] = gradient[l * cells_x : (l + 1) * cells_x, :]


def call(kernel, outs, scratch=(), scalars=0, smem=()):
    vmem = pl.BlockSpec(memory_space=pltpu.VMEM)
    scalar = pl.BlockSpec(memory_space=pltpu.SMEM)

    def run(*operands):
        return pl.pallas_call(
            kernel,
            out_shape=outs,
            in_specs=[scalar if i in smem else vmem for i in range(len(operands))],
            out_specs=jax.tree.map(lambda _: vmem, outs),
            scratch_shapes=[pltpu.VMEM(shape, kind) for shape, kind in scratch],
        )(*operands)

    return run


def shaped(shape, kind=f32):
    return jax.ShapeDtypeStruct(shape, kind)


def swap(value, axis, distance):
    peers = lax.axis_size(axis)
    return lax.ppermute(value, axis, [(i, i ^ distance) for i in range(peers)])


def body(labels, background, contrasts, kernels, observed):
    layers, cells_x, cells_y = labels.shape
    span = kernels.shape[1]
    lanes = layers * cells_x
    width = cells_y + 128
    depth_peers, row_peers = lax.axis_size("gz"), lax.axis_size("gx")
    assert cells_x == 32 and span == 15 and lanes <= 192 and lax.axis_size("gy") == 2
    assert depth_peers & (depth_peers - 1) == 0
    share = cells_x // depth_peers
    upward = [(i, (i - 1) % row_peers) for i in range(row_peers)]
    downward = [(j, i) for i, j in upward]
    stack = ((span * PART, cells_y), bf16)
    prod = ((span * PART, cells_y), f32)
    full = ((FULL, width), f32)

    part, edge, q, density, bands = call(
        first_kernel,
        (
            shaped((PART, width)),
            shaped((2 * PART, 128)),
            shaped((PART, width)),
            shaped((lanes, cells_y)),
            shaped((span * PART, WIDE), bf16),
        ),
        (
            ((span, WIDE), f32),
            ((span * 8, WIDE), f32),
            ((span * PART, WIDE), f32),
            prod,
            ((3, PART, width), f32),
        ),
        smem=(2,),
    )(labels, background, contrasts, kernels, observed)
    turned = call(transpose_kernel, shaped((WIDE, span * PART), bf16))(bands)
    start = (lax.axis_index("gz") * share).astype(jnp.int32).reshape(1)

    for iteration in range(ITERS):
        others = swap(edge, "gy", 1)
        part = call(edges_kernel, shaped((PART, width)))(part, others)
        for bit in range(depth_peers.bit_length() - 2):
            part = part + swap(part, "gz", 2 << bit)
        other = swap(part, "gz", 1)
        if iteration == 0:
            total, up, down, q = call(
                rows_kernel,
                (
                    shaped((PART, width)),
                    shaped((24, width)),
                    shaped((24, width)),
                    shaped((PART, width)),
                ),
            )(part, other, q, others)
        else:
            total, up, down = call(
                lambda a, b, c, d, e: rows_kernel(a, b, None, None, c, d, e, None),
                (shaped((PART, width)), shaped((16, width)), shaped((16, width))),
            )(part, other)
        below = lax.ppermute(up, "gx", upward)
        above = lax.ppermute(down, "gx", downward)
        if iteration == 0:
            part, edge, q = call(
                functools.partial(middle_kernel, span=span),
                (shaped((PART, width)), shaped((PART, 128)), shaped((PART, width))),
                (full, stack, prod),
            )(total, above, below, q, density, bands, turned)
    return call(
        functools.partial(last_kernel, span=span),
        (shaped((3, share, cells_y)), shaped((layers, cells_x, cells_y))),
        (full, stack, ((3, cells_x, cells_y), f32)),
        smem=(0,),
    )(start, total, above, below, q, turned, observed)


def solution(mesh):
    placed = (
        P(("runs", "gz"), "gx", "gy"),
        P(("runs", "gz"), "gx", "gy"),
        P("runs"),
        P(("runs", "gz"), None, None),
        P("runs", "gx", "gy"),
    )
    return jax.shard_map(
        body,
        mesh=mesh,
        in_specs=placed,
        out_specs=(P("runs", ("gx", "gz"), "gy"), P(("runs", "gz"), "gx", "gy")),
        check_vma=False,
    )
```

```python
import functools

import jax
import jax.numpy as jnp
from jax import lax
from jax.experimental import pallas as pl
from jax.experimental.pallas import tpu as pltpu
from jax.sharding import PartitionSpec as P


descent = 0.01
ITERS = 2
PART = 48
FULL = 64
SHIFTS = 16
WIDE = 256
GRANT = 16 * 2**20

f32 = jnp.float32
bf16 = jnp.bfloat16


def iota(shape, dim):
    return lax.broadcasted_iota(jnp.int32, shape, dim)


def up_rows(v):
    return pltpu.roll(v, v.shape[0] - 1, 0)


def down_rows(v):
    return pltpu.roll(v, 1, 0)


def right(v):
    return pltpu.roll(v, v.shape[1] - 1, 1)


def left(v):
    return pltpu.roll(v, 1, 1)


def tensor_fields(s):
    above, below = up_rows(s), down_rows(s)
    along_x = above + below - 2.0 * s
    along_y = right(s) + left(s) - 2.0 * s
    diff = above - below
    mixed = 0.25 * (right(diff) - left(diff))
    return along_x, along_y, mixed


def adjoint_of(r0, r1, r2):
    cross = 0.25 * (right(r2) - left(r2))
    return (
        up_rows(r0 + cross)
        + down_rows(r0 - cross)
        - 2.0 * r0
        + right(r1)
        + left(r1)
        - 2.0 * r1
    )


def edge_message(field):
    width = field.shape[1]
    lane = iota((field.shape[0], 128), 1)
    first = field[:, :128]
    last = field[:, width - 256 : width - 128]
    side = pltpu.roll(field[:, width - 128 :], 64, 1)
    return jnp.where(lane < 32, first, jnp.where(lane < 96, side, last))


def add_edges(field, message):
    width = field.shape[1]
    lane = iota(message.shape, 1)
    swapped = pltpu.roll(message, 64, 1)
    zero = jnp.zeros_like(message)
    first = field[:, :128] + jnp.where(lane < 32, swapped, zero)
    last = field[:, width - 256 : width - 128] + jnp.where(lane >= 96, swapped, zero)
    side = field[:, width - 128 :] + jnp.where((lane < 32) | (lane >= 96), message, zero)
    return jnp.concatenate([first, field[:, 128 : width - 256], last, side], axis=1)


def build_bands(k_ref, base_ref, rows_ref, bands_ref):
    layers, span, _ = k_ref.shape
    base = jnp.zeros((span, WIDE), f32)
    for l in range(layers):
        place = jnp.where(
            iota((span, WIDE), 1) == l * 32 + iota((span, WIDE), 0), 1.0, 0.0
        )
        base = base + lax.dot_general(
            k_ref[l],
            place.astype(bf16),
            (((0,), (0,)), ((), ())),
            preferred_element_type=f32,
        )
    base_ref[...] = base
    for j in range(span):
        rows_ref[j * 8 : j * 8 + 8, :] = jnp.broadcast_to(base_ref[j : j + 1, :], (8, WIDE))
    rows = rows_ref[...]
    sub = iota(rows.shape, 0) & 7
    for bit in (1, 2, 4):
        rows = jnp.where((sub & bit) != 0, pltpu.roll(rows, bit, 1), rows)
    lane = iota(rows.shape, 1)
    for g in range(PART // 8):
        tap = (lane & 31) - (sub + 8 * g) + 15
        keep = (tap >= 0) & (tap < span) & (lane < layers * 32)
        moved = jnp.where(keep, pltpu.roll(rows, (8 * g - 15) % WIDE, 1), 0.0)
        for j in range(span):
            bands_ref[j * PART + 8 * g : j * PART + 8 * g + 8, :] = moved[8 * j : 8 * j + 8]


def scatter_surface(bands, rounded, prod_ref, span, radius):
    cells_y = rounded.shape[1]
    prod_ref[...] = jnp.dot(bands, rounded, preferred_element_type=f32)
    total = jnp.zeros((PART, cells_y + 128), f32)
    side = jnp.zeros((PART, 128), f32)
    for j in range(span):
        piece = jnp.concatenate([prod_ref[j * PART : (j + 1) * PART, :], side], axis=1)
        shift = (radius - j) % (cells_y + 128)
        total = total + (pltpu.roll(piece, shift, 1) if shift else piece)
    return total


def first_kernel(
    labels_hbm, background_hbm, contrasts_hbm, k_hbm, observed_hbm,
    part_ref, edge_ref, q_ref, density_ref, bands_ref,
    labels_ref, background_ref, contrasts_ref, k_ref, observed_ref, sems,
    base_ref, rows_ref, wide_ref, prod_ref, obs_ref,
):
    layers, cells_x, cells_y = labels_ref.shape
    span = k_ref.shape[1]
    copies = [
        pltpu.make_async_copy(source, target, sems.at[n])
        for n, (source, target) in enumerate(
            (
                (k_hbm, k_ref),
                (labels_hbm, labels_ref),
                (background_hbm, background_ref),
                (contrasts_hbm, contrasts_ref),
                (observed_hbm, observed_ref),
            )
        )
    ]
    for copy in copies:
        copy.start()
    copies[0].wait()
    build_bands(k_ref, base_ref, rows_ref, wide_ref)
    bands = wide_ref[...].astype(bf16)
    bands_ref[...] = bands
    for copy in copies[1:]:
        copy.wait()
    classes = contrasts_ref.shape[0]
    for l in range(layers):
        label = labels_ref[l]
        value = jnp.full(label.shape, contrasts_ref[0], f32)
        for c in range(1, classes):
            value = jnp.where(label == c, contrasts_ref[c], value)
        density_ref[l * cells_x : (l + 1) * cells_x, :] = value + background_ref[l].astype(f32)
    rounded = density_ref[...].astype(bf16)
    bands_x = bands[:, : layers * cells_x]
    part = scatter_surface(bands_x, rounded, prod_ref, span, (span - 1) // 2)
    part_ref[...] = part
    edge_ref[:PART, :] = edge_message(part)
    obs_ref[...] = jnp.zeros(obs_ref.shape, f32)
    for k in range(3):
        obs_ref[k, 8 : 8 + cells_x, :cells_y] = observed_ref[k]
    q = adjoint_of(obs_ref[0], obs_ref[1], obs_ref[2])
    q_ref[...] = q
    edge_ref[PART:, :] = edge_message(q)


def transpose_kernel(bands_ref, out_ref):
    out_ref[...] = bands_ref[...].astype(f32).T.astype(bf16)


def edges_kernel(part_ref, edge_ref, out_ref):
    out_ref[...] = add_edges(part_ref[...], edge_ref[: part_ref.shape[0], :])


def rows_kernel(part_ref, other_ref, q_ref, edge_ref, sum_ref, up_ref, down_ref, q_out_ref):
    sum_ref[...] = part_ref[...] + other_ref[...]
    up_ref[:16, :] = sum_ref[1:17, :]
    down_ref[:16, :] = sum_ref[31:47, :]
    if q_ref is not None:
        q_out_ref[...] = add_edges(q_ref[...], edge_ref[PART:, :])
        up_ref[16:24, :] = q_out_ref[7:15, :]
        down_ref[16:24, :] = q_out_ref[33:41, :]


def full_surface(sum_ref, above_ref, below_ref, full_ref):
    zero = jnp.zeros((8, full_ref.shape[1]), f32)
    full_ref[:8, :] = zero
    full_ref[8:56, :] = sum_ref[...]
    full_ref[56:, :] = zero
    full_ref[7:23, :] = full_ref[7:23, :] + above_ref[:16, :]
    full_ref[41:57, :] = full_ref[41:57, :] + below_ref[:16, :]
    return full_ref[...]


def gradient_of(adjoint, turned, stack_ref, span, radius):
    cells_y = stack_ref.shape[1]
    for j in range(span):
        shift = (j - radius) % adjoint.shape[1]
        moved = pltpu.roll(adjoint, shift, 1) if shift else adjoint
        stack_ref[j * PART : (j + 1) * PART, :] = moved[:, :cells_y].astype(bf16)
    return jnp.dot(turned, stack_ref[...], preferred_element_type=f32)


def middle_kernel(
    sum_ref, above_ref, below_ref, q_ref, density_ref, bands_ref, turned_ref,
    part_ref, edge_ref, q_out_ref,
    full_ref, stack_ref, prod_ref, *, span,
):
    radius = (span - 1) // 2
    lanes = density_ref.shape[0]
    q_out_ref[...] = q_ref[...]
    q_out_ref[1:9, :] = q_out_ref[1:9, :] + above_ref[16:24, :]
    q_out_ref[39:47, :] = q_out_ref[39:47, :] + below_ref[16:24, :]
    s = full_surface(sum_ref, above_ref, below_ref, full_ref)
    adjoint = adjoint_of(*tensor_fields(s))[8:56] - q_out_ref[...]
    adjoint = adjoint.astype(bf16).astype(f32)
    gradient = gradient_of(adjoint, turned_ref[:lanes, :], stack_ref, span, radius)
    density = density_ref[...] - descent * gradient
    part = scatter_surface(
        bands_ref[:, :lanes], density.astype(bf16), prod_ref, span, radius
    )
    part_ref[...] = part
    edge_ref[...] = edge_message(part)


def last_kernel(
    start_ref, sum_ref, above_ref, below_ref, q_ref, turned_ref, observed_ref,
    residual_ref, gradient_ref,
    full_ref, stack_ref, misfit_ref, *, span,
):
    radius = (span - 1) // 2
    layers, cells_x, cells_y = gradient_ref.shape
    s = full_surface(sum_ref, above_ref, below_ref, full_ref)
    fields = tensor_fields(s)
    adjoint = adjoint_of(*fields)[8:56] - q_ref[...]
    adjoint = adjoint.astype(bf16).astype(f32)
    share = residual_ref.shape[1]
    for k in range(3):
        misfit_ref[k] = fields[k][16 : 16 + cells_x, :cells_y] - observed_ref[k]
    for start in range(0, cells_x, share):

        @pl.when(start_ref[0] == start)
        def _():
            residual_ref[...] = misfit_ref[:, start : start + share, :]

    gradient = gradient_of(adjoint, turned_ref[: layers * cells_x, :], stack_ref, span, radius)
    for l in range(layers):
        gradient_ref[l] = gradient[l * cells_x : (l + 1) * cells_x, :]


def call(kernel, outs, scratch=(), inputs=pltpu.VMEM, smem=()):
    vmem = pl.BlockSpec(memory_space=pltpu.VMEM)
    given = pl.BlockSpec(memory_space=inputs)
    scalar = pl.BlockSpec(memory_space=pltpu.SMEM)

    def run(*operands):
        if inputs is pltpu.HBM:
            operands = [pltpu.with_memory_space_constraint(v, pltpu.HBM) for v in operands]
        return pl.pallas_call(
            kernel,
            out_shape=outs,
            in_specs=[scalar if i in smem else given for i in range(len(operands))],
            out_specs=jax.tree.map(lambda _: vmem, outs),
            scratch_shapes=[
                item if not isinstance(item, tuple) else pltpu.VMEM(*item) for item in scratch
            ],
            compiler_params=pltpu.CompilerParams(vmem_limit_bytes=GRANT),
        )(*operands)

    return run


def shaped(shape, kind=f32):
    return jax.ShapeDtypeStruct(shape, kind)


def swap(value, axis, distance):
    peers = lax.axis_size(axis)
    return lax.ppermute(value, axis, [(i, i ^ distance) for i in range(peers)])


def body(labels, background, contrasts, kernels, observed):
    layers, cells_x, cells_y = labels.shape
    span = kernels.shape[1]
    lanes = layers * cells_x
    width = cells_y + 128
    depth_peers, row_peers = lax.axis_size("gz"), lax.axis_size("gx")
    assert cells_x == 32 and span == 15 and lanes <= 192 and lax.axis_size("gy") == 2
    assert depth_peers & (depth_peers - 1) == 0
    share = cells_x // depth_peers
    upward = [(i, (i - 1) % row_peers) for i in range(row_peers)]
    downward = [(j, i) for i, j in upward]
    stack = ((span * PART, cells_y), bf16)
    prod = ((span * PART, cells_y), f32)
    full = ((FULL, width), f32)

    part, edge, q, density, bands = call(
        first_kernel,
        (
            shaped((PART, width)),
            shaped((2 * PART, 128)),
            shaped((PART, width)),
            shaped((lanes, cells_y)),
            shaped((span * PART, WIDE), bf16),
        ),
        (
            (labels.shape, labels.dtype),
            (background.shape, background.dtype),
            pltpu.SMEM(contrasts.shape, contrasts.dtype),
            (kernels.shape, kernels.dtype),
            (observed.shape, observed.dtype),
            pltpu.SemaphoreType.DMA((5,)),
            ((span, WIDE), f32),
            ((span * 8, WIDE), f32),
            ((span * PART, WIDE), f32),
            prod,
            ((3, PART, width), f32),
        ),
        inputs=pltpu.HBM,
    )(labels, background, contrasts, kernels, observed)
    turned = call(transpose_kernel, shaped((WIDE, span * PART), bf16))(bands)
    start = (lax.axis_index("gz") * share).astype(jnp.int32).reshape(1)

    for iteration in range(ITERS):
        others = swap(edge, "gy", 1)
        part = call(edges_kernel, shaped((PART, width)))(part, others)
        for bit in range(depth_peers.bit_length() - 2):
            part = part + swap(part, "gz", 2 << bit)
        other = swap(part, "gz", 1)
        if iteration == 0:
            total, up, down, q = call(
                rows_kernel,
                (
                    shaped((PART, width)),
                    shaped((24, width)),
                    shaped((24, width)),
                    shaped((PART, width)),
                ),
            )(part, other, q, others)
        else:
            total, up, down = call(
                lambda a, b, c, d, e: rows_kernel(a, b, None, None, c, d, e, None),
                (shaped((PART, width)), shaped((16, width)), shaped((16, width))),
            )(part, other)
        below = lax.ppermute(up, "gx", upward)
        above = lax.ppermute(down, "gx", downward)
        if iteration == 0:
            part, edge, q = call(
                functools.partial(middle_kernel, span=span),
                (shaped((PART, width)), shaped((PART, 128)), shaped((PART, width))),
                (full, stack, prod),
            )(total, above, below, q, density, bands, turned)
    return call(
        functools.partial(last_kernel, span=span),
        (shaped((3, share, cells_y)), shaped((layers, cells_x, cells_y))),
        (full, stack, ((3, cells_x, cells_y), f32)),
        smem=(0,),
    )(start, total, above, below, q, turned, observed)


def solution(mesh):
    placed = (
        P(("runs", "gz"), "gx", "gy"),
        P(("runs", "gz"), "gx", "gy"),
        P("runs"),
        P(("runs", "gz"), None, None),
        P("runs", "gx", "gy"),
    )
    return jax.shard_map(
        body,
        mesh=mesh,
        in_specs=placed,
        out_specs=(P("runs", ("gx", "gz"), "gy"), P(("runs", "gz"), "gx", "gy")),
        check_vma=False,
    )
```

```python
import functools

import jax
import jax.numpy as jnp
from jax import lax
from jax.experimental import pallas as pl
from jax.experimental.pallas import tpu as pltpu
from jax.sharding import PartitionSpec as P


descent = 0.01
ITERS = 2
PART = 48
EDGE = 9
FULL = 64
WIDE = 256
GRANT = 16 * 2**20

f32 = jnp.float32
bf16 = jnp.bfloat16


def iota(shape, dim):
    return lax.broadcasted_iota(jnp.int32, shape, dim)


def up_rows(v):
    return pltpu.roll(v, v.shape[0] - 1, 0)


def down_rows(v):
    return pltpu.roll(v, 1, 0)


def right(v):
    return pltpu.roll(v, v.shape[1] - 1, 1)


def left(v):
    return pltpu.roll(v, 1, 1)


def tensor_fields(s):
    above, below = up_rows(s), down_rows(s)
    along_x = above + below - 2.0 * s
    along_y = right(s) + left(s) - 2.0 * s
    diff = above - below
    mixed = 0.25 * (right(diff) - left(diff))
    return along_x, along_y, mixed


def adjoint_of(r0, r1, r2):
    cross = 0.25 * (right(r2) - left(r2))
    return (
        up_rows(r0 + cross)
        + down_rows(r0 - cross)
        - 2.0 * r0
        + right(r1)
        + left(r1)
        - 2.0 * r1
    )


def edge_message(field):
    width = field.shape[1]
    lane = iota((field.shape[0], 128), 1)
    first = field[:, :128]
    last = field[:, width - 256 : width - 128]
    side = pltpu.roll(field[:, width - 128 :], 64, 1)
    return jnp.where(lane < 32, first, jnp.where(lane < 96, side, last))


def add_edges(field, message):
    width = field.shape[1]
    lane = iota(message.shape, 1)
    swapped = pltpu.roll(message, 64, 1)
    zero = jnp.zeros_like(message)
    first = field[:, :128] + jnp.where(lane < 32, swapped, zero)
    last = field[:, width - 256 : width - 128] + jnp.where(lane >= 96, swapped, zero)
    side = field[:, width - 128 :] + jnp.where((lane < 32) | (lane >= 96), message, zero)
    return jnp.concatenate([first, field[:, 128 : width - 256], last, side], axis=1)


def build_bands(k_ref, base_ref, rows_ref, bands_ref):
    layers, span, _ = k_ref.shape
    base = jnp.zeros((span, WIDE), f32)
    for l in range(layers):
        place = jnp.where(
            iota((span, WIDE), 1) == l * 32 + iota((span, WIDE), 0), 1.0, 0.0
        )
        base = base + lax.dot_general(
            k_ref[l],
            place.astype(bf16),
            (((0,), (0,)), ((), ())),
            preferred_element_type=f32,
        )
    base_ref[...] = base
    for j in range(span):
        rows_ref[j * 8 : j * 8 + 8, :] = jnp.broadcast_to(base_ref[j : j + 1, :], (8, WIDE))
    rows = rows_ref[...]
    sub = iota(rows.shape, 0) & 7
    for bit in (1, 2, 4):
        rows = jnp.where((sub & bit) != 0, pltpu.roll(rows, bit, 1), rows)
    lane = iota(rows.shape, 1)
    for g in range(PART // 8):
        tap = (lane & 31) - (sub + 8 * g) + 15
        keep = (tap >= 0) & (tap < span) & (lane < layers * 32)
        moved = jnp.where(keep, pltpu.roll(rows, (8 * g - 15) % WIDE, 1), 0.0)
        for j in range(span):
            bands_ref[j * PART + 8 * g : j * PART + 8 * g + 8, :] = moved[8 * j : 8 * j + 8]


def outer_columns(v):
    return jnp.concatenate([v[:, :128], v[:, v.shape[1] - 128 :]], axis=1)


def edge_product(outer_ref, span, radius):
    total = jnp.zeros((PART, 384), f32)
    side = jnp.zeros((PART, 128), f32)
    for j in range(span):
        rows = outer_ref[j * PART : (j + 1) * PART, :]
        piece = jnp.concatenate([rows[:, 128:], side, rows[:, :128]], axis=1)
        shift = (radius - j) % 384
        total = total + (pltpu.roll(piece, shift, 1) if shift else piece)
    return edge_message(
        jnp.concatenate([total[:, 256:], total[:, :128], total[:, 128:256]], axis=1)
    )


def scatter_surface(bands, inner, outer_ref, prod_ref, span, radius):
    prod_ref[...] = jnp.dot(bands, inner, preferred_element_type=f32)
    width = inner.shape[1] + 384
    total = jnp.zeros((PART, width), f32)
    side = jnp.zeros((PART, 128), f32)
    for j in range(span):
        rows = slice(j * PART, (j + 1) * PART)
        piece = jnp.concatenate(
            [outer_ref[rows, :128], prod_ref[rows, :], outer_ref[rows, 128:], side], axis=1
        )
        shift = (radius - j) % width
        total = total + (pltpu.roll(piece, shift, 1) if shift else piece)
    return total


def fold_side(side):
    lane = iota((8, 128), 1)
    turned = pltpu.roll(side, EDGE, 1)
    folded = jnp.zeros((8, 128), f32)
    for g in range(PART // 8):
        piece = jnp.where(lane < 2 * EDGE, turned[8 * g : 8 * g + 8], 0.0)
        folded = folded + (pltpu.roll(piece, 2 * EDGE * g, 1) if g else piece)
    return folded


def unfold_side(folded):
    lane = iota((8, 128), 1)
    pieces = []
    for g in range(PART // 8):
        piece = pltpu.roll(folded, 128 - 2 * EDGE * g, 1) if g else folded
        pieces.append(jnp.where(lane < 2 * EDGE, piece, 0.0))
    return pltpu.roll(jnp.concatenate(pieces, axis=0), 128 - EDGE, 1)


def first_kernel(
    labels_hbm, background_hbm, contrasts_hbm, k_hbm, observed_hbm,
    edge_ref, q_ref, density_ref, bands_ref, outer_ref,
    labels_ref, background_ref, contrasts_ref, k_ref, observed_ref, sems,
    base_ref, rows_ref, wide_ref, obs_ref,
):
    layers, cells_x, cells_y = labels_ref.shape
    span = k_ref.shape[1]
    copies = [
        pltpu.make_async_copy(source, target, sems.at[n])
        for n, (source, target) in enumerate(
            (
                (k_hbm, k_ref),
                (labels_hbm, labels_ref),
                (background_hbm, background_ref),
                (contrasts_hbm, contrasts_ref),
                (observed_hbm, observed_ref),
            )
        )
    ]
    for copy in copies:
        copy.start()
    copies[0].wait()
    build_bands(k_ref, base_ref, rows_ref, wide_ref)
    bands = wide_ref[...].astype(bf16)
    bands_ref[...] = bands
    for copy in copies[1:]:
        copy.wait()
    classes = contrasts_ref.shape[0]
    for l in range(layers):
        label = labels_ref[l]
        value = jnp.full(label.shape, contrasts_ref[0], f32)
        for c in range(1, classes):
            value = jnp.where(label == c, contrasts_ref[c], value)
        density_ref[l * cells_x : (l + 1) * cells_x, :] = value + background_ref[l].astype(f32)
    rounded = outer_columns(density_ref[...]).astype(bf16)
    outer_ref[...] = jnp.dot(
        bands[:, : layers * cells_x], rounded, preferred_element_type=f32
    )
    edge_ref[:PART, :] = edge_product(outer_ref, span, (span - 1) // 2)
    obs_ref[...] = jnp.zeros(obs_ref.shape, f32)
    for k in range(3):
        obs_ref[k, 8 : 8 + cells_x, :cells_y] = observed_ref[k]
    q = adjoint_of(obs_ref[0], obs_ref[1], obs_ref[2])
    q_ref[...] = q
    edge_ref[PART:, :] = edge_message(q)


def transpose_kernel(bands_ref, out_ref):
    out_ref[...] = bands_ref[...].astype(f32).T.astype(bf16)


def inner_kernel(density_ref, bands_ref, outer_ref, part_ref, prod_ref, *, span):
    lanes, cells_y = density_ref.shape
    rounded = density_ref[:, 128 : cells_y - 128].astype(bf16)
    part_ref[...] = scatter_surface(
        bands_ref[:, :lanes], rounded, outer_ref, prod_ref, span, (span - 1) // 2
    )


def edges_kernel(part_ref, edge_ref, out_ref):
    cells_y = out_ref.shape[1]
    part = add_edges(part_ref[...], edge_ref[:PART, :])
    out_ref[...] = part[:, :cells_y]
    folded = fold_side(part[:, cells_y:])
    for n in range(8):
        row = (PART - 1) * (n // 4)
        out_ref[row : row + 1, 128 * (n % 4) : 128 * (n % 4 + 1)] = folded[n : n + 1]


def rows_kernel(
    part_ref, other_ref, q_ref, edge_ref, sum_ref, up_ref, down_ref, q_out_ref, fold_ref
):
    cells_y = part_ref.shape[1]
    sum_ref[:, :cells_y] = part_ref[...] + other_ref[...]
    for n in range(8):
        row = (PART - 1) * (n // 4)
        fold_ref[n : n + 1, :] = sum_ref[row : row + 1, 128 * (n % 4) : 128 * (n % 4 + 1)]
    sum_ref[:, cells_y:] = unfold_side(fold_ref[...])
    zero = jnp.zeros((1, cells_y), f32)
    sum_ref[:1, :cells_y] = zero
    sum_ref[PART - 1 :, :cells_y] = zero
    up_ref[:16, :] = sum_ref[1:17, :]
    down_ref[:16, :] = sum_ref[31:47, :]
    if q_ref is not None:
        q_out_ref[...] = add_edges(q_ref[...], edge_ref[PART:, :])
        up_ref[16:24, :] = q_out_ref[7:15, :]
        down_ref[16:24, :] = q_out_ref[33:41, :]


def full_surface(sum_ref, above_ref, below_ref, full_ref):
    zero = jnp.zeros((8, full_ref.shape[1]), f32)
    full_ref[:8, :] = zero
    full_ref[8:56, :] = sum_ref[...]
    full_ref[56:, :] = zero
    full_ref[7:23, :] = full_ref[7:23, :] + above_ref[:16, :]
    full_ref[41:57, :] = full_ref[41:57, :] + below_ref[:16, :]
    return full_ref[...]


def stack_shifts(adjoint, stack_ref, columns, span, radius):
    for j in range(span):
        shift = (j - radius) % adjoint.shape[1]
        moved = pltpu.roll(adjoint, shift, 1) if shift else adjoint
        stack_ref[j * PART : (j + 1) * PART, :] = columns(moved).astype(bf16)


def middle_kernel(
    sum_ref, above_ref, below_ref, q_ref, density_ref, bands_ref, turned_ref,
    edge_ref, q_out_ref, adjoint_ref, outer_ref,
    full_ref, stack_ref, *, span,
):
    radius = (span - 1) // 2
    lanes, cells_y = density_ref.shape
    q_out_ref[...] = q_ref[...]
    q_out_ref[1:9, :] = q_out_ref[1:9, :] + above_ref[16:24, :]
    q_out_ref[39:47, :] = q_out_ref[39:47, :] + below_ref[16:24, :]
    s = full_surface(sum_ref, above_ref, below_ref, full_ref)
    adjoint = adjoint_of(*tensor_fields(s))[8:56] - q_out_ref[...]
    adjoint_ref[...] = adjoint.astype(bf16).astype(f32)
    stack_shifts(
        adjoint_ref[...], stack_ref, lambda v: outer_columns(v[:, :cells_y]), span, radius
    )
    gradient = jnp.dot(turned_ref[:lanes, :], stack_ref[...], preferred_element_type=f32)
    density = outer_columns(density_ref[...]) - descent * gradient
    outer_ref[...] = jnp.dot(
        bands_ref[:, :lanes], density.astype(bf16), preferred_element_type=f32
    )
    edge_ref[...] = edge_product(outer_ref, span, radius)


def middle_inner_kernel(
    adjoint_ref, density_ref, bands_ref, turned_ref, outer_ref,
    part_ref,
    stack_ref, prod_ref, *, span,
):
    radius = (span - 1) // 2
    lanes, cells_y = density_ref.shape
    stack_shifts(
        adjoint_ref[:, :cells_y],
        stack_ref,
        lambda v: v[:, 128 : cells_y - 128],
        span,
        radius,
    )
    gradient = jnp.dot(turned_ref[:lanes, :], stack_ref[...], preferred_element_type=f32)
    density = density_ref[:, 128 : cells_y - 128] - descent * gradient
    part_ref[...] = scatter_surface(
        bands_ref[:, :lanes], density.astype(bf16), outer_ref, prod_ref, span, radius
    )


def last_kernel(
    start_ref, sum_ref, above_ref, below_ref, q_ref, turned_ref, observed_ref,
    residual_hbm, gradient_hbm,
    residual_ref, gradient_ref, sems, full_ref, stack_ref, misfit_ref, *, span,
):
    radius = (span - 1) // 2
    layers, cells_x, cells_y = gradient_ref.shape
    s = full_surface(sum_ref, above_ref, below_ref, full_ref)
    fields = tensor_fields(s)
    adjoint = adjoint_of(*fields)[8:56] - q_ref[...]
    adjoint = adjoint.astype(bf16).astype(f32)
    share = residual_ref.shape[1]
    for k in range(3):
        misfit_ref[k] = fields[k][16 : 16 + cells_x, :cells_y] - observed_ref[k]
    for start in range(0, cells_x, share):

        @pl.when(start_ref[0] == start)
        def _():
            residual_ref[...] = misfit_ref[:, start : start + share, :]

    copies = [pltpu.make_async_copy(residual_ref, residual_hbm, sems.at[0])]
    copies[0].start()
    stack_shifts(adjoint, stack_ref, lambda v: v[:, :cells_y], span, radius)
    turned = turned_ref[: layers * cells_x, :]
    half = cells_y // 2
    for n in range(2):
        columns = slice(n * half, (n + 1) * half)
        gradient = jnp.dot(turned, stack_ref[:, columns], preferred_element_type=f32)
        for l in range(layers):
            gradient_ref[l, :, columns] = gradient[l * cells_x : (l + 1) * cells_x, :]
        copy = pltpu.make_async_copy(
            gradient_ref.at[:, :, columns], gradient_hbm.at[:, :, columns], sems.at[1 + n]
        )
        copy.start()
        copies.append(copy)
    for copy in copies:
        copy.wait()


def call(kernel, outs, scratch=(), inputs=pltpu.VMEM, smem=(), results=pltpu.VMEM):
    made = pl.BlockSpec(memory_space=results)
    given = pl.BlockSpec(memory_space=inputs)
    scalar = pl.BlockSpec(memory_space=pltpu.SMEM)

    def run(*operands):
        if inputs is pltpu.HBM:
            operands = [pltpu.with_memory_space_constraint(v, pltpu.HBM) for v in operands]
        return pl.pallas_call(
            kernel,
            out_shape=outs,
            in_specs=[scalar if i in smem else given for i in range(len(operands))],
            out_specs=jax.tree.map(lambda _: made, outs),
            scratch_shapes=[
                item if not isinstance(item, tuple) else pltpu.VMEM(*item) for item in scratch
            ],
            compiler_params=pltpu.CompilerParams(vmem_limit_bytes=GRANT),
        )(*operands)

    return run


def shaped(shape, kind=f32):
    return jax.ShapeDtypeStruct(shape, kind)


def swap(value, axis, distance):
    peers = lax.axis_size(axis)
    return lax.ppermute(value, axis, [(i, i ^ distance) for i in range(peers)])


def body(labels, background, contrasts, kernels, observed):
    layers, cells_x, cells_y = labels.shape
    span = kernels.shape[1]
    lanes = layers * cells_x
    width = cells_y + 128
    depth_peers, row_peers = lax.axis_size("gz"), lax.axis_size("gx")
    assert cells_x == 32 and span == 15 and lanes <= 192 and cells_y == 512 and lax.axis_size("gy") == 2
    assert depth_peers & (depth_peers - 1) == 0
    share = cells_x // depth_peers
    upward = [(i, (i - 1) % row_peers) for i in range(row_peers)]
    downward = [(j, i) for i, j in upward]
    half = cells_y - 256
    full = ((FULL, width), f32)
    outer = shaped((span * PART, 256))
    inner = ((span * PART, half), f32)
    field = shaped((PART, width))

    def kernel_of(body_of):
        return functools.partial(body_of, span=span)

    edge, q, density, bands, outer_product = call(
        first_kernel,
        (
            shaped((2 * PART, 128)),
            field,
            shaped((lanes, cells_y)),
            shaped((span * PART, WIDE), bf16),
            outer,
        ),
        (
            (labels.shape, labels.dtype),
            (background.shape, background.dtype),
            pltpu.SMEM(contrasts.shape, contrasts.dtype),
            (kernels.shape, kernels.dtype),
            (observed.shape, observed.dtype),
            pltpu.SemaphoreType.DMA((5,)),
            ((span, WIDE), f32),
            ((span * 8, WIDE), f32),
            ((span * PART, WIDE), f32),
            ((3, PART, width), f32),
        ),
        inputs=pltpu.HBM,
    )(labels, background, contrasts, kernels, observed)
    part = call(kernel_of(inner_kernel), field, (inner,))(density, bands, outer_product)
    turned = call(transpose_kernel, shaped((WIDE, span * PART), bf16))(bands)
    start = (lax.axis_index("gz") * share).astype(jnp.int32).reshape(1)

    for iteration in range(ITERS):
        others = swap(edge, "gy", 1)
        part = call(edges_kernel, shaped((PART, cells_y)))(part, others)
        for bit in range(depth_peers.bit_length() - 2):
            part = part + swap(part, "gz", 2 << bit)
        other = swap(part, "gz", 1)
        fold = (((8, 128), f32),)
        if iteration == 0:
            total, up, down, q = call(
                rows_kernel, (field, shaped((24, width)), shaped((24, width)), field), fold
            )(part, other, q, others)
        else:
            total, up, down = call(
                lambda a, b, c, d, e, g: rows_kernel(a, b, None, None, c, d, e, None, g),
                (field, shaped((16, width)), shaped((16, width))),
                fold,
            )(part, other)
        below = lax.ppermute(up, "gx", upward)
        above = lax.ppermute(down, "gx", downward)
        if iteration == 0:
            edge, q, adjoint, outer_product = call(
                kernel_of(middle_kernel),
                (shaped((PART, 128)), field, field, outer),
                (full, ((span * PART, 256), bf16)),
            )(total, above, below, q, density, bands, turned)
            part = call(
                kernel_of(middle_inner_kernel),
                field,
                (((span * PART, half), bf16), inner),
            )(adjoint, density, bands, turned, outer_product)
    return call(
        kernel_of(last_kernel),
        (shaped((3, share, cells_y)), shaped((layers, cells_x, cells_y))),
        (
            ((3, share, cells_y), f32),
            ((layers, cells_x, cells_y), f32),
            pltpu.SemaphoreType.DMA((3,)),
            full,
            ((span * PART, cells_y), bf16),
            ((3, cells_x, cells_y), f32),
        ),
        smem=(0,),
        results=pltpu.HBM,
    )(start, total, above, below, q, turned, observed)


def solution(mesh):
    placed = (
        P(("runs", "gz"), "gx", "gy"),
        P(("runs", "gz"), "gx", "gy"),
        P("runs"),
        P(("runs", "gz"), None, None),
        P("runs", "gx", "gy"),
    )
    return jax.shard_map(
        body,
        mesh=mesh,
        in_specs=placed,
        out_specs=(P("runs", ("gx", "gz"), "gy"), P(("runs", "gz"), "gx", "gy")),
        check_vma=False,
    )
```

```python
import functools

import jax
import jax.numpy as jnp
from jax import lax
from jax.experimental import pallas as pl
from jax.experimental.pallas import tpu as pltpu
from jax.sharding import PartitionSpec as P


descent = 0.01
ITERS = 2
PART = 48
EDGE = 9
FULL = 64
WIDE = 256
GRANT = 16 * 2**20

f32 = jnp.float32
bf16 = jnp.bfloat16


def iota(shape, dim):
    return lax.broadcasted_iota(jnp.int32, shape, dim)


def up_rows(v):
    return pltpu.roll(v, v.shape[0] - 1, 0)


def down_rows(v):
    return pltpu.roll(v, 1, 0)


def right(v):
    return pltpu.roll(v, v.shape[1] - 1, 1)


def left(v):
    return pltpu.roll(v, 1, 1)


def tensor_fields(s):
    above, below = up_rows(s), down_rows(s)
    along_x = above + below - 2.0 * s
    along_y = right(s) + left(s) - 2.0 * s
    diff = above - below
    mixed = 0.25 * (right(diff) - left(diff))
    return along_x, along_y, mixed


def adjoint_of(r0, r1, r2):
    cross = 0.25 * (right(r2) - left(r2))
    return (
        up_rows(r0 + cross)
        + down_rows(r0 - cross)
        - 2.0 * r0
        + right(r1)
        + left(r1)
        - 2.0 * r1
    )


def adjoint_square(s):
    def row(k):
        return pltpu.roll(s, -k % FULL, 0)[8 : 8 + PART]

    def column(v, k):
        return pltpu.roll(v, -k % v.shape[1], 1)

    centre = s[8 : 8 + PART]
    near, far = row(1) + row(-1), row(2) + row(-2)
    mixed = 0.0625 * (far - 2.0 * centre)
    both = centre + mixed
    return (
        (far - 4.0 * near + 12.0 * centre - 2.0 * mixed)
        + (column(both, 2) + column(both, -2))
        - 4.0 * (column(centre, 1) + column(centre, -1))
    )


def edge_columns(first, last, side=None):
    lane = iota(first.shape, 1)
    inside = jnp.where(lane < 64, pltpu.roll(first, 32, 1), last)
    if side is None:
        return jnp.where(lane < 32, jnp.zeros_like(first), inside)
    outside = jnp.where(lane < 16, side, pltpu.roll(side, 32, 1))
    return jnp.where(lane < 32, outside, inside)


def edges_of(v):
    width = v.shape[1]
    return edge_columns(v[:, :128], v[:, width - 256 : width - 128], v[:, width - 128 :])


def add_edges(field, message):
    width = field.shape[1]
    lane = iota(message.shape, 1)
    turned = pltpu.roll(message, 96, 1)
    zero = jnp.zeros_like(message)
    first = field[:, :128] + jnp.where(lane < EDGE, message, zero)
    last = field[:, width - 256 : width - 128] + jnp.where(lane >= 128 - EDGE, turned, zero)
    side = field[:, width - 128 :] + jnp.where(
        lane < EDGE, turned, jnp.where(lane >= 128 - EDGE, message, zero)
    )
    return jnp.concatenate([first, field[:, 128 : width - 256], last, side], axis=1)


def build_bands(k_ref, taps_ref, base_ref, bands_ref):
    layers, span, _ = k_ref.shape
    taps_ref[...] = jnp.zeros(taps_ref.shape, f32)
    for l in range(layers):
        taps_ref[16 * l : 16 * l + span, :span] = k_ref[l].astype(f32)
    shape = (taps_ref.shape[0], WIDE)
    source = iota(shape, 0)
    place = jnp.where(32 * (source >> 4) + (source & 15) == iota(shape, 1), 1.0, 0.0)
    base_ref[...] = lax.dot_general(
        taps_ref[...].astype(bf16),
        place.astype(bf16),
        (((0,), (0,)), ((), ())),
        preferred_element_type=f32,
    )
    tap = (iota((8, 128), 1) & 31) - iota((8, 128), 0) + 15
    keep = [(tap - 8 * g >= 0) & (tap - 8 * g < span) for g in range(PART // 8)]
    for block in range(WIDE // 128):
        columns = slice(128 * block, 128 * block + 128)
        for j in range(span):
            row = jnp.broadcast_to(base_ref[j : j + 1, columns], (8, 128))
            moved = [
                jnp.where(
                    keep[g],
                    pltpu.roll(row, (8 * g - 15) % 128, 1, stride=1, stride_axis=0),
                    0.0,
                )
                for g in range(PART // 8)
            ]
            bands_ref[j * PART : (j + 1) * PART, columns] = jnp.concatenate(
                moved, axis=0
            ).astype(bf16)


def edge_message(bands, rounded, prod_ref, span, radius):
    prod_ref[...] = jnp.dot(bands, rounded, preferred_element_type=f32)
    total = prod_ref[radius * PART : (radius + 1) * PART, :]
    for j in range(span):
        if j != radius:
            piece = prod_ref[j * PART : (j + 1) * PART, :]
            total = total + pltpu.roll(piece, (radius - j) % 128, 1)
    return total


def scatter_surface(bands, rounded, prod_ref, span, radius):
    width = rounded.shape[1] + 128
    prod_ref[...] = jnp.dot(bands, rounded, preferred_element_type=f32)
    total = jnp.zeros((PART, width), f32)
    side = jnp.zeros((PART, 128), f32)
    for j in range(span):
        piece = jnp.concatenate([prod_ref[j * PART : (j + 1) * PART, :], side], axis=1)
        shift = (radius - j) % width
        total = total + (pltpu.roll(piece, shift, 1) if shift else piece)
    return total


def fold_side(side):
    lane = iota((8, 128), 1)
    turned = pltpu.roll(side, EDGE, 1)
    folded = jnp.zeros((8, 128), f32)
    for g in range(PART // 8):
        piece = jnp.where(lane < 2 * EDGE, turned[8 * g : 8 * g + 8], 0.0)
        folded = folded + (pltpu.roll(piece, 2 * EDGE * g, 1) if g else piece)
    return folded


def unfold_side(folded):
    lane = iota((8, 128), 1)
    pieces = []
    for g in range(PART // 8):
        piece = pltpu.roll(folded, 128 - 2 * EDGE * g, 1) if g else folded
        pieces.append(jnp.where(lane < 2 * EDGE, piece, 0.0))
    return pltpu.roll(jnp.concatenate(pieces, axis=0), 128 - EDGE, 1)


def first_kernel(
    labels_hbm, background_hbm, contrasts_hbm, k_hbm, observed_hbm,
    edge_ref, density_edge_ref, density_ref, bands_ref, observed_ref,
    labels_ref, background_ref, contrasts_ref, k_ref, sems,
    taps_ref, base_ref, prod_ref,
):
    layers, cells_x, cells_y = labels_ref.shape
    span = k_ref.shape[1]
    copies = [
        pltpu.make_async_copy(source, target, sems.at[n])
        for n, (source, target) in enumerate(
            (
                (k_hbm, k_ref),
                (contrasts_hbm, contrasts_ref),
                (labels_hbm, labels_ref),
                (background_hbm, background_ref),
                (observed_hbm, observed_ref),
            )
        )
    ]
    for copy in copies:
        copy.start()
    copies[0].wait()
    build_bands(k_ref, taps_ref, base_ref, bands_ref)
    for copy in copies[1:]:
        copy.wait()
    classes = contrasts_ref.shape[0]
    for l in range(layers):
        label = labels_ref[l]
        value = jnp.full(label.shape, contrasts_ref[0], f32)
        for c in range(1, classes):
            value = jnp.where(label == c, contrasts_ref[c], value)
        density = value + background_ref[l].astype(f32)
        rows = slice(l * cells_x, (l + 1) * cells_x)
        density_ref[rows, :] = density
        density_edge_ref[rows, :] = edge_columns(density[:, :128], density[:, cells_y - 128 :])
    edge_ref[:PART, :] = edge_message(
        bands_ref[:, : layers * cells_x],
        density_edge_ref[...].astype(bf16),
        prod_ref,
        span,
        (span - 1) // 2,
    )
    empty = jnp.zeros((8, 128), f32)
    edge_ref[PART:, :] = adjoint_of(
        *(
            jnp.concatenate(
                [
                    empty,
                    edge_columns(observed_ref[k, :, :128], observed_ref[k, :, cells_y - 128 :]),
                    empty,
                ],
                axis=0,
            )
            for k in range(3)
        )
    )


def first_field_kernel(
    density_ref, bands_ref, observed_ref, part_ref, q_ref, prod_ref, obs_ref, *, span
):
    lanes, cells_y = density_ref.shape
    part_ref[...] = scatter_surface(
        bands_ref[:, :lanes], density_ref[...].astype(bf16), prod_ref, span, (span - 1) // 2
    )
    obs_ref[...] = jnp.zeros(obs_ref.shape, f32)
    for k in range(3):
        obs_ref[k, 8 : PART - 8, :cells_y] = observed_ref[k]
    q_ref[...] = adjoint_of(obs_ref[0], obs_ref[1], obs_ref[2])


def transpose_kernel(bands_ref, out_ref):
    out_ref[...] = bands_ref[...].astype(f32).T.astype(bf16)


def edges_kernel(part_ref, edge_ref, out_ref):
    cells_y = out_ref.shape[1]
    part = add_edges(part_ref[...], edge_ref[:PART, :])
    out_ref[...] = part[:, :cells_y]
    folded = fold_side(part[:, cells_y:])
    for n in range(8):
        row = (PART - 1) * (n // 4)
        out_ref[row : row + 1, 128 * (n % 4) : 128 * (n % 4 + 1)] = folded[n : n + 1]


def rows_kernel(
    part_ref, other_ref, q_ref, edge_ref, sum_ref, up_ref, down_ref, q_out_ref, fold_ref
):
    cells_y = part_ref.shape[1]
    sum_ref[:, :cells_y] = part_ref[...] + other_ref[...]
    for n in range(8):
        row = (PART - 1) * (n // 4)
        fold_ref[n : n + 1, :] = sum_ref[row : row + 1, 128 * (n % 4) : 128 * (n % 4 + 1)]
    sum_ref[:, cells_y:] = unfold_side(fold_ref[...])
    zero = jnp.zeros((1, cells_y), f32)
    sum_ref[:1, :cells_y] = zero
    sum_ref[PART - 1 :, :cells_y] = zero
    sub = iota((8, sum_ref.shape[1]), 0)
    up_ref[:8, :] = sum_ref[8:16, :]
    up_ref[8:16, :] = jnp.where(sub >= 1, sum_ref[:8, :], sum_ref[16:24, :])
    down_ref[:8, :] = sum_ref[32:40, :]
    down_ref[8:16, :] = jnp.where(sub < 7, sum_ref[40:48, :], sum_ref[24:32, :])
    if q_ref is not None:
        q_out_ref[...] = add_edges(q_ref[...], edge_ref[PART:, :])
        up_ref[16:24, :] = jnp.where(sub < 7, q_out_ref[8:16, :], q_out_ref[:8, :])
        down_ref[16:24, :] = jnp.where(sub >= 1, q_out_ref[32:40, :], q_out_ref[40:48, :])


def full_surface(total, above, below):
    shape = (8, total.shape[1])
    sub = iota(shape, 0)
    zero = jnp.zeros(shape, f32)
    return jnp.concatenate(
        [
            jnp.where(sub == 7, above[8:16], zero),
            total[:8] + above[:8],
            total[8:16] + jnp.where(sub < 7, above[8:16], zero),
            total[16:32],
            total[32:40] + jnp.where(sub >= 1, below[8:16], zero),
            total[40:48] + below[:8],
            jnp.where(sub == 0, below[8:16], zero),
        ],
        axis=0,
    )


def full_q(q, above, below):
    shape = (8, q.shape[1])
    sub = iota(shape, 0)
    zero = jnp.zeros(shape, f32)
    return jnp.concatenate(
        [
            q[:8] + jnp.where(sub >= 1, above[16:24], zero),
            q[8:16] + jnp.where(sub == 0, above[16:24], zero),
            q[16:32],
            q[32:40] + jnp.where(sub == 7, below[16:24], zero),
            q[40:48] + jnp.where(sub < 7, below[16:24], zero),
        ],
        axis=0,
    )


def stack_shifts(adjoint, stack_ref, columns, span, radius):
    for j in range(span):
        shift = (j - radius) % adjoint.shape[1]
        moved = pltpu.roll(adjoint, shift, 1) if shift else adjoint
        stack_ref[j * PART : (j + 1) * PART, columns] = moved[:, columns].astype(bf16)


def rounded_adjoint(s, q):
    return (adjoint_square(s) - q).astype(bf16).astype(f32)


def middle_kernel(
    sum_ref, above_ref, below_ref, q_ref, density_edge_ref, bands_ref, turned_ref,
    edge_ref,
    stack_ref, prod_ref, *, span,
):
    radius = (span - 1) // 2
    lanes = density_edge_ref.shape[0]
    total, q = edges_of(sum_ref[...]), edges_of(q_ref[...])
    above, below = edges_of(above_ref[...]), edges_of(below_ref[...])
    adjoint = rounded_adjoint(full_surface(total, above, below), full_q(q, above, below))
    stack_shifts(adjoint, stack_ref, slice(0, 128), span, radius)
    gradient = jnp.dot(turned_ref[:lanes, :], stack_ref[...], preferred_element_type=f32)
    density = density_edge_ref[...] - descent * gradient
    lane = iota(density.shape, 1)
    keep = ((lane >= 32) & (lane < 48)) | (lane >= 112)
    density = jnp.where(keep, density, 0.0)
    edge_ref[...] = edge_message(
        bands_ref[:, :lanes], density.astype(bf16), prod_ref, span, radius
    )


def middle_field_kernel(
    sum_ref, above_ref, below_ref, q_ref, density_ref, bands_ref, turned_ref,
    part_ref, q_out_ref,
    stack_ref, prod_ref, *, span,
):
    radius = (span - 1) // 2
    lanes, cells_y = density_ref.shape
    above, below = above_ref[...], below_ref[...]
    q = full_q(q_ref[...], above, below)
    q_out_ref[...] = q
    adjoint = rounded_adjoint(full_surface(sum_ref[...], above, below), q)
    stack_shifts(adjoint, stack_ref, slice(0, cells_y), span, radius)
    gradient = jnp.dot(turned_ref[:lanes, :], stack_ref[...], preferred_element_type=f32)
    density = density_ref[...] - descent * gradient
    part_ref[...] = scatter_surface(
        bands_ref[:, :lanes], density.astype(bf16), prod_ref, span, radius
    )


def last_kernel(
    start_ref, sum_ref, above_ref, below_ref, q_ref, turned_ref, observed_ref,
    residual_hbm, gradient_hbm,
    residual_ref, gradient_ref, sems, full_ref, stack_ref, misfit_ref, *, span,
):
    radius = (span - 1) // 2
    layers, cells_x, cells_y = gradient_ref.shape
    s = full_surface(sum_ref[...], above_ref[...], below_ref[...])
    full_ref[...] = s
    adjoint = rounded_adjoint(s, q_ref[...])
    turned = turned_ref[: layers * cells_x, :]
    half = cells_y // 2
    copies = []
    for n in range(2):
        columns = slice(n * half, (n + 1) * half)
        stack_shifts(adjoint, stack_ref, columns, span, radius)
        gradient = jnp.dot(turned, stack_ref[:, columns], preferred_element_type=f32)
        for l in range(layers):
            gradient_ref[l, :, columns] = gradient[l * cells_x : (l + 1) * cells_x, :]
        copies.append(
            pltpu.make_async_copy(
                gradient_ref.at[:, :, columns], gradient_hbm.at[:, :, columns], sems.at[n]
            )
        )
        copies[-1].start()
    share = residual_ref.shape[1]
    for start in range(0, cells_x, share):

        @pl.when(start_ref[0] == start)
        def _():
            top = 16 + start
            low, high = (top - 1) // 8 * 8, -(-(top + share + 1) // 8) * 8
            fields = tensor_fields(full_ref[low:high, :])
            for k in range(3):
                misfit_ref[k, : high - low, :] = fields[k][:, :cells_y]
                residual_ref[k] = (
                    misfit_ref[k, top - low : top - low + share, :]
                    - observed_ref[k, start : start + share, :]
                )

    copies.append(pltpu.make_async_copy(residual_ref, residual_hbm, sems.at[2]))
    copies[-1].start()
    for copy in copies:
        copy.wait()


def call(kernel, outs, scratch=(), inputs=pltpu.VMEM, smem=(), results=pltpu.VMEM):
    made = pl.BlockSpec(memory_space=results)
    given = pl.BlockSpec(memory_space=inputs)
    scalar = pl.BlockSpec(memory_space=pltpu.SMEM)

    def run(*operands):
        if inputs is pltpu.HBM:
            operands = [pltpu.with_memory_space_constraint(v, pltpu.HBM) for v in operands]
        return pl.pallas_call(
            kernel,
            out_shape=outs,
            in_specs=[scalar if i in smem else given for i in range(len(operands))],
            out_specs=jax.tree.map(lambda _: made, outs),
            scratch_shapes=[
                item if not isinstance(item, tuple) else pltpu.VMEM(*item) for item in scratch
            ],
            compiler_params=pltpu.CompilerParams(vmem_limit_bytes=GRANT),
        )(*operands)

    return run


def shaped(shape, kind=f32):
    return jax.ShapeDtypeStruct(shape, kind)


def swap(value, axis, distance):
    peers = lax.axis_size(axis)
    return lax.ppermute(value, axis, [(i, i ^ distance) for i in range(peers)])


def body(labels, background, contrasts, kernels, observed):
    layers, cells_x, cells_y = labels.shape
    span = kernels.shape[1]
    lanes = layers * cells_x
    width = cells_y + 128
    depth_peers, row_peers = lax.axis_size("gz"), lax.axis_size("gx")
    assert cells_x == 32 and span == 15 and lanes <= 192 and cells_y == 512 and lax.axis_size("gy") == 2
    assert depth_peers & (depth_peers - 1) == 0
    share = cells_x // depth_peers
    upward = [(i, (i - 1) % row_peers) for i in range(row_peers)]
    downward = [(j, i) for i, j in upward]
    full = ((FULL, width), f32)
    prod = ((span * PART, cells_y), f32)
    stack = ((span * PART, cells_y), bf16)
    edge_prod = ((span * PART, 128), f32)
    edge_stack = ((span * PART, 128), bf16)
    field = shaped((PART, width))

    def kernel_of(body_of):
        return functools.partial(body_of, span=span)

    edge, density_edge, density, bands, observed = call(
        first_kernel,
        (
            shaped((2 * PART, 128)),
            shaped((lanes, 128)),
            shaped((lanes, cells_y)),
            shaped((span * PART, WIDE), bf16),
            shaped(observed.shape),
        ),
        (
            (labels.shape, labels.dtype),
            (background.shape, background.dtype),
            pltpu.SMEM(contrasts.shape, contrasts.dtype),
            (kernels.shape, kernels.dtype),
            pltpu.SemaphoreType.DMA((5,)),
            ((16 * layers, 16), f32),
            ((16, WIDE), f32),
            edge_prod,
        ),
        inputs=pltpu.HBM,
    )(labels, background, contrasts, kernels, observed)
    part, q = call(
        kernel_of(first_field_kernel), (field, field), (prod, ((3, PART, width), f32))
    )(density, bands, observed)
    turned = call(transpose_kernel, shaped((WIDE, span * PART), bf16))(bands)
    start = (lax.axis_index("gz") * share).astype(jnp.int32).reshape(1)

    for iteration in range(ITERS):
        others = swap(edge, "gy", 1)
        part = call(edges_kernel, shaped((PART, cells_y)))(part, others)
        for bit in range(depth_peers.bit_length() - 2):
            part = part + swap(part, "gz", 2 << bit)
        other = swap(part, "gz", 1)
        fold = (((8, 128), f32),)
        if iteration == 0:
            total, up, down, q = call(
                rows_kernel, (field, shaped((24, width)), shaped((24, width)), field), fold
            )(part, other, q, others)
        else:
            total, up, down = call(
                lambda a, b, c, d, e, g: rows_kernel(a, b, None, None, c, d, e, None, g),
                (field, shaped((16, width)), shaped((16, width))),
                fold,
            )(part, other)
        below = lax.ppermute(up, "gx", upward)
        above = lax.ppermute(down, "gx", downward)
        if iteration == 0:
            edge = call(
                kernel_of(middle_kernel), shaped((PART, 128)), (edge_stack, edge_prod)
            )(total, above, below, q, density_edge, bands, turned)
            part, q = call(kernel_of(middle_field_kernel), (field, field), (stack, prod))(
                total, above, below, q, density, bands, turned
            )
    return call(
        kernel_of(last_kernel),
        (shaped((3, share, cells_y)), shaped((layers, cells_x, cells_y))),
        (
            ((3, share, cells_y), f32),
            ((layers, cells_x, cells_y), f32),
            pltpu.SemaphoreType.DMA((3,)),
            full,
            ((span * PART, cells_y), bf16),
            ((3, cells_x, cells_y), f32),
        ),
        smem=(0,),
        results=pltpu.HBM,
    )(start, total, above, below, q, turned, observed)


def solution(mesh):
    placed = (
        P(("runs", "gz"), "gx", "gy"),
        P(("runs", "gz"), "gx", "gy"),
        P("runs"),
        P(("runs", "gz"), None, None),
        P("runs", "gx", "gy"),
    )
    return jax.shard_map(
        body,
        mesh=mesh,
        in_specs=placed,
        out_specs=(P("runs", ("gx", "gz"), "gy"), P(("runs", "gz"), "gx", "gy")),
        check_vma=False,
    )
```

```python
import functools

import jax
import jax.numpy as jnp
from jax import lax
from jax.experimental import pallas as pl
from jax.experimental.pallas import tpu as pltpu
from jax.sharding import PartitionSpec as P


descent = 0.01
ITERS = 2
PART = 48
EDGE = 9
FULL = 64
WIDE = 256
GRANT = 16 * 2**20

f32 = jnp.float32
bf16 = jnp.bfloat16


def iota(shape, dim):
    return lax.broadcasted_iota(jnp.int32, shape, dim)


def up_rows(v):
    return pltpu.roll(v, v.shape[0] - 1, 0)


def down_rows(v):
    return pltpu.roll(v, 1, 0)


def right(v):
    return pltpu.roll(v, v.shape[1] - 1, 1)


def left(v):
    return pltpu.roll(v, 1, 1)


def tensor_fields(s):
    above, below = up_rows(s), down_rows(s)
    along_x = above + below - 2.0 * s
    along_y = right(s) + left(s) - 2.0 * s
    diff = above - below
    mixed = 0.25 * (right(diff) - left(diff))
    return along_x, along_y, mixed


def adjoint_of(r0, r1, r2):
    cross = 0.25 * (right(r2) - left(r2))
    return (
        up_rows(r0 + cross)
        + down_rows(r0 - cross)
        - 2.0 * r0
        + right(r1)
        + left(r1)
        - 2.0 * r1
    )


def adjoint_square(s):
    def row(k):
        return pltpu.roll(s, -k % FULL, 0)[8 : 8 + PART]

    def column(v, k):
        return pltpu.roll(v, -k % v.shape[1], 1)

    centre = s[8 : 8 + PART]
    near, far = row(1) + row(-1), row(2) + row(-2)
    mixed = 0.0625 * (far - 2.0 * centre)
    both = centre + mixed
    return (
        (far - 4.0 * near + 12.0 * centre - 2.0 * mixed)
        + (column(both, 2) + column(both, -2))
        - 4.0 * (column(centre, 1) + column(centre, -1))
    )


def edge_columns(first, last, side=None):
    lane = iota(first.shape, 1)
    inside = jnp.where(lane < 64, pltpu.roll(first, 32, 1), last)
    if side is None:
        return jnp.where(lane < 32, jnp.zeros_like(first), inside)
    outside = jnp.where(lane < 16, side, pltpu.roll(side, 32, 1))
    return jnp.where(lane < 32, outside, inside)


def edges_of(v):
    width = v.shape[1]
    return edge_columns(v[:, :128], v[:, width - 256 : width - 128], v[:, width - 128 :])


def add_edges(field, message):
    width = field.shape[1]
    lane = iota(message.shape, 1)
    turned = pltpu.roll(message, 96, 1)
    zero = jnp.zeros_like(message)
    first = field[:, :128] + jnp.where(lane < EDGE, message, zero)
    last = field[:, width - 256 : width - 128] + jnp.where(lane >= 128 - EDGE, turned, zero)
    side = field[:, width - 128 :] + jnp.where(
        lane < EDGE, turned, jnp.where(lane >= 128 - EDGE, message, zero)
    )
    return jnp.concatenate([first, field[:, 128 : width - 256], last, side], axis=1)


def kernel_rows(k_ref, taps_ref):
    layers, span, _ = k_ref.shape
    taps_ref[...] = jnp.zeros(taps_ref.shape, f32)
    for l in range(layers):
        taps_ref[16 * l : 16 * l + span, :span] = k_ref[l].astype(f32)
    shape = (taps_ref.shape[0], WIDE)
    source = iota(shape, 0)
    place = jnp.where(32 * (source >> 4) + (source & 15) == iota(shape, 1), 1.0, 0.0)
    return lax.dot_general(
        taps_ref[...].astype(bf16),
        place.astype(bf16),
        (((0,), (0,)), ((), ())),
        preferred_element_type=f32,
    )


def build_bands(base_ref, bands_ref, span, offset=0):
    tap = (iota((8, 128), 1) & 31) - iota((8, 128), 0) + 15
    keep = [(tap - 8 * g >= 0) & (tap - 8 * g < span) for g in range(PART // 8)]
    for block in range(WIDE // 128):
        for j in range(span):
            row = jnp.broadcast_to(
                base_ref[j : j + 1, 128 * block : 128 * block + 128], (8, 128)
            )
            moved = [
                jnp.where(
                    keep[g],
                    pltpu.roll(row, (8 * g - 15) % 128, 1, stride=1, stride_axis=0),
                    0.0,
                )
                for g in range(PART // 8)
            ]
            bands_ref[
                j * PART : (j + 1) * PART,
                offset + 128 * block : offset + 128 * block + 128,
            ] = jnp.concatenate(moved, axis=0).astype(bf16)


def edge_message(bands, rounded, prod_ref, span, radius):
    prod_ref[...] = jnp.dot(bands, rounded, preferred_element_type=f32)
    total = prod_ref[radius * PART : (radius + 1) * PART, :]
    for j in range(span):
        if j != radius:
            piece = prod_ref[j * PART : (j + 1) * PART, :]
            total = total + pltpu.roll(piece, (radius - j) % 128, 1)
    return total


def scatter_surface(bands, rounded, prod_ref, span, radius):
    width = rounded.shape[1] + 128
    prod_ref[...] = jnp.dot(bands, rounded, preferred_element_type=f32)
    total = jnp.zeros((PART, width), f32)
    side = jnp.zeros((PART, 128), f32)
    for j in range(span):
        piece = jnp.concatenate([prod_ref[j * PART : (j + 1) * PART, :], side], axis=1)
        shift = (radius - j) % width
        total = total + (pltpu.roll(piece, shift, 1) if shift else piece)
    return total


def fold_side(side):
    lane = iota((8, 128), 1)
    turned = pltpu.roll(side, EDGE, 1)
    folded = jnp.zeros((8, 128), f32)
    for g in range(PART // 8):
        piece = jnp.where(lane < 2 * EDGE, turned[8 * g : 8 * g + 8], 0.0)
        folded = folded + (pltpu.roll(piece, 2 * EDGE * g, 1) if g else piece)
    return folded


def unfold_side(folded):
    lane = iota((8, 128), 1)
    pieces = []
    for g in range(PART // 8):
        piece = pltpu.roll(folded, 128 - 2 * EDGE * g, 1) if g else folded
        pieces.append(jnp.where(lane < 2 * EDGE, piece, 0.0))
    return pltpu.roll(jnp.concatenate(pieces, axis=0), 128 - EDGE, 1)


def first_kernel(
    labels_hbm, background_hbm, contrasts_hbm, k_hbm, observed_hbm,
    edge_ref, density_edge_ref, density_ref, base_ref, bands_ref, observed_ref,
    labels_ref, background_ref, contrasts_ref, k_ref, sems,
    taps_ref, prod_ref,
):
    layers, cells_x, cells_y = labels_ref.shape
    span = k_ref.shape[1]
    copies = [
        pltpu.make_async_copy(source, target, sems.at[n])
        for n, (source, target) in enumerate(
            (
                (k_hbm, k_ref),
                (contrasts_hbm, contrasts_ref),
                (labels_hbm, labels_ref),
                (background_hbm, background_ref),
                (observed_hbm, observed_ref),
            )
        )
    ]
    for copy in copies:
        copy.start()
    copies[0].wait()
    base_ref[...] = kernel_rows(k_ref, taps_ref)
    build_bands(base_ref, bands_ref, span)
    for copy in copies[1:]:
        copy.wait()
    classes = contrasts_ref.shape[0]
    for l in range(layers):
        label = labels_ref[l]
        value = jnp.full(label.shape, contrasts_ref[0], f32)
        for c in range(1, classes):
            value = jnp.where(label == c, contrasts_ref[c], value)
        density = value + background_ref[l].astype(f32)
        rows = slice(l * cells_x, (l + 1) * cells_x)
        density_ref[rows, :] = density
        density_edge_ref[rows, :] = edge_columns(density[:, :128], density[:, cells_y - 128 :])
    edge_ref[:PART, :] = edge_message(
        bands_ref[:, : layers * cells_x],
        density_edge_ref[...].astype(bf16),
        prod_ref,
        span,
        (span - 1) // 2,
    )
    empty = jnp.zeros((8, 128), f32)
    edge_ref[PART:, :] = adjoint_of(
        *(
            jnp.concatenate(
                [
                    empty,
                    edge_columns(observed_ref[k, :, :128], observed_ref[k, :, cells_y - 128 :]),
                    empty,
                ],
                axis=0,
            )
            for k in range(3)
        )
    )


def first_field_kernel(
    density_ref, bands_ref, observed_ref, part_ref, q_ref, prod_ref, obs_ref, *, span
):
    lanes, cells_y = density_ref.shape
    part_ref[...] = scatter_surface(
        bands_ref[:, :lanes], density_ref[...].astype(bf16), prod_ref, span, (span - 1) // 2
    )
    obs_ref[...] = jnp.zeros(obs_ref.shape, f32)
    for k in range(3):
        obs_ref[k, 8 : PART - 8, :cells_y] = observed_ref[k]
    q_ref[...] = adjoint_of(obs_ref[0], obs_ref[1], obs_ref[2])


def turn_kernel(*refs, span):
    *base_refs, own_ref, bands_ref, turned_ref = refs
    bands_ref[:, :WIDE] = own_ref[...]
    for n, base_ref in enumerate(base_refs):
        build_bands(base_ref, bands_ref, span, WIDE * (n + 1))
    turned_ref[...] = bands_ref[...].astype(f32).T.astype(bf16)


def edges_kernel(part_ref, edge_ref, out_ref):
    cells_y = out_ref.shape[1]
    part = add_edges(part_ref[...], edge_ref[:PART, :])
    out_ref[...] = part[:, :cells_y]
    folded = fold_side(part[:, cells_y:])
    for n in range(8):
        row = (PART - 1) * (n // 4)
        out_ref[row : row + 1, 128 * (n % 4) : 128 * (n % 4 + 1)] = folded[n : n + 1]


def send_rows(sum_ref, up_ref, down_ref):
    sub = iota((8, sum_ref.shape[1]), 0)
    up_ref[:8, :] = sum_ref[8:16, :]
    up_ref[8:16, :] = jnp.where(sub >= 1, sum_ref[:8, :], sum_ref[16:24, :])
    down_ref[:8, :] = sum_ref[32:40, :]
    down_ref[8:16, :] = jnp.where(sub < 7, sum_ref[40:48, :], sum_ref[24:32, :])


def rows_kernel(
    part_ref, other_ref, q_ref, edge_ref, sum_ref, up_ref, down_ref, q_out_ref, fold_ref
):
    cells_y = part_ref.shape[1]
    sum_ref[:, :cells_y] = part_ref[...] + other_ref[...]
    for n in range(8):
        row = (PART - 1) * (n // 4)
        fold_ref[n : n + 1, :] = sum_ref[row : row + 1, 128 * (n % 4) : 128 * (n % 4 + 1)]
    sum_ref[:, cells_y:] = unfold_side(fold_ref[...])
    zero = jnp.zeros((1, cells_y), f32)
    sum_ref[:1, :cells_y] = zero
    sum_ref[PART - 1 :, :cells_y] = zero
    send_rows(sum_ref, up_ref, down_ref)
    if q_ref is not None:
        sub = iota((8, sum_ref.shape[1]), 0)
        q_out_ref[...] = add_edges(q_ref[...], edge_ref[PART:, :])
        up_ref[16:24, :] = jnp.where(sub < 7, q_out_ref[8:16, :], q_out_ref[:8, :])
        down_ref[16:24, :] = jnp.where(sub >= 1, q_out_ref[32:40, :], q_out_ref[40:48, :])


def whole_rows_kernel(part_ref, edge_ref, sum_ref, up_ref, down_ref):
    sum_ref[...] = add_edges(part_ref[...], edge_ref[...])
    send_rows(sum_ref, up_ref, down_ref)


def full_surface(total, above, below):
    shape = (8, total.shape[1])
    sub = iota(shape, 0)
    zero = jnp.zeros(shape, f32)
    return jnp.concatenate(
        [
            jnp.where(sub == 7, above[8:16], zero),
            total[:8] + above[:8],
            total[8:16] + jnp.where(sub < 7, above[8:16], zero),
            total[16:32],
            total[32:40] + jnp.where(sub >= 1, below[8:16], zero),
            total[40:48] + below[:8],
            jnp.where(sub == 0, below[8:16], zero),
        ],
        axis=0,
    )


def full_q(q, above, below):
    shape = (8, q.shape[1])
    sub = iota(shape, 0)
    zero = jnp.zeros(shape, f32)
    return jnp.concatenate(
        [
            q[:8] + jnp.where(sub >= 1, above[16:24], zero),
            q[8:16] + jnp.where(sub == 0, above[16:24], zero),
            q[16:32],
            q[32:40] + jnp.where(sub == 7, below[16:24], zero),
            q[40:48] + jnp.where(sub < 7, below[16:24], zero),
        ],
        axis=0,
    )


def stack_shifts(adjoint, stack_ref, columns, span, radius):
    for j in range(span):
        shift = (j - radius) % adjoint.shape[1]
        moved = pltpu.roll(adjoint, shift, 1) if shift else adjoint
        stack_ref[j * PART : (j + 1) * PART, columns] = moved[:, columns]


def rounded_adjoint(s, q):
    return (adjoint_square(s) - q).astype(bf16)


def descended(densities, gradient, keep=None):
    pieces = []
    for n, density in enumerate(densities):
        rows, columns = density.shape
        moved = density - descent * gradient[n * WIDE : n * WIDE + rows]
        if keep is not None:
            moved = jnp.where(keep, moved, 0.0)
        pieces.append(moved.astype(bf16))
        pieces.append(jnp.zeros((WIDE - rows, columns), bf16))
    return jnp.concatenate(pieces, axis=0)


def middle_kernel(
    sum_ref, above_ref, below_ref, q_ref, density_edge_ref, bands_ref, turned_ref,
    *rest, span,
):
    *twin_refs, edge_ref, stack_ref, prod_ref = rest
    radius = (span - 1) // 2
    total, q = edges_of(sum_ref[...]), edges_of(q_ref[...])
    above, below = edges_of(above_ref[...]), edges_of(below_ref[...])
    adjoint = rounded_adjoint(full_surface(total, above, below), full_q(q, above, below))
    stack_shifts(adjoint, stack_ref, slice(0, 128), span, radius)
    gradient = jnp.dot(turned_ref[...], stack_ref[...], preferred_element_type=f32)
    densities = [density_edge_ref[...]] + [
        edge_columns(ref[:, :128], ref[:, ref.shape[1] - 128 :]) for ref in twin_refs
    ]
    lane = iota(densities[0].shape, 1)
    keep = ((lane >= 32) & (lane < 48)) | (lane >= 112)
    edge_ref[...] = edge_message(
        bands_ref[...], descended(densities, gradient, keep), prod_ref, span, radius
    )


def middle_field_kernel(
    sum_ref, above_ref, below_ref, q_ref, density_ref, bands_ref, turned_ref,
    *rest, span,
):
    *twin_refs, part_ref, q_out_ref, stack_ref, prod_ref = rest
    radius = (span - 1) // 2
    cells_y = density_ref.shape[1]
    above, below = above_ref[...], below_ref[...]
    q = full_q(q_ref[...], above, below)
    q_out_ref[...] = q
    adjoint = rounded_adjoint(full_surface(sum_ref[...], above, below), q)
    stack_shifts(adjoint, stack_ref, slice(0, cells_y), span, radius)
    gradient = jnp.dot(turned_ref[...], stack_ref[...], preferred_element_type=f32)
    densities = [ref[...] for ref in (density_ref, *twin_refs)]
    part_ref[...] = scatter_surface(
        bands_ref[...], descended(densities, gradient), prod_ref, span, radius
    )


def last_kernel(
    start_ref, sum_ref, above_ref, below_ref, q_ref, turned_ref, observed_ref,
    residual_hbm, gradient_hbm,
    residual_ref, gradient_ref, sems, full_ref, stack_ref, misfit_ref, *, span,
):
    radius = (span - 1) // 2
    layers, cells_x, cells_y = gradient_ref.shape
    s = full_surface(sum_ref[...], above_ref[...], below_ref[...])
    full_ref[...] = s
    adjoint = rounded_adjoint(s, q_ref[...])
    turned = turned_ref[: layers * cells_x, :]
    half = cells_y // 2
    copies = []
    for n in range(2):
        columns = slice(n * half, (n + 1) * half)
        stack_shifts(adjoint, stack_ref, columns, span, radius)
        gradient = jnp.dot(turned, stack_ref[:, columns], preferred_element_type=f32)
        for l in range(layers):
            gradient_ref[l, :, columns] = gradient[l * cells_x : (l + 1) * cells_x, :]
        copies.append(
            pltpu.make_async_copy(
                gradient_ref.at[:, :, columns], gradient_hbm.at[:, :, columns], sems.at[n]
            )
        )
        copies[-1].start()
    share = residual_ref.shape[1]
    if share % 8 == 0:
        start = pl.multiple_of(start_ref[0], 8)
        fields = tensor_fields(full_ref[pl.ds(start + 8, share + 16), :])
        for k in range(3):
            residual_ref[k] = (
                fields[k][8 : 8 + share, :cells_y] - observed_ref[k, pl.ds(start, share), :]
            )
    else:
        fields = tensor_fields(full_ref[...])
        for k in range(3):
            misfit_ref[k] = fields[k][16 : 16 + cells_x, :cells_y] - observed_ref[k]
        for start in range(0, cells_x, share):

            @pl.when(start_ref[0] == start)
            def _():
                residual_ref[...] = misfit_ref[:, start : start + share, :]

    copies.append(pltpu.make_async_copy(residual_ref, residual_hbm, sems.at[2]))
    copies[-1].start()
    for copy in copies:
        copy.wait()


def call(kernel, outs, scratch=(), inputs=pltpu.VMEM, smem=(), results=pltpu.VMEM):
    made = pl.BlockSpec(memory_space=results)
    given = pl.BlockSpec(memory_space=inputs)
    scalar = pl.BlockSpec(memory_space=pltpu.SMEM)

    def run(*operands):
        if inputs is pltpu.HBM:
            operands = [pltpu.with_memory_space_constraint(v, pltpu.HBM) for v in operands]
        return pl.pallas_call(
            kernel,
            out_shape=outs,
            in_specs=[scalar if i in smem else given for i in range(len(operands))],
            out_specs=jax.tree.map(lambda _: made, outs),
            scratch_shapes=[
                item if not isinstance(item, tuple) else pltpu.VMEM(*item) for item in scratch
            ],
            compiler_params=pltpu.CompilerParams(vmem_limit_bytes=GRANT),
        )(*operands)

    return run


def shaped(shape, kind=f32):
    return jax.ShapeDtypeStruct(shape, kind)


def swap(value, axis, distance):
    peers = lax.axis_size(axis)
    return lax.ppermute(value, axis, [(i, i ^ distance) for i in range(peers)])


def body(labels, background, contrasts, kernels, observed):
    layers, cells_x, cells_y = labels.shape
    span = kernels.shape[1]
    lanes = layers * cells_x
    width = cells_y + 128
    depth_peers, row_peers = lax.axis_size("gz"), lax.axis_size("gx")
    assert cells_x == 32 and span == 15 and lanes <= 192 and cells_y == 512 and lax.axis_size("gy") == 2
    assert depth_peers & (depth_peers - 1) == 0
    share = cells_x // depth_peers
    upward = [(i, (i - 1) % row_peers) for i in range(row_peers)]
    downward = [(j, i) for i, j in upward]
    full = ((FULL, width), f32)
    prod = ((span * PART, cells_y), f32)
    stack = ((span * PART, cells_y), bf16)
    edge_prod = ((span * PART, 128), f32)
    edge_stack = ((span * PART, 128), bf16)
    field = shaped((PART, width))

    def kernel_of(body_of):
        return functools.partial(body_of, span=span)

    edge, density_edge, density, base, bands, observed = call(
        first_kernel,
        (
            shaped((2 * PART, 128)),
            shaped((lanes, 128)),
            shaped((lanes, cells_y)),
            shaped((16, WIDE)),
            shaped((span * PART, WIDE), bf16),
            shaped(observed.shape),
        ),
        (
            (labels.shape, labels.dtype),
            (background.shape, background.dtype),
            pltpu.SMEM(contrasts.shape, contrasts.dtype),
            (kernels.shape, kernels.dtype),
            pltpu.SemaphoreType.DMA((5,)),
            ((16 * layers, 16), f32),
            edge_prod,
        ),
        inputs=pltpu.HBM,
    )(labels, background, contrasts, kernels, observed)
    part, q = call(
        kernel_of(first_field_kernel), (field, field), (prod, ((3, PART, width), f32))
    )(density, bands, observed)
    start = (lax.axis_index("gz") * share).astype(jnp.int32).reshape(1)

    twins = depth_peers == 2
    fold = (((8, 128), f32),)
    for iteration in range(ITERS):
        others = swap(edge, "gy", 1)
        if iteration == 1 and twins:
            total, up, down = call(
                whole_rows_kernel, (field, shaped((16, width)), shaped((16, width)))
            )(part, others)
        else:
            part = call(edges_kernel, shaped((PART, cells_y)))(part, others)
            for bit in range(depth_peers.bit_length() - 2):
                part = part + swap(part, "gz", 2 << bit)
            other = swap(part, "gz", 1)
            if iteration == 0:
                total, up, down, q = call(
                    rows_kernel,
                    (field, shaped((24, width)), shaped((24, width)), field),
                    fold,
                )(part, other, q, others)
            else:
                total, up, down = call(
                    lambda a, b, c, d, e, g: rows_kernel(a, b, None, None, c, d, e, None, g),
                    (field, shaped((16, width)), shaped((16, width))),
                    fold,
                )(part, other)
        if iteration == 0:
            twin_base, twin_density = (), ()
            if twins:
                sent = lax.optimization_barrier((part, base, density))
                twin_base = (swap(sent[1], "gz", 1),)
                twin_density = (swap(sent[2], "gz", 1),)
            wide = WIDE * (1 + len(twin_base))
            bands, turned = call(
                kernel_of(turn_kernel),
                (shaped((span * PART, wide), bf16), shaped((wide, span * PART), bf16)),
            )(*twin_base, bands)
        below = lax.ppermute(up, "gx", upward)
        above = lax.ppermute(down, "gx", downward)
        if iteration == 0:
            edge = call(
                kernel_of(middle_kernel), shaped((PART, 128)), (edge_stack, edge_prod)
            )(total, above, below, q, density_edge, bands, turned, *twin_density)
            part, q = call(kernel_of(middle_field_kernel), (field, field), (stack, prod))(
                total, above, below, q, density, bands, turned, *twin_density
            )
    return call(
        kernel_of(last_kernel),
        (shaped((3, share, cells_y)), shaped((layers, cells_x, cells_y))),
        (
            ((3, share, cells_y), f32),
            ((layers, cells_x, cells_y), f32),
            pltpu.SemaphoreType.DMA((3,)),
            full,
            ((span * PART, cells_y), bf16),
            ((3, cells_x, cells_y), f32),
        ),
        smem=(0,),
        results=pltpu.HBM,
    )(start, total, above, below, q, turned, observed)


def solution(mesh):
    placed = (
        P(("runs", "gz"), "gx", "gy"),
        P(("runs", "gz"), "gx", "gy"),
        P("runs"),
        P(("runs", "gz"), None, None),
        P("runs", "gx", "gy"),
    )
    return jax.shard_map(
        body,
        mesh=mesh,
        in_specs=placed,
        out_specs=(P("runs", ("gx", "gz"), "gy"), P(("runs", "gz"), "gx", "gy")),
        check_vma=False,
    )
```

```python
import functools

import jax
import jax.numpy as jnp
from jax import lax
from jax.experimental import pallas as pl
from jax.experimental.pallas import tpu as pltpu
from jax.sharding import PartitionSpec as P


descent = 0.01
ITERS = 2
PART = 48
EDGE = 9
FULL = 64
WIDE = 256
GRANT = 16 * 2**20

f32 = jnp.float32
bf16 = jnp.bfloat16


def iota(shape, dim):
    return lax.broadcasted_iota(jnp.int32, shape, dim)


def up_rows(v):
    return pltpu.roll(v, v.shape[0] - 1, 0)


def down_rows(v):
    return pltpu.roll(v, 1, 0)


def right(v):
    return pltpu.roll(v, v.shape[1] - 1, 1)


def left(v):
    return pltpu.roll(v, 1, 1)


def tensor_fields(s):
    above, below = up_rows(s), down_rows(s)
    along_x = above + below - 2.0 * s
    along_y = right(s) + left(s) - 2.0 * s
    diff = above - below
    mixed = 0.25 * (right(diff) - left(diff))
    return along_x, along_y, mixed


def adjoint_of(r0, r1, r2):
    cross = 0.25 * (right(r2) - left(r2))
    return (
        up_rows(r0 + cross)
        + down_rows(r0 - cross)
        - 2.0 * r0
        + right(r1)
        + left(r1)
        - 2.0 * r1
    )


def adjoint_square(s):
    def row(k):
        return pltpu.roll(s, -k % FULL, 0)[8 : 8 + PART]

    def column(v, k):
        return pltpu.roll(v, -k % v.shape[1], 1)

    centre = s[8 : 8 + PART]
    near, far = row(1) + row(-1), row(2) + row(-2)
    mixed = 0.0625 * (far - 2.0 * centre)
    both = centre + mixed
    return (
        (far - 4.0 * near + 12.0 * centre - 2.0 * mixed)
        + (column(both, 2) + column(both, -2))
        - 4.0 * (column(centre, 1) + column(centre, -1))
    )


def edge_columns(first, last, side=None):
    lane = iota(first.shape, 1)
    inside = jnp.where(lane < 64, pltpu.roll(first, 32, 1), last)
    if side is None:
        return jnp.where(lane < 32, jnp.zeros_like(first), inside)
    outside = jnp.where(lane < 16, side, pltpu.roll(side, 32, 1))
    return jnp.where(lane < 32, outside, inside)


def edges_of(v):
    width = v.shape[1]
    return edge_columns(v[:, :128], v[:, width - 256 : width - 128], v[:, width - 128 :])


def add_edges(field, message):
    width = field.shape[1]
    lane = iota(message.shape, 1)
    turned = pltpu.roll(message, 96, 1)
    zero = jnp.zeros_like(message)
    first = field[:, :128] + jnp.where(lane < EDGE, message, zero)
    last = field[:, width - 256 : width - 128] + jnp.where(lane >= 128 - EDGE, turned, zero)
    side = field[:, width - 128 :] + jnp.where(
        lane < EDGE, turned, jnp.where(lane >= 128 - EDGE, message, zero)
    )
    return jnp.concatenate([first, field[:, 128 : width - 256], last, side], axis=1)


def kernel_rows(k_ref, taps_ref):
    layers, span, _ = k_ref.shape
    taps_ref[...] = jnp.zeros(taps_ref.shape, f32)
    for l in range(layers):
        taps_ref[16 * l : 16 * l + span, :span] = k_ref[l].astype(f32)
    shape = (taps_ref.shape[0], WIDE)
    source = iota(shape, 0)
    place = jnp.where(32 * (source >> 4) + (source & 15) == iota(shape, 1), 1.0, 0.0)
    return lax.dot_general(
        taps_ref[...].astype(bf16),
        place.astype(bf16),
        (((0,), (0,)), ((), ())),
        preferred_element_type=f32,
    )


def build_bands(base_ref, bands_ref, span):
    tap = (iota((8, 128), 1) & 31) - iota((8, 128), 0) + 15
    keep = [(tap - 8 * g >= 0) & (tap - 8 * g < span) for g in range(PART // 8)]
    for block in range(WIDE // 128):
        for j in range(span):
            row = jnp.broadcast_to(
                base_ref[j : j + 1, 128 * block : 128 * block + 128], (8, 128)
            )
            moved = [
                jnp.where(
                    keep[g],
                    pltpu.roll(row, (8 * g - 15) % 128, 1, stride=1, stride_axis=0),
                    0.0,
                )
                for g in range(PART // 8)
            ]
            bands_ref[
                j * PART : (j + 1) * PART, 128 * block : 128 * block + 128
            ] = jnp.concatenate(moved, axis=0).astype(bf16)


def edge_message(bands, rounded, prod_ref, span, radius):
    prod_ref[...] = jnp.dot(bands, rounded, preferred_element_type=f32)
    total = prod_ref[radius * PART : (radius + 1) * PART, :]
    for j in range(span):
        if j != radius:
            piece = prod_ref[j * PART : (j + 1) * PART, :]
            total = total + pltpu.roll(piece, (radius - j) % 128, 1)
    return total


def scatter_surface(bands, rounded, prod_ref, span, radius):
    width = rounded.shape[1] + 128
    prod_ref[...] = jnp.dot(bands, rounded, preferred_element_type=f32)
    total = jnp.zeros((PART, width), f32)
    side = jnp.zeros((PART, 128), f32)
    for j in range(span):
        piece = jnp.concatenate([prod_ref[j * PART : (j + 1) * PART, :], side], axis=1)
        shift = (radius - j) % width
        total = total + (pltpu.roll(piece, shift, 1) if shift else piece)
    return total


def fold_side(side):
    lane = iota((8, 128), 1)
    turned = pltpu.roll(side, EDGE, 1)
    folded = jnp.zeros((8, 128), f32)
    for g in range(PART // 8):
        piece = jnp.where(lane < 2 * EDGE, turned[8 * g : 8 * g + 8], 0.0)
        folded = folded + (pltpu.roll(piece, 2 * EDGE * g, 1) if g else piece)
    return folded


def unfold_side(folded):
    lane = iota((8, 128), 1)
    pieces = []
    for g in range(PART // 8):
        piece = pltpu.roll(folded, 128 - 2 * EDGE * g, 1) if g else folded
        pieces.append(jnp.where(lane < 2 * EDGE, piece, 0.0))
    return pltpu.roll(jnp.concatenate(pieces, axis=0), 128 - EDGE, 1)


def first_kernel(
    labels_hbm, background_hbm, contrasts_hbm, k_hbm, observed_hbm,
    edge_ref, density_edge_ref, density_ref, bands_ref, observed_ref,
    labels_ref, background_ref, contrasts_ref, k_ref, sems,
    taps_ref, base_ref, prod_ref,
):
    layers, cells_x, cells_y = labels_ref.shape
    span = k_ref.shape[1]
    copies = [
        pltpu.make_async_copy(source, target, sems.at[n])
        for n, (source, target) in enumerate(
            (
                (k_hbm, k_ref),
                (contrasts_hbm, contrasts_ref),
                (labels_hbm, labels_ref),
                (background_hbm, background_ref),
                (observed_hbm, observed_ref),
            )
        )
    ]
    for copy in copies:
        copy.start()
    copies[0].wait()
    base_ref[...] = kernel_rows(k_ref, taps_ref)
    build_bands(base_ref, bands_ref, span)
    for copy in copies[1:]:
        copy.wait()
    classes = contrasts_ref.shape[0]
    for l in range(layers):
        label = labels_ref[l]
        value = jnp.full(label.shape, contrasts_ref[0], f32)
        for c in range(1, classes):
            value = jnp.where(label == c, contrasts_ref[c], value)
        density = value + background_ref[l].astype(f32)
        rows = slice(l * cells_x, (l + 1) * cells_x)
        density_ref[rows, :] = density
        density_edge_ref[rows, :] = edge_columns(density[:, :128], density[:, cells_y - 128 :])
    edge_ref[:PART, :] = edge_message(
        bands_ref[:, : layers * cells_x],
        density_edge_ref[...].astype(bf16),
        prod_ref,
        span,
        (span - 1) // 2,
    )
    empty = jnp.zeros((8, 128), f32)
    edge_ref[PART:, :] = adjoint_of(
        *(
            jnp.concatenate(
                [
                    empty,
                    edge_columns(observed_ref[k, :, :128], observed_ref[k, :, cells_y - 128 :]),
                    empty,
                ],
                axis=0,
            )
            for k in range(3)
        )
    )


def first_field_kernel(
    density_ref, bands_ref, observed_ref, part_ref, q_ref, prod_ref, obs_ref, *, span
):
    lanes, cells_y = density_ref.shape
    part_ref[...] = scatter_surface(
        bands_ref[:, :lanes], density_ref[...].astype(bf16), prod_ref, span, (span - 1) // 2
    )
    obs_ref[...] = jnp.zeros(obs_ref.shape, f32)
    for k in range(3):
        obs_ref[k, 8 : PART - 8, :cells_y] = observed_ref[k]
    q_ref[...] = adjoint_of(obs_ref[0], obs_ref[1], obs_ref[2])


def transpose_kernel(bands_ref, out_ref):
    out_ref[...] = bands_ref[...].astype(f32).T.astype(bf16)


def edges_kernel(part_ref, edge_ref, out_ref):
    cells_y = out_ref.shape[1]
    part = add_edges(part_ref[...], edge_ref[:PART, :])
    out_ref[...] = part[:, :cells_y]
    folded = fold_side(part[:, cells_y:])
    for n in range(8):
        row = (PART - 1) * (n // 4)
        out_ref[row : row + 1, 128 * (n % 4) : 128 * (n % 4 + 1)] = folded[n : n + 1]


def send_rows(sum_ref, up_ref, down_ref):
    sub = iota((8, sum_ref.shape[1]), 0)
    up_ref[:8, :] = sum_ref[8:16, :]
    up_ref[8:16, :] = jnp.where(sub >= 1, sum_ref[:8, :], sum_ref[16:24, :])
    down_ref[:8, :] = sum_ref[32:40, :]
    down_ref[8:16, :] = jnp.where(sub < 7, sum_ref[40:48, :], sum_ref[24:32, :])


def rows_kernel(
    part_ref, other_ref, q_ref, edge_ref, sum_ref, up_ref, down_ref, q_out_ref, fold_ref
):
    cells_y = part_ref.shape[1]
    sum_ref[:, :cells_y] = part_ref[...] + other_ref[...]
    for n in range(8):
        row = (PART - 1) * (n // 4)
        fold_ref[n : n + 1, :] = sum_ref[row : row + 1, 128 * (n % 4) : 128 * (n % 4 + 1)]
    sum_ref[:, cells_y:] = unfold_side(fold_ref[...])
    zero = jnp.zeros((1, cells_y), f32)
    sum_ref[:1, :cells_y] = zero
    sum_ref[PART - 1 :, :cells_y] = zero
    send_rows(sum_ref, up_ref, down_ref)
    if q_ref is not None:
        sub = iota((8, sum_ref.shape[1]), 0)
        q_out_ref[...] = add_edges(q_ref[...], edge_ref[PART:, :])
        up_ref[16:24, :] = jnp.where(sub < 7, q_out_ref[8:16, :], q_out_ref[:8, :])
        down_ref[16:24, :] = jnp.where(sub >= 1, q_out_ref[32:40, :], q_out_ref[40:48, :])


def full_surface(total, above, below):
    shape = (8, total.shape[1])
    sub = iota(shape, 0)
    zero = jnp.zeros(shape, f32)
    return jnp.concatenate(
        [
            jnp.where(sub == 7, above[8:16], zero),
            total[:8] + above[:8],
            total[8:16] + jnp.where(sub < 7, above[8:16], zero),
            total[16:32],
            total[32:40] + jnp.where(sub >= 1, below[8:16], zero),
            total[40:48] + below[:8],
            jnp.where(sub == 0, below[8:16], zero),
        ],
        axis=0,
    )


def full_q(q, above, below):
    shape = (8, q.shape[1])
    sub = iota(shape, 0)
    zero = jnp.zeros(shape, f32)
    return jnp.concatenate(
        [
            q[:8] + jnp.where(sub >= 1, above[16:24], zero),
            q[8:16] + jnp.where(sub == 0, above[16:24], zero),
            q[16:32],
            q[32:40] + jnp.where(sub == 7, below[16:24], zero),
            q[40:48] + jnp.where(sub < 7, below[16:24], zero),
        ],
        axis=0,
    )


def stack_shifts(adjoint, stack_ref, columns, span, radius):
    for j in range(span):
        shift = (j - radius) % adjoint.shape[1]
        moved = pltpu.roll(adjoint, shift, 1) if shift else adjoint
        stack_ref[j * PART : (j + 1) * PART, columns] = moved[:, columns]


def rounded_adjoint(s, q):
    return (adjoint_square(s) - q).astype(bf16)


def field_after_step(refs, out_refs, scratch_refs, span):
    sum_ref, above_ref, below_ref, q_ref, density_ref, bands_ref, turned_ref = refs
    part_ref, q_out_ref = out_refs
    stack_ref, prod_ref = scratch_refs
    radius = (span - 1) // 2
    lanes, cells_y = density_ref.shape
    above, below = above_ref[...], below_ref[...]
    q = full_q(q_ref[...], above, below)
    q_out_ref[...] = q
    adjoint = rounded_adjoint(full_surface(sum_ref[...], above, below), q)
    stack_shifts(adjoint, stack_ref, slice(0, cells_y), span, radius)
    gradient = jnp.dot(turned_ref[:lanes, :], stack_ref[...], preferred_element_type=f32)
    density = density_ref[...] - descent * gradient
    part_ref[...] = scatter_surface(
        bands_ref[:, :lanes], density.astype(bf16), prod_ref, span, radius
    )


def middle_kernel(
    sum_ref, above_ref, below_ref, q_ref, density_ref, bands_ref, turned_ref,
    density_edge_ref,
    edge_ref, part_ref, q_out_ref,
    edge_stack_ref, edge_prod_ref, stack_ref, prod_ref, *, span,
):
    radius = (span - 1) // 2
    lanes = density_edge_ref.shape[0]
    total, q = edges_of(sum_ref[...]), edges_of(q_ref[...])
    above, below = edges_of(above_ref[...]), edges_of(below_ref[...])
    adjoint = rounded_adjoint(full_surface(total, above, below), full_q(q, above, below))
    stack_shifts(adjoint, edge_stack_ref, slice(0, 128), span, radius)
    gradient = jnp.dot(
        turned_ref[:lanes, :], edge_stack_ref[...], preferred_element_type=f32
    )
    density = density_edge_ref[...] - descent * gradient
    lane = iota(density.shape, 1)
    keep = ((lane >= 32) & (lane < 48)) | (lane >= 112)
    density = jnp.where(keep, density, 0.0)
    edge_ref[...] = edge_message(
        bands_ref[:, :lanes], density.astype(bf16), edge_prod_ref, span, radius
    )

    @pl.when(lax.axis_index("gy") == 1)
    def _():
        field_after_step(
            (sum_ref, above_ref, below_ref, q_ref, density_ref, bands_ref, turned_ref),
            (part_ref, q_out_ref),
            (stack_ref, prod_ref),
            span,
        )


def middle_field_kernel(
    sum_ref, above_ref, below_ref, q_ref, density_ref, bands_ref, turned_ref,
    part_in_ref, q_in_ref,
    part_ref, q_out_ref,
    stack_ref, prod_ref, *, span,
):
    @pl.when(lax.axis_index("gy") == 0)
    def _():
        field_after_step(
            (sum_ref, above_ref, below_ref, q_ref, density_ref, bands_ref, turned_ref),
            (part_ref, q_out_ref),
            (stack_ref, prod_ref),
            span,
        )


def last_kernel(
    start_ref, sum_ref, above_ref, below_ref, q_ref, turned_ref, observed_ref,
    residual_hbm, gradient_hbm,
    residual_ref, gradient_ref, sems, full_ref, stack_ref, misfit_ref, *, span,
):
    radius = (span - 1) // 2
    layers, cells_x, cells_y = gradient_ref.shape
    s = full_surface(sum_ref[...], above_ref[...], below_ref[...])
    full_ref[...] = s
    adjoint = rounded_adjoint(s, q_ref[...])
    turned = turned_ref[: layers * cells_x, :]
    half = cells_y // 2
    copies = []
    for n in range(2):
        columns = slice(n * half, (n + 1) * half)
        stack_shifts(adjoint, stack_ref, columns, span, radius)
        gradient = jnp.dot(turned, stack_ref[:, columns], preferred_element_type=f32)
        for l in range(layers):
            gradient_ref[l, :, columns] = gradient[l * cells_x : (l + 1) * cells_x, :]
        copies.append(
            pltpu.make_async_copy(
                gradient_ref.at[:, :, columns], gradient_hbm.at[:, :, columns], sems.at[n]
            )
        )
        copies[-1].start()
    share = residual_ref.shape[1]
    if share % 8 == 0:
        start = pl.multiple_of(start_ref[0], 8)
        fields = tensor_fields(full_ref[pl.ds(start + 8, share + 16), :])
        for k in range(3):
            residual_ref[k] = (
                fields[k][8 : 8 + share, :cells_y] - observed_ref[k, pl.ds(start, share), :]
            )
    else:
        fields = tensor_fields(full_ref[...])
        for k in range(3):
            misfit_ref[k] = fields[k][16 : 16 + cells_x, :cells_y] - observed_ref[k]
        for start in range(0, cells_x, share):

            @pl.when(start_ref[0] == start)
            def _():
                residual_ref[...] = misfit_ref[:, start : start + share, :]

    copies.append(pltpu.make_async_copy(residual_ref, residual_hbm, sems.at[2]))
    copies[-1].start()
    for copy in copies:
        copy.wait()


def call(
    kernel, outs, scratch=(), inputs=pltpu.VMEM, smem=(), results=pltpu.VMEM, aliases={}
):
    made = pl.BlockSpec(memory_space=results)
    given = pl.BlockSpec(memory_space=inputs)
    scalar = pl.BlockSpec(memory_space=pltpu.SMEM)

    def run(*operands):
        if inputs is pltpu.HBM:
            operands = [pltpu.with_memory_space_constraint(v, pltpu.HBM) for v in operands]
        return pl.pallas_call(
            kernel,
            out_shape=outs,
            in_specs=[scalar if i in smem else given for i in range(len(operands))],
            out_specs=jax.tree.map(lambda _: made, outs),
            scratch_shapes=[
                item if not isinstance(item, tuple) else pltpu.VMEM(*item) for item in scratch
            ],
            compiler_params=pltpu.CompilerParams(vmem_limit_bytes=GRANT),
            input_output_aliases=aliases,
        )(*operands)

    return run


def shaped(shape, kind=f32):
    return jax.ShapeDtypeStruct(shape, kind)


def swap(value, axis, distance):
    peers = lax.axis_size(axis)
    return lax.ppermute(value, axis, [(i, i ^ distance) for i in range(peers)])


def body(labels, background, contrasts, kernels, observed):
    layers, cells_x, cells_y = labels.shape
    span = kernels.shape[1]
    lanes = layers * cells_x
    width = cells_y + 128
    depth_peers, row_peers = lax.axis_size("gz"), lax.axis_size("gx")
    assert cells_x == 32 and span == 15 and lanes <= 192 and cells_y == 512 and lax.axis_size("gy") == 2
    assert depth_peers & (depth_peers - 1) == 0
    share = cells_x // depth_peers
    upward = [(i, (i - 1) % row_peers) for i in range(row_peers)]
    downward = [(j, i) for i, j in upward]
    full = ((FULL, width), f32)
    prod = ((span * PART, cells_y), f32)
    stack = ((span * PART, cells_y), bf16)
    edge_prod = ((span * PART, 128), f32)
    edge_stack = ((span * PART, 128), bf16)
    field = shaped((PART, width))

    def kernel_of(body_of):
        return functools.partial(body_of, span=span)

    edge, density_edge, density, bands, observed = call(
        first_kernel,
        (
            shaped((2 * PART, 128)),
            shaped((lanes, 128)),
            shaped((lanes, cells_y)),
            shaped((span * PART, WIDE), bf16),
            shaped(observed.shape),
        ),
        (
            (labels.shape, labels.dtype),
            (background.shape, background.dtype),
            pltpu.SMEM(contrasts.shape, contrasts.dtype),
            (kernels.shape, kernels.dtype),
            pltpu.SemaphoreType.DMA((5,)),
            ((16 * layers, 16), f32),
            ((16, WIDE), f32),
            edge_prod,
        ),
        inputs=pltpu.HBM,
    )(labels, background, contrasts, kernels, observed)
    part, q = call(
        kernel_of(first_field_kernel), (field, field), (prod, ((3, PART, width), f32))
    )(density, bands, observed)
    start = (lax.axis_index("gz") * share).astype(jnp.int32).reshape(1)

    turned = call(transpose_kernel, shaped((WIDE, span * PART), bf16))(bands)
    fold = (((8, 128), f32),)
    for iteration in range(ITERS):
        others = swap(edge, "gy", 1)
        part = call(edges_kernel, shaped((PART, cells_y)))(part, others)
        for bit in range(depth_peers.bit_length() - 2):
            part = part + swap(part, "gz", 2 << bit)
        other = swap(part, "gz", 1)
        if iteration == 0:
            total, up, down, q = call(
                rows_kernel, (field, shaped((24, width)), shaped((24, width)), field), fold
            )(part, other, q, others)
        else:
            total, up, down = call(
                lambda a, b, c, d, e, g: rows_kernel(a, b, None, None, c, d, e, None, g),
                (field, shaped((16, width)), shaped((16, width))),
                fold,
            )(part, other)
        below = lax.ppermute(up, "gx", upward)
        above = lax.ppermute(down, "gx", downward)
        if iteration == 0:
            known = (total, above, below, q, density, bands, turned)
            edge, part, q = call(
                kernel_of(middle_kernel),
                (shaped((PART, 128)), field, field),
                (edge_stack, edge_prod, stack, prod),
            )(*known, density_edge)
            part, q = call(
                kernel_of(middle_field_kernel),
                (field, field),
                (stack, prod),
                aliases={7: 0, 8: 1},
            )(*known, part, q)
    return call(
        kernel_of(last_kernel),
        (shaped((3, share, cells_y)), shaped((layers, cells_x, cells_y))),
        (
            ((3, share, cells_y), f32),
            ((layers, cells_x, cells_y), f32),
            pltpu.SemaphoreType.DMA((3,)),
            full,
            ((span * PART, cells_y), bf16),
            ((3, cells_x, cells_y), f32),
        ),
        smem=(0,),
        results=pltpu.HBM,
    )(start, total, above, below, q, turned, observed)


def solution(mesh):
    placed = (
        P(("runs", "gz"), "gx", "gy"),
        P(("runs", "gz"), "gx", "gy"),
        P("runs"),
        P(("runs", "gz"), None, None),
        P("runs", "gx", "gy"),
    )
    return jax.shard_map(
        body,
        mesh=mesh,
        in_specs=placed,
        out_specs=(P("runs", ("gx", "gz"), "gy"), P(("runs", "gz"), "gx", "gy")),
        check_vma=False,
    )
```

```python
import functools

import jax
import jax.numpy as jnp
from jax import lax
from jax.experimental import pallas as pl
from jax.experimental.pallas import tpu as pltpu
from jax.sharding import PartitionSpec as P


descent = 0.01
ITERS = 2
PART = 48
EDGE = 9
FULL = 64
WIDE = 256
GRANT = 16 * 2**20

f32 = jnp.float32
bf16 = jnp.bfloat16


def iota(shape, dim):
    return lax.broadcasted_iota(jnp.int32, shape, dim)


def up_rows(v):
    return pltpu.roll(v, v.shape[0] - 1, 0)


def down_rows(v):
    return pltpu.roll(v, 1, 0)


def right(v):
    return pltpu.roll(v, v.shape[1] - 1, 1)


def left(v):
    return pltpu.roll(v, 1, 1)


def tensor_fields(s):
    above, below = up_rows(s), down_rows(s)
    along_x = above + below - 2.0 * s
    along_y = right(s) + left(s) - 2.0 * s
    diff = above - below
    mixed = 0.25 * (right(diff) - left(diff))
    return along_x, along_y, mixed


def adjoint_of(r0, r1, r2):
    cross = 0.25 * (right(r2) - left(r2))
    return (
        up_rows(r0 + cross)
        + down_rows(r0 - cross)
        - 2.0 * r0
        + right(r1)
        + left(r1)
        - 2.0 * r1
    )


def adjoint_square(s):
    def row(k):
        return pltpu.roll(s, -k % FULL, 0)[8 : 8 + PART]

    def column(v, k):
        return pltpu.roll(v, -k % v.shape[1], 1)

    centre = s[8 : 8 + PART]
    near, far = row(1) + row(-1), row(2) + row(-2)
    mixed = 0.0625 * (far - 2.0 * centre)
    both = centre + mixed
    return (
        (far - 4.0 * near + 12.0 * centre - 2.0 * mixed)
        + (column(both, 2) + column(both, -2))
        - 4.0 * (column(centre, 1) + column(centre, -1))
    )


def edge_columns(first, last, side=None):
    lane = iota(first.shape, 1)
    inside = jnp.where(lane < 64, pltpu.roll(first, 32, 1), last)
    if side is None:
        return jnp.where(lane < 32, jnp.zeros_like(first), inside)
    outside = jnp.where(lane < 16, side, pltpu.roll(side, 32, 1))
    return jnp.where(lane < 32, outside, inside)


def edges_of(v):
    width = v.shape[1]
    return edge_columns(v[:, :128], v[:, width - 256 : width - 128], v[:, width - 128 :])


def add_edges(field, message):
    width = field.shape[1]
    lane = iota(message.shape, 1)
    turned = pltpu.roll(message, 96, 1)
    zero = jnp.zeros_like(message)
    first = field[:, :128] + jnp.where(lane < EDGE, message, zero)
    last = field[:, width - 256 : width - 128] + jnp.where(lane >= 128 - EDGE, turned, zero)
    side = field[:, width - 128 :] + jnp.where(
        lane < EDGE, turned, jnp.where(lane >= 128 - EDGE, message, zero)
    )
    return jnp.concatenate([first, field[:, 128 : width - 256], last, side], axis=1)


def kernel_rows(k_ref, taps_ref):
    layers, span, _ = k_ref.shape
    taps_ref[...] = jnp.zeros(taps_ref.shape, f32)
    for l in range(layers):
        taps_ref[16 * l : 16 * l + span, :span] = k_ref[l].astype(f32)
    shape = (taps_ref.shape[0], WIDE)
    source = iota(shape, 0)
    place = jnp.where(32 * (source >> 4) + (source & 15) == iota(shape, 1), 1.0, 0.0)
    return lax.dot_general(
        taps_ref[...].astype(bf16),
        place.astype(bf16),
        (((0,), (0,)), ((), ())),
        preferred_element_type=f32,
    )


def build_bands(base_ref, bands_ref, span):
    tap = (iota((8, 128), 1) & 31) - iota((8, 128), 0) + 15
    keep = [(tap - 8 * g >= 0) & (tap - 8 * g < span) for g in range(PART // 8)]
    for block in range(WIDE // 128):
        for j in range(span):
            row = jnp.broadcast_to(
                base_ref[j : j + 1, 128 * block : 128 * block + 128], (8, 128)
            )
            moved = [
                jnp.where(
                    keep[g],
                    pltpu.roll(row, (8 * g - 15) % 128, 1, stride=1, stride_axis=0),
                    0.0,
                )
                for g in range(PART // 8)
            ]
            bands_ref[
                j * PART : (j + 1) * PART, 128 * block : 128 * block + 128
            ] = jnp.concatenate(moved, axis=0).astype(bf16)


def edge_message(bands, rounded, prod_ref, span, radius):
    prod_ref[...] = jnp.dot(bands, rounded, preferred_element_type=f32)
    total = prod_ref[radius * PART : (radius + 1) * PART, :]
    for j in range(span):
        if j != radius:
            piece = prod_ref[j * PART : (j + 1) * PART, :]
            total = total + pltpu.roll(piece, (radius - j) % 128, 1)
    return total


def scatter_surface(bands, rounded, prod_ref, span, radius):
    width = rounded.shape[1] + 128
    prod_ref[...] = jnp.dot(bands, rounded, preferred_element_type=f32)
    total = jnp.zeros((PART, width), f32)
    side = jnp.zeros((PART, 128), f32)
    for j in range(span):
        piece = jnp.concatenate([prod_ref[j * PART : (j + 1) * PART, :], side], axis=1)
        shift = (radius - j) % width
        total = total + (pltpu.roll(piece, shift, 1) if shift else piece)
    return total


def fold_side(side):
    lane = iota((8, 128), 1)
    used = (lane < EDGE) | (lane >= 128 - EDGE)
    folded = jnp.zeros((8, 128), f32)
    for g in range(PART // 8):
        piece = jnp.where(used, side[8 * g : 8 * g + 8], 0.0)
        folded = folded + pltpu.roll(piece, EDGE + 2 * EDGE * g, 1)
    return folded


def unfold_side(folded):
    lane = iota((8, 128), 1)
    used = (lane < EDGE) | (lane >= 128 - EDGE)
    pieces = []
    for g in range(PART // 8):
        piece = pltpu.roll(folded, 128 - EDGE - 2 * EDGE * g, 1)
        pieces.append(jnp.where(used, piece, 0.0))
    return jnp.concatenate(pieces, axis=0)


def first_kernel(
    labels_hbm, background_hbm, contrasts_hbm, k_hbm, observed_hbm,
    edge_ref, density_edge_ref, density_ref, bands_ref, observed_ref,
    labels_ref, background_ref, contrasts_ref, k_ref, sems,
    taps_ref, base_ref, prod_ref,
):
    layers, cells_x, cells_y = labels_ref.shape
    span = k_ref.shape[1]
    copies = [
        pltpu.make_async_copy(source, target, sems.at[n])
        for n, (source, target) in enumerate(
            (
                (k_hbm, k_ref),
                (contrasts_hbm, contrasts_ref),
                (labels_hbm, labels_ref),
                (background_hbm, background_ref),
                (observed_hbm, observed_ref),
            )
        )
    ]
    for copy in copies:
        copy.start()
    copies[0].wait()
    base_ref[...] = kernel_rows(k_ref, taps_ref)
    build_bands(base_ref, bands_ref, span)
    for copy in copies[1:]:
        copy.wait()
    classes = contrasts_ref.shape[0]
    for l in range(layers):
        label = labels_ref[l]
        value = jnp.full(label.shape, contrasts_ref[0], f32)
        for c in range(1, classes):
            value = jnp.where(label == c, contrasts_ref[c], value)
        density = value + background_ref[l].astype(f32)
        rows = slice(l * cells_x, (l + 1) * cells_x)
        density_ref[rows, :] = density
        density_edge_ref[rows, :] = edge_columns(density[:, :128], density[:, cells_y - 128 :])
    edge_ref[:PART, :] = edge_message(
        bands_ref[:, : layers * cells_x],
        density_edge_ref[...].astype(bf16),
        prod_ref,
        span,
        (span - 1) // 2,
    )
    empty = jnp.zeros((8, 128), f32)
    edge_ref[PART:, :] = adjoint_of(
        *(
            jnp.concatenate(
                [
                    empty,
                    edge_columns(observed_ref[k, :, :128], observed_ref[k, :, cells_y - 128 :]),
                    empty,
                ],
                axis=0,
            )
            for k in range(3)
        )
    )


def first_field_kernel(
    density_ref, bands_ref, observed_ref, part_ref, q_ref, prod_ref, obs_ref, *, span
):
    lanes, cells_y = density_ref.shape
    part_ref[...] = scatter_surface(
        bands_ref[:, :lanes], density_ref[...].astype(bf16), prod_ref, span, (span - 1) // 2
    )
    obs_ref[...] = jnp.zeros(obs_ref.shape, f32)
    for k in range(3):
        obs_ref[k, 8 : PART - 8, :cells_y] = observed_ref[k]
    q_ref[...] = adjoint_of(obs_ref[0], obs_ref[1], obs_ref[2])


def transpose_kernel(bands_ref, out_ref):
    out_ref[...] = bands_ref[...].astype(f32).T.astype(bf16)


def edges_kernel(part_ref, edge_ref, out_ref):
    cells_y = out_ref.shape[1]
    part = add_edges(part_ref[...], edge_ref[:PART, :])
    out_ref[...] = part[:, :cells_y]
    folded = fold_side(part[:, cells_y:])
    for n in range(8):
        row = (PART - 1) * (n // 4)
        out_ref[row : row + 1, 128 * (n % 4) : 128 * (n % 4 + 1)] = folded[n : n + 1]


def send_rows(sum_ref, up_ref, down_ref):
    sub = iota((8, sum_ref.shape[1]), 0)
    up_ref[:8, :] = sum_ref[8:16, :]
    up_ref[8:16, :] = jnp.where(sub >= 1, sum_ref[:8, :], sum_ref[16:24, :])
    down_ref[:8, :] = sum_ref[32:40, :]
    down_ref[8:16, :] = jnp.where(sub < 7, sum_ref[40:48, :], sum_ref[24:32, :])


def rows_kernel(
    part_ref, other_ref, q_ref, edge_ref, sum_ref, up_ref, down_ref, q_out_ref, fold_ref
):
    cells_y = part_ref.shape[1]
    sum_ref[:, :cells_y] = part_ref[...] + other_ref[...]
    for n in range(8):
        row = (PART - 1) * (n // 4)
        fold_ref[n : n + 1, :] = sum_ref[row : row + 1, 128 * (n % 4) : 128 * (n % 4 + 1)]
    sum_ref[:, cells_y:] = unfold_side(fold_ref[...])
    zero = jnp.zeros((1, cells_y), f32)
    sum_ref[:1, :cells_y] = zero
    sum_ref[PART - 1 :, :cells_y] = zero
    send_rows(sum_ref, up_ref, down_ref)
    if q_ref is not None:
        sub = iota((8, sum_ref.shape[1]), 0)
        q_out_ref[...] = add_edges(q_ref[...], edge_ref[PART:, :])
        up_ref[16:24, :] = jnp.where(sub < 7, q_out_ref[8:16, :], q_out_ref[:8, :])
        down_ref[16:24, :] = jnp.where(sub >= 1, q_out_ref[32:40, :], q_out_ref[40:48, :])


def full_surface(total, above, below):
    shape = (8, total.shape[1])
    sub = iota(shape, 0)
    zero = jnp.zeros(shape, f32)
    return jnp.concatenate(
        [
            jnp.where(sub == 7, above[8:16], zero),
            total[:8] + above[:8],
            total[8:16] + jnp.where(sub < 7, above[8:16], zero),
            total[16:32],
            total[32:40] + jnp.where(sub >= 1, below[8:16], zero),
            total[40:48] + below[:8],
            jnp.where(sub == 0, below[8:16], zero),
        ],
        axis=0,
    )


def full_q(q, above, below):
    shape = (8, q.shape[1])
    sub = iota(shape, 0)
    zero = jnp.zeros(shape, f32)
    return jnp.concatenate(
        [
            q[:8] + jnp.where(sub >= 1, above[16:24], zero),
            q[8:16] + jnp.where(sub == 0, above[16:24], zero),
            q[16:32],
            q[32:40] + jnp.where(sub == 7, below[16:24], zero),
            q[40:48] + jnp.where(sub < 7, below[16:24], zero),
        ],
        axis=0,
    )


def stack_shifts(adjoint, stack_ref, columns, span, radius):
    for j in range(span):
        shift = (j - radius) % adjoint.shape[1]
        moved = pltpu.roll(adjoint, shift, 1) if shift else adjoint
        stack_ref[j * PART : (j + 1) * PART, columns] = moved[:, columns]


def rounded_adjoint(s, q):
    return (adjoint_square(s) - q).astype(bf16)


def field_after_step(refs, out_refs, scratch_refs, span):
    sum_ref, above_ref, below_ref, q_ref, density_ref, bands_ref, turned_ref = refs
    part_ref, q_out_ref = out_refs
    stack_ref, prod_ref = scratch_refs
    radius = (span - 1) // 2
    lanes, cells_y = density_ref.shape
    above, below = above_ref[...], below_ref[...]
    q = full_q(q_ref[...], above, below)
    q_out_ref[...] = q
    adjoint = rounded_adjoint(full_surface(sum_ref[...], above, below), q)
    stack_shifts(adjoint, stack_ref, slice(0, cells_y), span, radius)
    gradient = jnp.dot(turned_ref[:lanes, :], stack_ref[...], preferred_element_type=f32)
    density = density_ref[...] - descent * gradient
    part_ref[...] = scatter_surface(
        bands_ref[:, :lanes], density.astype(bf16), prod_ref, span, radius
    )


def middle_kernel(
    sum_ref, above_ref, below_ref, q_ref, density_ref, bands_ref, turned_ref,
    density_edge_ref,
    edge_ref, part_ref, q_out_ref,
    edge_stack_ref, edge_prod_ref, stack_ref, prod_ref, *, span,
):
    radius = (span - 1) // 2
    lanes = density_edge_ref.shape[0]
    total, q = edges_of(sum_ref[...]), edges_of(q_ref[...])
    above, below = edges_of(above_ref[...]), edges_of(below_ref[...])
    adjoint = rounded_adjoint(full_surface(total, above, below), full_q(q, above, below))
    stack_shifts(adjoint, edge_stack_ref, slice(0, 128), span, radius)
    gradient = jnp.dot(
        turned_ref[:lanes, :], edge_stack_ref[...], preferred_element_type=f32
    )
    density = density_edge_ref[...] - descent * gradient
    lane = iota(density.shape, 1)
    keep = ((lane >= 32) & (lane < 48)) | (lane >= 112)
    density = jnp.where(keep, density, 0.0)
    edge_ref[...] = edge_message(
        bands_ref[:, :lanes], density.astype(bf16), edge_prod_ref, span, radius
    )

    @pl.when(lax.axis_index("gy") == 1)
    def _():
        field_after_step(
            (sum_ref, above_ref, below_ref, q_ref, density_ref, bands_ref, turned_ref),
            (part_ref, q_out_ref),
            (stack_ref, prod_ref),
            span,
        )


def middle_field_kernel(
    sum_ref, above_ref, below_ref, q_ref, density_ref, bands_ref, turned_ref,
    part_in_ref, q_in_ref,
    part_ref, q_out_ref,
    stack_ref, prod_ref, *, span,
):
    @pl.when(lax.axis_index("gy") == 0)
    def _():
        field_after_step(
            (sum_ref, above_ref, below_ref, q_ref, density_ref, bands_ref, turned_ref),
            (part_ref, q_out_ref),
            (stack_ref, prod_ref),
            span,
        )


def last_kernel(
    start_ref, sum_ref, above_ref, below_ref, q_ref, turned_ref, observed_ref,
    residual_hbm, gradient_hbm,
    residual_ref, gradient_ref, sems, full_ref, stack_ref, misfit_ref, *, span,
):
    radius = (span - 1) // 2
    layers, cells_x, cells_y = gradient_ref.shape
    s = full_surface(sum_ref[...], above_ref[...], below_ref[...])
    full_ref[...] = s
    adjoint = rounded_adjoint(s, q_ref[...])
    turned = turned_ref[: layers * cells_x, :]
    half = cells_y // 2
    copies = []
    for n in range(2):
        columns = slice(n * half, (n + 1) * half)
        stack_shifts(adjoint, stack_ref, columns, span, radius)
        gradient = jnp.dot(turned, stack_ref[:, columns], preferred_element_type=f32)
        for l in range(layers):
            gradient_ref[l, :, columns] = gradient[l * cells_x : (l + 1) * cells_x, :]
        copies.append(
            pltpu.make_async_copy(
                gradient_ref.at[:, :, columns], gradient_hbm.at[:, :, columns], sems.at[n]
            )
        )
        copies[-1].start()
    share = residual_ref.shape[1]
    if share % 8 == 0:
        start = pl.multiple_of(start_ref[0], 8)
        fields = tensor_fields(full_ref[pl.ds(start + 8, share + 16), :])
        for k in range(3):
            residual_ref[k] = (
                fields[k][8 : 8 + share, :cells_y] - observed_ref[k, pl.ds(start, share), :]
            )
    else:
        fields = tensor_fields(full_ref[...])
        for k in range(3):
            misfit_ref[k] = fields[k][16 : 16 + cells_x, :cells_y] - observed_ref[k]
        for start in range(0, cells_x, share):

            @pl.when(start_ref[0] == start)
            def _():
                residual_ref[...] = misfit_ref[:, start : start + share, :]

    copies.append(pltpu.make_async_copy(residual_ref, residual_hbm, sems.at[2]))
    copies[-1].start()
    for copy in copies:
        copy.wait()


def call(
    kernel, outs, scratch=(), inputs=pltpu.VMEM, smem=(), results=pltpu.VMEM, aliases={}
):
    made = pl.BlockSpec(memory_space=results)
    given = pl.BlockSpec(memory_space=inputs)
    scalar = pl.BlockSpec(memory_space=pltpu.SMEM)

    def run(*operands):
        if inputs is pltpu.HBM:
            operands = [pltpu.with_memory_space_constraint(v, pltpu.HBM) for v in operands]
        return pl.pallas_call(
            kernel,
            out_shape=outs,
            in_specs=[scalar if i in smem else given for i in range(len(operands))],
            out_specs=jax.tree.map(lambda _: made, outs),
            scratch_shapes=[
                item if not isinstance(item, tuple) else pltpu.VMEM(*item) for item in scratch
            ],
            compiler_params=pltpu.CompilerParams(vmem_limit_bytes=GRANT),
            input_output_aliases=aliases,
        )(*operands)

    return run


def shaped(shape, kind=f32):
    return jax.ShapeDtypeStruct(shape, kind)


def swap(value, axis, distance):
    peers = lax.axis_size(axis)
    return lax.ppermute(value, axis, [(i, i ^ distance) for i in range(peers)])


def body(labels, background, contrasts, kernels, observed):
    layers, cells_x, cells_y = labels.shape
    span = kernels.shape[1]
    lanes = layers * cells_x
    width = cells_y + 128
    depth_peers, row_peers = lax.axis_size("gz"), lax.axis_size("gx")
    assert cells_x == 32 and span == 15 and lanes <= 192 and cells_y == 512 and lax.axis_size("gy") == 2
    assert depth_peers & (depth_peers - 1) == 0
    share = cells_x // depth_peers
    upward = [(i, (i - 1) % row_peers) for i in range(row_peers)]
    downward = [(j, i) for i, j in upward]
    full = ((FULL, width), f32)
    prod = ((span * PART, cells_y), f32)
    stack = ((span * PART, cells_y), bf16)
    edge_prod = ((span * PART, 128), f32)
    edge_stack = ((span * PART, 128), bf16)
    field = shaped((PART, width))

    def kernel_of(body_of):
        return functools.partial(body_of, span=span)

    edge, density_edge, density, bands, observed = call(
        first_kernel,
        (
            shaped((2 * PART, 128)),
            shaped((lanes, 128)),
            shaped((lanes, cells_y)),
            shaped((span * PART, WIDE), bf16),
            shaped(observed.shape),
        ),
        (
            (labels.shape, labels.dtype),
            (background.shape, background.dtype),
            pltpu.SMEM(contrasts.shape, contrasts.dtype),
            (kernels.shape, kernels.dtype),
            pltpu.SemaphoreType.DMA((5,)),
            ((16 * layers, 16), f32),
            ((16, WIDE), f32),
            edge_prod,
        ),
        inputs=pltpu.HBM,
    )(labels, background, contrasts, kernels, observed)
    part, q = call(
        kernel_of(first_field_kernel), (field, field), (prod, ((3, PART, width), f32))
    )(density, bands, observed)
    start = (lax.axis_index("gz") * share).astype(jnp.int32).reshape(1)

    turned = call(transpose_kernel, shaped((WIDE, span * PART), bf16))(bands)
    fold = (((8, 128), f32),)
    for iteration in range(ITERS):
        others = swap(edge, "gy", 1)
        part = call(edges_kernel, shaped((PART, cells_y)))(part, others)
        for bit in range(depth_peers.bit_length() - 2):
            part = part + swap(part, "gz", 2 << bit)
        other = swap(part, "gz", 1)
        if iteration == 0:
            total, up, down, q = call(
                rows_kernel, (field, shaped((24, width)), shaped((24, width)), field), fold
            )(part, other, q, others)
        else:
            total, up, down = call(
                lambda a, b, c, d, e, g: rows_kernel(a, b, None, None, c, d, e, None, g),
                (field, shaped((16, width)), shaped((16, width))),
                fold,
            )(part, other)
        below = lax.ppermute(up, "gx", upward)
        above = lax.ppermute(down, "gx", downward)
        if iteration == 0:
            known = (total, above, below, q, density, bands, turned)
            edge, part, q = call(
                kernel_of(middle_kernel),
                (shaped((PART, 128)), field, field),
                (edge_stack, edge_prod, stack, prod),
            )(*known, density_edge)
            part, q = call(
                kernel_of(middle_field_kernel),
                (field, field),
                (stack, prod),
                aliases={7: 0, 8: 1},
            )(*known, part, q)
    return call(
        kernel_of(last_kernel),
        (shaped((3, share, cells_y)), shaped((layers, cells_x, cells_y))),
        (
            ((3, share, cells_y), f32),
            ((layers, cells_x, cells_y), f32),
            pltpu.SemaphoreType.DMA((3,)),
            full,
            ((span * PART, cells_y), bf16),
            ((3, cells_x, cells_y), f32),
        ),
        smem=(0,),
        results=pltpu.HBM,
    )(start, total, above, below, q, turned, observed)


def solution(mesh):
    placed = (
        P(("runs", "gz"), "gx", "gy"),
        P(("runs", "gz"), "gx", "gy"),
        P("runs"),
        P(("runs", "gz"), None, None),
        P("runs", "gx", "gy"),
    )
    return jax.shard_map(
        body,
        mesh=mesh,
        in_specs=placed,
        out_specs=(P("runs", ("gx", "gz"), "gy"), P(("runs", "gz"), "gx", "gy")),
        check_vma=False,
    )
```

```python
import functools

import jax
import jax.numpy as jnp
from jax import lax
from jax.experimental import pallas as pl
from jax.experimental.pallas import tpu as pltpu
from jax.sharding import PartitionSpec as P


descent = 0.01
ITERS = 2
PART = 48
NEAR, HALO = 9, 25
FULL = 64
WIDE = 256
GRANT = 16 * 2**20

f32 = jnp.float32
bf16 = jnp.bfloat16


def iota(shape, dim):
    return lax.broadcasted_iota(jnp.int32, shape, dim)


def up_rows(v):
    return pltpu.roll(v, v.shape[0] - 1, 0)


def down_rows(v):
    return pltpu.roll(v, 1, 0)


def right(v):
    return pltpu.roll(v, v.shape[1] - 1, 1)


def left(v):
    return pltpu.roll(v, 1, 1)


def tensor_fields(s):
    above, below = up_rows(s), down_rows(s)
    along_x = above + below - 2.0 * s
    along_y = right(s) + left(s) - 2.0 * s
    diff = above - below
    mixed = 0.25 * (right(diff) - left(diff))
    return along_x, along_y, mixed


def adjoint_of(r0, r1, r2):
    cross = 0.25 * (right(r2) - left(r2))
    return (
        up_rows(r0 + cross)
        + down_rows(r0 - cross)
        - 2.0 * r0
        + right(r1)
        + left(r1)
        - 2.0 * r1
    )


def adjoint_square(s):
    def row(k):
        return pltpu.roll(s, -k % FULL, 0)[8 : 8 + PART]

    def column(v, k):
        return pltpu.roll(v, -k % v.shape[1], 1)

    centre = s[8 : 8 + PART]
    near, far = row(1) + row(-1), row(2) + row(-2)
    mixed = 0.0625 * (far - 2.0 * centre)
    both = centre + mixed
    return (
        (far - 4.0 * near + 12.0 * centre - 2.0 * mixed)
        + (column(both, 2) + column(both, -2))
        - 4.0 * (column(centre, 1) + column(centre, -1))
    )


def edge_columns(first, last, side=None):
    lane = iota(first.shape, 1)
    inside = jnp.where(lane < 64, pltpu.roll(first, 32, 1), last)
    if side is None:
        return jnp.where(lane < 32, jnp.zeros_like(first), inside)
    outside = jnp.where(lane < 16, side, pltpu.roll(side, 32, 1))
    return jnp.where(lane < 32, outside, inside)


def edges_of(v):
    width = v.shape[1]
    return edge_columns(v[:, :128], v[:, width - 256 : width - 128], v[:, width - 128 :])


def add_edges(field, message):
    width = field.shape[1]
    lane = iota(message.shape, 1)
    turned = pltpu.roll(message, 96, 1)
    zero = jnp.zeros_like(message)
    first = field[:, :128] + jnp.where(lane < NEAR, message, zero)
    last = field[:, width - 256 : width - 128] + jnp.where(lane >= 128 - NEAR, turned, zero)
    side = field[:, width - 128 :] + jnp.where(
        lane < HALO, turned, jnp.where(lane >= 128 - HALO, message, zero)
    )
    return jnp.concatenate([first, field[:, 128 : width - 256], last, side], axis=1)


def kernel_rows(k_ref, taps_ref):
    layers, span, _ = k_ref.shape
    taps_ref[...] = jnp.zeros(taps_ref.shape, f32)
    for l in range(layers):
        taps_ref[16 * l : 16 * l + span, :span] = k_ref[l].astype(f32)
    shape = (taps_ref.shape[0], WIDE)
    source = iota(shape, 0)
    place = jnp.where(32 * (source >> 4) + (source & 15) == iota(shape, 1), 1.0, 0.0)
    return lax.dot_general(
        taps_ref[...].astype(bf16),
        place.astype(bf16),
        (((0,), (0,)), ((), ())),
        preferred_element_type=f32,
    )


def build_bands(base_ref, bands_ref, span):
    tap = (iota((8, 128), 1) & 31) - iota((8, 128), 0) + 15
    keep = [(tap - 8 * g >= 0) & (tap - 8 * g < span) for g in range(PART // 8)]
    for block in range(WIDE // 128):
        for j in range(span):
            row = jnp.broadcast_to(
                base_ref[j : j + 1, 128 * block : 128 * block + 128], (8, 128)
            )
            moved = [
                jnp.where(
                    keep[g],
                    pltpu.roll(row, (8 * g - 15) % 128, 1, stride=1, stride_axis=0),
                    0.0,
                )
                for g in range(PART // 8)
            ]
            bands_ref[
                j * PART : (j + 1) * PART, 128 * block : 128 * block + 128
            ] = jnp.concatenate(moved, axis=0).astype(bf16)


def edge_message(bands, rounded, prod_ref, span, radius):
    prod_ref[...] = jnp.dot(bands, rounded, preferred_element_type=f32)
    total = prod_ref[radius * PART : (radius + 1) * PART, :]
    for j in range(span):
        if j != radius:
            piece = prod_ref[j * PART : (j + 1) * PART, :]
            total = total + pltpu.roll(piece, (radius - j) % 128, 1)
    return total


def scatter_surface(bands, rounded, prod_ref, span, radius):
    width = rounded.shape[1]
    prod_ref[...] = jnp.dot(bands, rounded, preferred_element_type=f32)
    total = prod_ref[radius * PART : (radius + 1) * PART, :]
    for j in range(span):
        if j != radius:
            piece = prod_ref[j * PART : (j + 1) * PART, :]
            total = total + pltpu.roll(piece, (radius - j) % width, 1)
    return total


def fold_side(side, reach):
    lane = iota((8, 128), 1)
    used = (lane < reach) | (lane >= 128 - reach)
    count = 128 // (2 * reach)
    blocks = []
    for first in range(0, PART // 8, count):
        folded = jnp.zeros((8, 128), f32)
        for n, g in enumerate(range(first, min(first + count, PART // 8))):
            piece = jnp.where(used, side[8 * g : 8 * g + 8], 0.0)
            folded = folded + pltpu.roll(piece, reach + 2 * reach * n, 1)
        blocks.append(folded)
    return blocks


def unfold_side(blocks, reach):
    lane = iota((8, 128), 1)
    used = (lane < reach) | (lane >= 128 - reach)
    count = 128 // (2 * reach)
    pieces = []
    for g in range(PART // 8):
        piece = pltpu.roll(blocks[g // count], 128 - reach - 2 * reach * (g % count), 1)
        pieces.append(jnp.where(used, piece, 0.0))
    return jnp.concatenate(pieces, axis=0)


def depth_message_rows(cells_y, reach):
    blocks = -(-(PART // 8) // (128 // (2 * reach)))
    return PART * (cells_y // 128) + 8 * (blocks - 1)


def fold_places(cells_y):
    blocks = cells_y // 128
    return [PART * (n % blocks) + (PART - 1) * (n // blocks) for n in range(8)]


def store_depth_message(out_ref, part, cells_y, reach):
    for start in range(0, cells_y, 128):
        row = PART * (start // 128)
        out_ref[row : row + PART, :] = part[:, start : start + 128]
    folded, *others = fold_side(part[:, cells_y:], reach)
    for n, row in enumerate(fold_places(cells_y)):
        out_ref[row : row + 1, :] = folded[n : n + 1]
    for n, block in enumerate(others):
        row = PART * (cells_y // 128) + 8 * n
        out_ref[row : row + 8, :] = block


def first_kernel(
    labels_hbm, background_hbm, contrasts_hbm, k_hbm, observed_hbm,
    edge_ref, density_ref, bands_ref, observed_ref,
    labels_ref, background_ref, contrasts_ref, k_ref, sems,
    taps_ref, base_ref, prod_ref,
):
    layers, cells_x, cells_y = labels_ref.shape
    span = k_ref.shape[1]
    copies = [
        pltpu.make_async_copy(source, target, sems.at[n])
        for n, (source, target) in enumerate(
            (
                (k_hbm, k_ref),
                (contrasts_hbm, contrasts_ref),
                (labels_hbm, labels_ref),
                (background_hbm, background_ref),
                (observed_hbm, observed_ref),
            )
        )
    ]
    for copy in copies:
        copy.start()
    copies[0].wait()
    base_ref[...] = kernel_rows(k_ref, taps_ref)
    build_bands(base_ref, bands_ref, span)
    for copy in copies[1:]:
        copy.wait()
    classes = contrasts_ref.shape[0]
    for l in range(layers):
        label = labels_ref[l]
        value = jnp.full(label.shape, contrasts_ref[0], f32)
        for c in range(1, classes):
            value = jnp.where(label == c, contrasts_ref[c], value)
        density = value + background_ref[l].astype(f32)
        rows = slice(l * cells_x, (l + 1) * cells_x)
        density_ref[rows, :] = density
        edge_ref[2 * PART + l * cells_x : 2 * PART + (l + 1) * cells_x, :] = edge_columns(
            density[:, :128], density[:, cells_y - 128 :]
        )
    edge_ref[:PART, :] = edge_message(
        bands_ref[:, : layers * cells_x],
        edge_ref[2 * PART :, :].astype(bf16),
        prod_ref,
        span,
        (span - 1) // 2,
    )
    empty = jnp.zeros((8, 128), f32)
    edge_ref[PART : 2 * PART, :] = adjoint_of(
        *(
            jnp.concatenate(
                [
                    empty,
                    edge_columns(observed_ref[k, :, :128], observed_ref[k, :, cells_y - 128 :]),
                    empty,
                ],
                axis=0,
            )
            for k in range(3)
        )
    )


def first_field_kernel(
    density_ref, bands_ref, observed_ref, part_ref, q_ref, prod_ref, obs_ref, *, span
):
    lanes, cells_y = density_ref.shape
    radius = (span - 1) // 2
    width = cells_y + 128
    prod_ref[...] = jnp.dot(
        bands_ref[:, :lanes], density_ref[...].astype(bf16), preferred_element_type=f32
    )
    total = jnp.zeros((PART, width), f32)
    side = jnp.zeros((PART, 128), f32)
    for j in range(span):
        piece = jnp.concatenate([prod_ref[j * PART : (j + 1) * PART, :], side], axis=1)
        shift = (radius - j) % width
        total = total + (pltpu.roll(piece, shift, 1) if shift else piece)
    part_ref[...] = total
    obs_ref[...] = jnp.zeros(obs_ref.shape, f32)
    for k in range(3):
        obs_ref[k, 8 : PART - 8, :cells_y] = observed_ref[k]
    q_ref[...] = adjoint_of(obs_ref[0], obs_ref[1], obs_ref[2])


def transpose_kernel(bands_ref, out_ref):
    out_ref[...] = bands_ref[...].astype(f32).T.astype(bf16)


def edges_kernel(part_ref, edge_ref, out_ref, *, cells_y):
    part = add_edges(part_ref[...], edge_ref[:PART, :])
    store_depth_message(out_ref, part, cells_y, HALO)


def send_rows(sum_ref, up_ref, down_ref):
    sub = iota((8, sum_ref.shape[1]), 0)
    up_ref[:8, :] = sum_ref[8:16, :]
    up_ref[8:16, :] = jnp.where(sub >= 1, sum_ref[:8, :], sum_ref[16:24, :])
    down_ref[:8, :] = sum_ref[32:40, :]
    down_ref[8:16, :] = jnp.where(sub < 7, sum_ref[40:48, :], sum_ref[24:32, :])


def rows_kernel(
    part_ref, other_ref, q_ref, edge_ref, sum_ref, up_ref, down_ref, q_out_ref,
    dense_ref, fold_ref, *, reach,
):
    cells_y = sum_ref.shape[1] - 128
    dense_ref[...] = part_ref[...] + other_ref[...]
    zero = jnp.zeros((1, 128), f32)
    for n, row in enumerate(fold_places(cells_y)):
        fold_ref[n : n + 1, :] = dense_ref[row : row + 1, :]
    folded = [fold_ref[...]]
    for row in range(PART * (cells_y // 128), dense_ref.shape[0], 8):
        folded.append(dense_ref[row : row + 8, :])
    for row in fold_places(cells_y):
        dense_ref[row : row + 1, :] = zero
    for start in range(0, cells_y, 128):
        row = PART * (start // 128)
        sum_ref[:, start : start + 128] = dense_ref[row : row + PART, :]
    sum_ref[:, cells_y:] = unfold_side(folded, reach)
    sub = iota((8, sum_ref.shape[1]), 0)
    up_ref[:8, :] = sum_ref[8:16, :]
    up_ref[8:16, :] = jnp.where(sub >= 1, sum_ref[:8, :], sum_ref[16:24, :])
    down_ref[:8, :] = sum_ref[32:40, :]
    down_ref[8:16, :] = jnp.where(sub < 7, sum_ref[40:48, :], sum_ref[24:32, :])
    if q_ref is not None:
        q_out_ref[...] = add_edges(q_ref[...], edge_ref[PART : 2 * PART, :])
        up_ref[16:24, :] = jnp.where(sub < 7, q_out_ref[8:16, :], q_out_ref[:8, :])
        down_ref[16:24, :] = jnp.where(sub >= 1, q_out_ref[32:40, :], q_out_ref[40:48, :])


def full_surface(total, above, below):
    shape = (8, total.shape[1])
    sub = iota(shape, 0)
    zero = jnp.zeros(shape, f32)
    return jnp.concatenate(
        [
            jnp.where(sub == 7, above[8:16], zero),
            total[:8] + above[:8],
            total[8:16] + jnp.where(sub < 7, above[8:16], zero),
            total[16:32],
            total[32:40] + jnp.where(sub >= 1, below[8:16], zero),
            total[40:48] + below[:8],
            jnp.where(sub == 0, below[8:16], zero),
        ],
        axis=0,
    )


def full_q(q, above, below):
    shape = (8, q.shape[1])
    sub = iota(shape, 0)
    zero = jnp.zeros(shape, f32)
    return jnp.concatenate(
        [
            q[:8] + jnp.where(sub >= 1, above[16:24], zero),
            q[8:16] + jnp.where(sub == 0, above[16:24], zero),
            q[16:32],
            q[32:40] + jnp.where(sub == 7, below[16:24], zero),
            q[40:48] + jnp.where(sub < 7, below[16:24], zero),
        ],
        axis=0,
    )


def stack_shifts(adjoint, stack_ref, columns, span, radius):
    for j in range(span):
        shift = (j - radius) % adjoint.shape[1]
        moved = pltpu.roll(adjoint, shift, 1) if shift else adjoint
        stack_ref[j * PART : (j + 1) * PART, columns] = moved[:, columns]


def rounded_adjoint(s, q):
    return (adjoint_square(s) - q).astype(bf16)


def middle_kernel(
    sum_ref, above_ref, below_ref, q_ref, density_ref, edge_ref, bands_ref, turned_ref,
    out_ref, q_out_ref,
    stack_ref, prod_ref, *, span,
):
    radius = (span - 1) // 2
    lanes, cells_y = density_ref.shape
    above, below = above_ref[...], below_ref[...]
    q = full_q(q_ref[...], above, below)
    q_out_ref[...] = q
    adjoint = rounded_adjoint(full_surface(sum_ref[...], above, below), q)
    stack_shifts(adjoint, stack_ref, slice(0, cells_y + 128), span, radius)
    gradient = jnp.dot(turned_ref[:lanes, :], stack_ref[...], preferred_element_type=f32)
    density = density_ref[...] - descent * gradient[:, :cells_y]
    message = edge_ref[2 * PART :, :]
    lane = iota(message.shape, 1)
    outside = jnp.where(lane < 16, pltpu.roll(message, 96, 1), message)
    outside = outside - descent * gradient[:, cells_y:]
    outside = jnp.where((lane < 16) | (lane >= 112), outside, 0.0)
    rounded = jnp.concatenate([density.astype(bf16), outside.astype(bf16)], axis=1)
    part = scatter_surface(bands_ref[:, :lanes], rounded, prod_ref, span, radius)
    store_depth_message(out_ref, part, cells_y, NEAR)


def last_kernel(
    start_ref, sum_ref, above_ref, below_ref, q_ref, turned_ref, observed_ref,
    residual_hbm, gradient_hbm,
    residual_ref, gradient_ref, sems, full_ref, stack_ref, misfit_ref, *, span,
):
    radius = (span - 1) // 2
    layers, cells_x, cells_y = gradient_ref.shape
    s = full_surface(sum_ref[...], above_ref[...], below_ref[...])
    full_ref[...] = s
    adjoint = rounded_adjoint(s, q_ref[...])
    turned = turned_ref[: layers * cells_x, :]
    half = cells_y // 2
    copies = []
    for n in range(2):
        columns = slice(n * half, (n + 1) * half)
        stack_shifts(adjoint, stack_ref, columns, span, radius)
        gradient = jnp.dot(turned, stack_ref[:, columns], preferred_element_type=f32)
        for l in range(layers):
            gradient_ref[l, :, columns] = gradient[l * cells_x : (l + 1) * cells_x, :]
        copies.append(
            pltpu.make_async_copy(
                gradient_ref.at[:, :, columns], gradient_hbm.at[:, :, columns], sems.at[n]
            )
        )
        copies[-1].start()
    share = residual_ref.shape[1]
    if share % 8 == 0:
        start = pl.multiple_of(start_ref[0], 8)
        fields = tensor_fields(full_ref[pl.ds(start + 8, share + 16), :])
        for k in range(3):
            residual_ref[k] = (
                fields[k][8 : 8 + share, :cells_y] - observed_ref[k, pl.ds(start, share), :]
            )
    else:
        fields = tensor_fields(full_ref[...])
        for k in range(3):
            misfit_ref[k] = fields[k][16 : 16 + cells_x, :cells_y] - observed_ref[k]
        for start in range(0, cells_x, share):

            @pl.when(start_ref[0] == start)
            def _():
                residual_ref[...] = misfit_ref[:, start : start + share, :]

    copies.append(pltpu.make_async_copy(residual_ref, residual_hbm, sems.at[2]))
    copies[-1].start()
    for copy in copies:
        copy.wait()


def call(
    kernel, outs, scratch=(), inputs=pltpu.VMEM, smem=(), results=pltpu.VMEM, aliases={}
):
    made = pl.BlockSpec(memory_space=results)
    given = pl.BlockSpec(memory_space=inputs)
    scalar = pl.BlockSpec(memory_space=pltpu.SMEM)

    def run(*operands):
        if inputs is pltpu.HBM:
            operands = [pltpu.with_memory_space_constraint(v, pltpu.HBM) for v in operands]
        return pl.pallas_call(
            kernel,
            out_shape=outs,
            in_specs=[scalar if i in smem else given for i in range(len(operands))],
            out_specs=jax.tree.map(lambda _: made, outs),
            scratch_shapes=[
                item if not isinstance(item, tuple) else pltpu.VMEM(*item) for item in scratch
            ],
            compiler_params=pltpu.CompilerParams(vmem_limit_bytes=GRANT),
            input_output_aliases=aliases,
        )(*operands)

    return run


def shaped(shape, kind=f32):
    return jax.ShapeDtypeStruct(shape, kind)


def swap(value, axis, distance):
    peers = lax.axis_size(axis)
    return lax.ppermute(value, axis, [(i, i ^ distance) for i in range(peers)])


def body(labels, background, contrasts, kernels, observed):
    layers, cells_x, cells_y = labels.shape
    span = kernels.shape[1]
    lanes = layers * cells_x
    width = cells_y + 128
    depth_peers, row_peers = lax.axis_size("gz"), lax.axis_size("gx")
    assert cells_x == 32 and span == 15 and lanes <= 192 and cells_y == 512 and lax.axis_size("gy") == 2
    assert depth_peers & (depth_peers - 1) == 0
    share = cells_x // depth_peers
    upward = [(i, (i - 1) % row_peers) for i in range(row_peers)]
    downward = [(j, i) for i, j in upward]
    full = ((FULL, width), f32)
    prod = ((span * PART, cells_y), f32)
    stack = ((span * PART, cells_y), bf16)
    edge_prod = ((span * PART, 128), f32)
    edge_stack = ((span * PART, 128), bf16)
    field = shaped((PART, width))

    def kernel_of(body_of):
        return functools.partial(body_of, span=span)

    edge, density, bands, observed = call(
        first_kernel,
        (
            shaped((2 * PART + lanes, 128)),
            shaped((lanes, cells_y)),
            shaped((span * PART, WIDE), bf16),
            shaped(observed.shape),
        ),
        (
            (labels.shape, labels.dtype),
            (background.shape, background.dtype),
            pltpu.SMEM(contrasts.shape, contrasts.dtype),
            (kernels.shape, kernels.dtype),
            pltpu.SemaphoreType.DMA((5,)),
            ((16 * layers, 16), f32),
            ((16, WIDE), f32),
            edge_prod,
        ),
        inputs=pltpu.HBM,
    )(labels, background, contrasts, kernels, observed)
    part, q = call(
        kernel_of(first_field_kernel), (field, field), (prod, ((3, PART, width), f32))
    )(density, bands, observed)
    start = (lax.axis_index("gz") * share).astype(jnp.int32).reshape(1)
    turned = call(transpose_kernel, shaped((WIDE, span * PART), bf16))(bands)

    others = swap(edge, "gy", 1)
    part = call(
        functools.partial(edges_kernel, cells_y=cells_y),
        shaped((depth_message_rows(cells_y, HALO), 128)),
    )(part, others)
    for iteration in range(ITERS):
        for bit in range(depth_peers.bit_length() - 2):
            part = part + swap(part, "gz", 2 << bit)
        other = swap(part, "gz", 1)
        scratch = ((part.shape, f32), ((8, 128), f32))
        if iteration == 0:
            total, up, down, q = call(
                functools.partial(rows_kernel, reach=HALO),
                (field, shaped((24, width)), shaped((24, width)), field),
                scratch,
            )(part, other, q, others)
        else:
            total, up, down = call(
                lambda a, b, c, d, e, f, g: rows_kernel(
                    a, b, None, None, c, d, e, None, f, g, reach=NEAR
                ),
                (field, shaped((16, width)), shaped((16, width))),
                scratch,
            )(part, other)
        below = lax.ppermute(up, "gx", upward)
        above = lax.ppermute(down, "gx", downward)
        if iteration == 0:
            part, q = call(
                kernel_of(middle_kernel),
                (shaped((depth_message_rows(cells_y, NEAR), 128)), field),
                (((span * PART, width), bf16), ((span * PART, width), f32)),
            )(total, above, below, q, density, others, bands, turned)
    return call(
        kernel_of(last_kernel),
        (shaped((3, share, cells_y)), shaped((layers, cells_x, cells_y))),
        (
            ((3, share, cells_y), f32),
            ((layers, cells_x, cells_y), f32),
            pltpu.SemaphoreType.DMA((3,)),
            full,
            ((span * PART, cells_y), bf16),
            ((3, cells_x, cells_y), f32),
        ),
        smem=(0,),
        results=pltpu.HBM,
    )(start, total, above, below, q, turned, observed)


def solution(mesh):
    placed = (
        P(("runs", "gz"), "gx", "gy"),
        P(("runs", "gz"), "gx", "gy"),
        P("runs"),
        P(("runs", "gz"), None, None),
        P("runs", "gx", "gy"),
    )
    return jax.shard_map(
        body,
        mesh=mesh,
        in_specs=placed,
        out_specs=(P("runs", ("gx", "gz"), "gy"), P(("runs", "gz"), "gx", "gy")),
        check_vma=False,
    )
```

```python
import functools

import jax
import jax.numpy as jnp
from jax import lax
from jax.experimental import pallas as pl
from jax.experimental.pallas import tpu as pltpu
from jax.sharding import PartitionSpec as P


descent = 0.01
ITERS = 2
PART = 48
NEAR, HALO = 9, 25
FULL = 64
WIDE = 256
GRANT = 16 * 2**20

f32 = jnp.float32
bf16 = jnp.bfloat16


def iota(shape, dim):
    return lax.broadcasted_iota(jnp.int32, shape, dim)


def up_rows(v):
    return pltpu.roll(v, v.shape[0] - 1, 0)


def down_rows(v):
    return pltpu.roll(v, 1, 0)


def right(v):
    return pltpu.roll(v, v.shape[1] - 1, 1)


def left(v):
    return pltpu.roll(v, 1, 1)


def tensor_fields(s):
    above, below = up_rows(s), down_rows(s)
    along_x = above + below - 2.0 * s
    along_y = right(s) + left(s) - 2.0 * s
    diff = above - below
    mixed = 0.25 * (right(diff) - left(diff))
    return along_x, along_y, mixed


def adjoint_of(r0, r1, r2):
    cross = 0.25 * (right(r2) - left(r2))
    return (
        up_rows(r0 + cross)
        + down_rows(r0 - cross)
        - 2.0 * r0
        + right(r1)
        + left(r1)
        - 2.0 * r1
    )


def adjoint_square(s):
    def row(k):
        return pltpu.roll(s, -k % FULL, 0)[8 : 8 + PART]

    def column(v, k):
        return pltpu.roll(v, -k % v.shape[1], 1)

    centre = s[8 : 8 + PART]
    near, far = row(1) + row(-1), row(2) + row(-2)
    mixed = 0.0625 * (far - 2.0 * centre)
    both = centre + mixed
    return (
        (far - 4.0 * near + 12.0 * centre - 2.0 * mixed)
        + (column(both, 2) + column(both, -2))
        - 4.0 * (column(centre, 1) + column(centre, -1))
    )


def edge_columns(first, last, side=None):
    lane = iota(first.shape, 1)
    inside = jnp.where(lane < 64, pltpu.roll(first, 32, 1), last)
    if side is None:
        return jnp.where(lane < 32, jnp.zeros_like(first), inside)
    outside = jnp.where(lane < 16, side, pltpu.roll(side, 32, 1))
    return jnp.where(lane < 32, outside, inside)


def edges_of(v):
    width = v.shape[1]
    return edge_columns(v[:, :128], v[:, width - 256 : width - 128], v[:, width - 128 :])


def add_edges(field, message):
    width = field.shape[1]
    lane = iota(message.shape, 1)
    turned = pltpu.roll(message, 96, 1)
    zero = jnp.zeros_like(message)
    first = field[:, :128] + jnp.where(lane < NEAR, message, zero)
    last = field[:, width - 256 : width - 128] + jnp.where(lane >= 128 - NEAR, turned, zero)
    side = field[:, width - 128 :] + jnp.where(
        lane < HALO, turned, jnp.where(lane >= 128 - HALO, message, zero)
    )
    return jnp.concatenate([first, field[:, 128 : width - 256], last, side], axis=1)


def kernel_rows(k_ref, taps_ref):
    layers, span, _ = k_ref.shape
    taps_ref[...] = jnp.zeros(taps_ref.shape, f32)
    for l in range(layers):
        taps_ref[16 * l : 16 * l + span, :span] = k_ref[l].astype(f32)
    shape = (taps_ref.shape[0], WIDE)
    source = iota(shape, 0)
    place = jnp.where(32 * (source >> 4) + (source & 15) == iota(shape, 1), 1.0, 0.0)
    return lax.dot_general(
        taps_ref[...].astype(bf16),
        place.astype(bf16),
        (((0,), (0,)), ((), ())),
        preferred_element_type=f32,
    )


def build_bands(base_ref, bands_ref, span):
    tap = (iota((8, 128), 1) & 31) - iota((8, 128), 0) + 15
    keep = [(tap - 8 * g >= 0) & (tap - 8 * g < span) for g in range(PART // 8)]
    for block in range(WIDE // 128):
        for j in range(span):
            row = jnp.broadcast_to(
                base_ref[j : j + 1, 128 * block : 128 * block + 128], (8, 128)
            )
            moved = [
                jnp.where(
                    keep[g],
                    pltpu.roll(row, (8 * g - 15) % 128, 1, stride=1, stride_axis=0),
                    0.0,
                )
                for g in range(PART // 8)
            ]
            bands_ref[
                j * PART : (j + 1) * PART, 128 * block : 128 * block + 128
            ] = jnp.concatenate(moved, axis=0).astype(bf16)


def scatter_surface(bands, rounded, prod_ref, span, radius):
    width = rounded.shape[1]
    prod_ref[...] = jnp.dot(bands, rounded, preferred_element_type=f32)
    total = prod_ref[radius * PART : (radius + 1) * PART, :]
    for j in range(span):
        if j != radius:
            piece = prod_ref[j * PART : (j + 1) * PART, :]
            total = total + pltpu.roll(piece, (radius - j) % width, 1)
    return total


def fold_side(side, reach):
    lane = iota((8, 128), 1)
    used = (lane < reach) | (lane >= 128 - reach)
    count = 128 // (2 * reach)
    blocks = []
    for first in range(0, PART // 8, count):
        folded = jnp.zeros((8, 128), f32)
        for n, g in enumerate(range(first, min(first + count, PART // 8))):
            piece = jnp.where(used, side[8 * g : 8 * g + 8], 0.0)
            folded = folded + pltpu.roll(piece, reach + 2 * reach * n, 1)
        blocks.append(folded)
    return blocks


def unfold_side(blocks, reach):
    lane = iota((8, 128), 1)
    used = (lane < reach) | (lane >= 128 - reach)
    count = 128 // (2 * reach)
    pieces = []
    for g in range(PART // 8):
        piece = pltpu.roll(blocks[g // count], 128 - reach - 2 * reach * (g % count), 1)
        pieces.append(jnp.where(used, piece, 0.0))
    return jnp.concatenate(pieces, axis=0)


def depth_message_rows(cells_y, reach):
    blocks = -(-(PART // 8) // (128 // (2 * reach)))
    return PART * (cells_y // 128) + 8 * (blocks - 1)


def fold_places(cells_y):
    blocks = cells_y // 128
    return [PART * (n % blocks) + (PART - 1) * (n // blocks) for n in range(8)]


def store_depth_message(out_ref, part, cells_y, reach):
    for start in range(0, cells_y, 128):
        row = PART * (start // 128)
        out_ref[row : row + PART, :] = part[:, start : start + 128]
    folded, *others = fold_side(part[:, cells_y:], reach)
    for n, row in enumerate(fold_places(cells_y)):
        out_ref[row : row + 1, :] = folded[n : n + 1]
    for n, block in enumerate(others):
        row = PART * (cells_y // 128) + 8 * n
        out_ref[row : row + 8, :] = block


def first_kernel(
    labels_hbm, background_hbm, contrasts_hbm, k_hbm,
    out_ref, edge_ref, density_edge_ref, density_ref, bands_ref,
    labels_ref, background_ref, contrasts_ref, k_ref, sems,
    taps_ref, base_ref, prod_ref,
):
    layers, cells_x, cells_y = labels_ref.shape
    span = k_ref.shape[1]
    copies = [
        pltpu.make_async_copy(source, target, sems.at[n])
        for n, (source, target) in enumerate(
            (
                (k_hbm, k_ref),
                (contrasts_hbm, contrasts_ref),
                (labels_hbm, labels_ref),
                (background_hbm, background_ref),
            )
        )
    ]
    for copy in copies:
        copy.start()
    copies[0].wait()
    base_ref[...] = kernel_rows(k_ref, taps_ref)
    build_bands(base_ref, bands_ref, span)
    for copy in copies[1:]:
        copy.wait()
    classes = contrasts_ref.shape[0]
    for l in range(layers):
        label = labels_ref[l]
        value = jnp.full(label.shape, contrasts_ref[0], f32)
        for c in range(1, classes):
            value = jnp.where(label == c, contrasts_ref[c], value)
        density = value + background_ref[l].astype(f32)
        rows = slice(l * cells_x, (l + 1) * cells_x)
        density_ref[rows, :] = density
        density_edge_ref[rows, :] = edge_columns(
            density[:, :128], density[:, cells_y - 128 :]
        )
    lanes = layers * cells_x
    radius = (span - 1) // 2
    width = cells_y + 128
    prod_ref[...] = jnp.dot(
        bands_ref[:, :lanes], density_ref[...].astype(bf16), preferred_element_type=f32
    )
    part = jnp.zeros((PART, width), f32)
    side = jnp.zeros((PART, 128), f32)
    for j in range(span):
        piece = jnp.concatenate([prod_ref[j * PART : (j + 1) * PART, :], side], axis=1)
        shift = (radius - j) % width
        part = part + (pltpu.roll(piece, shift, 1) if shift else piece)
    edge_ref[...] = edges_of(part)
    store_depth_message(out_ref, part, cells_y, NEAR)


def observed_kernel(
    density_edge_ref, observed_hbm, q_ref, edge_ref, observed_ref, obs_ref, sem
):
    cells_y = observed_ref.shape[2]
    copy = pltpu.make_async_copy(observed_hbm, observed_ref, sem)
    copy.start()
    edge_ref[PART:, :] = density_edge_ref[...]
    obs_ref[...] = jnp.zeros(obs_ref.shape, f32)
    copy.wait()
    for k in range(3):
        obs_ref[k, 8 : PART - 8, :cells_y] = observed_ref[k]
    q = adjoint_of(obs_ref[0], obs_ref[1], obs_ref[2])
    q_ref[...] = q
    edge_ref[:PART, :] = edges_of(q)


def transpose_kernel(bands_ref, out_ref):
    out_ref[...] = bands_ref[...].astype(f32).T.astype(bf16)


def rows_kernel(
    part_ref, other_ref, edge_ref, edge_other_ref, q_ref, q_edge_ref,
    sum_ref, up_ref, down_ref, q_out_ref,
    dense_ref, fold_ref,
):
    cells_y = sum_ref.shape[1] - 128
    dense_ref[...] = part_ref[...] + other_ref[...]
    zero = jnp.zeros((1, 128), f32)
    for n, row in enumerate(fold_places(cells_y)):
        fold_ref[n : n + 1, :] = dense_ref[row : row + 1, :]
    folded = [fold_ref[...]]
    for row in range(PART * (cells_y // 128), dense_ref.shape[0], 8):
        folded.append(dense_ref[row : row + 8, :])
    for row in fold_places(cells_y):
        dense_ref[row : row + 1, :] = zero
    for start in range(0, cells_y, 128):
        row = PART * (start // 128)
        sum_ref[:, start : start + 128] = dense_ref[row : row + PART, :]
    sum_ref[:, cells_y:] = unfold_side(folded, NEAR)
    if edge_ref is not None:
        sum_ref[...] = add_edges(sum_ref[...], edge_ref[...] + edge_other_ref[...])
    sub = iota((8, sum_ref.shape[1]), 0)
    up_ref[:8, :] = sum_ref[8:16, :]
    up_ref[8:16, :] = jnp.where(sub >= 1, sum_ref[:8, :], sum_ref[16:24, :])
    down_ref[:8, :] = sum_ref[32:40, :]
    down_ref[8:16, :] = jnp.where(sub < 7, sum_ref[40:48, :], sum_ref[24:32, :])
    if q_ref is not None:
        q_out_ref[...] = add_edges(q_ref[...], q_edge_ref[:PART, :])
        up_ref[16:24, :] = jnp.where(sub < 7, q_out_ref[8:16, :], q_out_ref[:8, :])
        down_ref[16:24, :] = jnp.where(sub >= 1, q_out_ref[32:40, :], q_out_ref[40:48, :])


def full_surface(total, above, below):
    shape = (8, total.shape[1])
    sub = iota(shape, 0)
    zero = jnp.zeros(shape, f32)
    return jnp.concatenate(
        [
            jnp.where(sub == 7, above[8:16], zero),
            total[:8] + above[:8],
            total[8:16] + jnp.where(sub < 7, above[8:16], zero),
            total[16:32],
            total[32:40] + jnp.where(sub >= 1, below[8:16], zero),
            total[40:48] + below[:8],
            jnp.where(sub == 0, below[8:16], zero),
        ],
        axis=0,
    )


def full_q(q, above, below):
    shape = (8, q.shape[1])
    sub = iota(shape, 0)
    zero = jnp.zeros(shape, f32)
    return jnp.concatenate(
        [
            q[:8] + jnp.where(sub >= 1, above[16:24], zero),
            q[8:16] + jnp.where(sub == 0, above[16:24], zero),
            q[16:32],
            q[32:40] + jnp.where(sub == 7, below[16:24], zero),
            q[40:48] + jnp.where(sub < 7, below[16:24], zero),
        ],
        axis=0,
    )


def stack_shifts(adjoint, stack_ref, columns, span, radius):
    for j in range(span):
        shift = (j - radius) % adjoint.shape[1]
        moved = pltpu.roll(adjoint, shift, 1) if shift else adjoint
        stack_ref[j * PART : (j + 1) * PART, columns] = moved[:, columns]


def rounded_adjoint(s, q):
    return (adjoint_square(s) - q).astype(bf16)


def middle_kernel(
    sum_ref, above_ref, below_ref, q_ref, density_ref, edge_ref, bands_ref, turned_ref,
    out_ref, q_out_ref,
    stack_ref, prod_ref, *, span,
):
    radius = (span - 1) // 2
    lanes, cells_y = density_ref.shape
    above, below = above_ref[...], below_ref[...]
    q = full_q(q_ref[...], above, below)
    q_out_ref[...] = q
    adjoint = rounded_adjoint(full_surface(sum_ref[...], above, below), q)
    stack_shifts(adjoint, stack_ref, slice(0, cells_y + 128), span, radius)
    gradient = jnp.dot(turned_ref[:lanes, :], stack_ref[...], preferred_element_type=f32)
    density = density_ref[...] - descent * gradient[:, :cells_y]
    message = edge_ref[PART:, :]
    lane = iota(message.shape, 1)
    outside = jnp.where(lane < 16, pltpu.roll(message, 96, 1), message)
    outside = outside - descent * gradient[:, cells_y:]
    outside = jnp.where((lane < 16) | (lane >= 112), outside, 0.0)
    rounded = jnp.concatenate([density.astype(bf16), outside.astype(bf16)], axis=1)
    part = scatter_surface(bands_ref[:, :lanes], rounded, prod_ref, span, radius)
    store_depth_message(out_ref, part, cells_y, NEAR)


def last_kernel(
    sum_ref, above_ref, below_ref, q_ref, turned_ref, observed_ref,
    residual_hbm, gradient_hbm,
    residual_ref, gradient_ref, sems, full_ref, stack_ref, misfit_ref, *, span,
):
    radius = (span - 1) // 2
    layers, cells_x, cells_y = gradient_ref.shape
    s = full_surface(sum_ref[...], above_ref[...], below_ref[...])
    full_ref[...] = s
    adjoint = rounded_adjoint(s, q_ref[...])
    turned = turned_ref[: layers * cells_x, :]
    half = cells_y // 2
    copies = []
    for n in range(2):
        columns = slice(n * half, (n + 1) * half)
        stack_shifts(adjoint, stack_ref, columns, span, radius)
        gradient = jnp.dot(turned, stack_ref[:, columns], preferred_element_type=f32)
        for l in range(layers):
            gradient_ref[l, :, columns] = gradient[l * cells_x : (l + 1) * cells_x, :]
        copies.append(
            pltpu.make_async_copy(
                gradient_ref.at[:, :, columns], gradient_hbm.at[:, :, columns], sems.at[n]
            )
        )
        copies[-1].start()
    share = residual_ref.shape[1]
    if share % 8 == 0:
        start = pl.multiple_of(lax.axis_index("gz") * share, 8)
        fields = tensor_fields(full_ref[pl.ds(start + 8, share + 16), :])
        for k in range(3):
            residual_ref[k] = (
                fields[k][8 : 8 + share, :cells_y] - observed_ref[k, pl.ds(start, share), :]
            )
    else:
        fields = tensor_fields(full_ref[...])
        for k in range(3):
            misfit_ref[k] = fields[k][16 : 16 + cells_x, :cells_y] - observed_ref[k]
        for start in range(0, cells_x, share):

            @pl.when(lax.axis_index("gz") * share == start)
            def _():
                residual_ref[...] = misfit_ref[:, start : start + share, :]

    copies.append(pltpu.make_async_copy(residual_ref, residual_hbm, sems.at[2]))
    copies[-1].start()
    for copy in copies:
        copy.wait()


def call(kernel, outs, scratch=(), inputs=None, results=pltpu.VMEM):
    made = pl.BlockSpec(memory_space=results)

    def run(*operands):
        spaces = inputs or (pltpu.VMEM,) * len(operands)
        operands = [
            pltpu.with_memory_space_constraint(v, space) if space is pltpu.HBM else v
            for v, space in zip(operands, spaces)
        ]
        return pl.pallas_call(
            kernel,
            out_shape=outs,
            in_specs=[pl.BlockSpec(memory_space=space) for space in spaces],
            out_specs=jax.tree.map(lambda _: made, outs),
            scratch_shapes=[
                pltpu.VMEM(*item) if isinstance(item, tuple) else item for item in scratch
            ],
            compiler_params=pltpu.CompilerParams(vmem_limit_bytes=GRANT),
        )(*operands)

    return run


def shaped(shape, kind=f32):
    return jax.ShapeDtypeStruct(shape, kind)


def swap(value, axis, distance):
    peers = lax.axis_size(axis)
    return lax.ppermute(value, axis, [(i, i ^ distance) for i in range(peers)])


def body(labels, background, contrasts, kernels, observed):
    layers, cells_x, cells_y = labels.shape
    span = kernels.shape[1]
    lanes = layers * cells_x
    width = cells_y + 128
    depth_peers, row_peers = lax.axis_size("gz"), lax.axis_size("gx")
    assert cells_x == 32 and span == 15 and lanes <= 192 and cells_y == 512 and lax.axis_size("gy") == 2
    assert depth_peers & (depth_peers - 1) == 0
    share = cells_x // depth_peers
    upward = [(i, (i - 1) % row_peers) for i in range(row_peers)]
    downward = [(j, i) for i, j in upward]
    full = ((FULL, width), f32)
    prod = ((span * PART, cells_y), f32)
    field = shaped((PART, width))

    def kernel_of(body_of):
        return functools.partial(body_of, span=span)

    message = shaped((depth_message_rows(cells_y, NEAR), 128))
    part, edge, density_edge, density, bands = call(
        first_kernel,
        (
            message,
            shaped((PART, 128)),
            shaped((lanes, 128)),
            shaped((lanes, cells_y)),
            shaped((span * PART, WIDE), bf16),
        ),
        (
            (labels.shape, labels.dtype),
            (background.shape, background.dtype),
            pltpu.SMEM(contrasts.shape, contrasts.dtype),
            (kernels.shape, kernels.dtype),
            pltpu.SemaphoreType.DMA((4,)),
            ((16 * layers, 16), f32),
            ((16, WIDE), f32),
            prod,
        ),
        inputs=(pltpu.HBM,) * 4,
    )(labels, background, contrasts, kernels)
    turned = call(transpose_kernel, shaped((WIDE, span * PART), bf16))(bands)

    distances = [2 << bit for bit in range(depth_peers.bit_length() - 2)] + [1]
    for iteration in range(ITERS):
        scratch = ((part.shape, f32), ((8, 128), f32))
        if iteration == 0:
            other = swap(part, "gz", distances[0])
            edge = swap(edge, "gy", 1)
            edge, density_edge = lax.optimization_barrier((edge, density_edge))
            edge_other = swap(edge, "gz", distances[0])
            q, q_edge, observed = call(
                observed_kernel,
                (field, shaped((PART + lanes, 128)), shaped(observed.shape)),
                (((3, PART, width), f32), pltpu.SemaphoreType.DMA),
                inputs=(pltpu.VMEM, pltpu.HBM),
            )(density_edge, observed)
            others = swap(q_edge, "gy", 1)
            for distance in distances[1:]:
                part, edge = part + other, edge + edge_other
                other = swap(part, "gz", distance)
                edge_other = swap(edge, "gz", distance)
        else:
            for distance in distances[:-1]:
                part = part + swap(part, "gz", distance)
            other = swap(part, "gz", 1)
        if iteration == 0:
            total, up, down, q = call(
                rows_kernel,
                (field, shaped((24, width)), shaped((24, width)), field),
                scratch,
            )(part, other, edge, edge_other, q, others)
        else:
            total, up, down = call(
                lambda a, b, c, d, e, f, g: rows_kernel(
                    a, b, None, None, None, None, c, d, e, None, f, g
                ),
                (field, shaped((16, width)), shaped((16, width))),
                scratch,
            )(part, other)
        below = lax.ppermute(up, "gx", upward)
        above = lax.ppermute(down, "gx", downward)
        if iteration == 0:
            part, q = call(
                kernel_of(middle_kernel),
                (shaped((depth_message_rows(cells_y, NEAR), 128)), field),
                (((span * PART, width), bf16), ((span * PART, width), f32)),
            )(total, above, below, q, density, others, bands, turned)
    return call(
        kernel_of(last_kernel),
        (shaped((3, share, cells_y)), shaped((layers, cells_x, cells_y))),
        (
            ((3, share, cells_y), f32),
            ((layers, cells_x, cells_y), f32),
            pltpu.SemaphoreType.DMA((3,)),
            full,
            ((span * PART, cells_y), bf16),
            ((3, cells_x, cells_y), f32),
        ),
        results=pltpu.HBM,
    )(total, above, below, q, turned, observed)


def solution(mesh):
    placed = (
        P(("runs", "gz"), "gx", "gy"),
        P(("runs", "gz"), "gx", "gy"),
        P("runs"),
        P(("runs", "gz"), None, None),
        P("runs", "gx", "gy"),
    )
    return jax.shard_map(
        body,
        mesh=mesh,
        in_specs=placed,
        out_specs=(P("runs", ("gx", "gz"), "gy"), P(("runs", "gz"), "gx", "gy")),
        check_vma=False,
    )
```

```python
import functools

import jax
import jax.numpy as jnp
from jax import lax
from jax.experimental import pallas as pl
from jax.experimental.pallas import tpu as pltpu
from jax.sharding import PartitionSpec as P


descent = 0.01
ITERS = 2
PART = 48
NEAR, HALO = 9, 25
FULL = 64
WIDE = 256
GRANT = 16 * 2**20

f32 = jnp.float32
bf16 = jnp.bfloat16


def iota(shape, dim):
    return lax.broadcasted_iota(jnp.int32, shape, dim)


def up_rows(v):
    return pltpu.roll(v, v.shape[0] - 1, 0)


def down_rows(v):
    return pltpu.roll(v, 1, 0)


def right(v):
    return pltpu.roll(v, v.shape[1] - 1, 1)


def left(v):
    return pltpu.roll(v, 1, 1)


def tensor_fields(s):
    above, below = up_rows(s), down_rows(s)
    along_x = above + below - 2.0 * s
    along_y = right(s) + left(s) - 2.0 * s
    diff = above - below
    mixed = 0.25 * (right(diff) - left(diff))
    return along_x, along_y, mixed


def adjoint_of(r0, r1, r2):
    cross = 0.25 * (right(r2) - left(r2))
    return (
        up_rows(r0 + cross)
        + down_rows(r0 - cross)
        - 2.0 * r0
        + right(r1)
        + left(r1)
        - 2.0 * r1
    )


def adjoint_square(s):
    def row(k):
        return pltpu.roll(s, -k % FULL, 0)[8 : 8 + PART]

    def column(v, k):
        return pltpu.roll(v, -k % v.shape[1], 1)

    centre = s[8 : 8 + PART]
    near, far = row(1) + row(-1), row(2) + row(-2)
    mixed = 0.0625 * (far - 2.0 * centre)
    both = centre + mixed
    return (
        (far - 4.0 * near + 12.0 * centre - 2.0 * mixed)
        + (column(both, 2) + column(both, -2))
        - 4.0 * (column(centre, 1) + column(centre, -1))
    )


def edge_columns(first, last, side=None):
    lane = iota(first.shape, 1)
    inside = jnp.where(lane < 64, pltpu.roll(first, 32, 1), last)
    if side is None:
        return jnp.where(lane < 32, jnp.zeros_like(first), inside)
    outside = jnp.where(lane < 16, side, pltpu.roll(side, 32, 1))
    return jnp.where(lane < 32, outside, inside)


def edges_of(v):
    width = v.shape[1]
    return edge_columns(v[:, :128], v[:, width - 256 : width - 128], v[:, width - 128 :])


def add_edges(field, message):
    width = field.shape[1]
    lane = iota(message.shape, 1)
    turned = pltpu.roll(message, 96, 1)
    zero = jnp.zeros_like(message)
    first = field[:, :128] + jnp.where(lane < NEAR, message, zero)
    last = field[:, width - 256 : width - 128] + jnp.where(lane >= 128 - NEAR, turned, zero)
    side = field[:, width - 128 :] + jnp.where(
        lane < HALO, turned, jnp.where(lane >= 128 - HALO, message, zero)
    )
    return jnp.concatenate([first, field[:, 128 : width - 256], last, side], axis=1)


def kernel_rows(k_ref, taps_ref):
    layers, span, _ = k_ref.shape
    taps_ref[...] = jnp.zeros(taps_ref.shape, f32)
    for l in range(layers):
        taps_ref[16 * l : 16 * l + span, :span] = k_ref[l].astype(f32)
    shape = (taps_ref.shape[0], WIDE)
    source = iota(shape, 0)
    place = jnp.where(32 * (source >> 4) + (source & 15) == iota(shape, 1), 1.0, 0.0)
    return lax.dot_general(
        taps_ref[...].astype(bf16),
        place.astype(bf16),
        (((0,), (0,)), ((), ())),
        preferred_element_type=f32,
    )


def build_bands(base_ref, bands_ref, span):
    tap = (iota((8, 128), 1) & 31) - iota((8, 128), 0) + 15
    keep = [(tap - 8 * g >= 0) & (tap - 8 * g < span) for g in range(PART // 8)]
    for block in range(WIDE // 128):
        for j in range(span):
            row = jnp.broadcast_to(
                base_ref[j : j + 1, 128 * block : 128 * block + 128], (8, 128)
            )
            moved = [
                jnp.where(
                    keep[g],
                    pltpu.roll(row, (8 * g - 15) % 128, 1, stride=1, stride_axis=0),
                    0.0,
                )
                for g in range(PART // 8)
            ]
            bands_ref[
                j * PART : (j + 1) * PART, 128 * block : 128 * block + 128
            ] = jnp.concatenate(moved, axis=0).astype(bf16)


def scatter_surface(bands, rounded, prod_ref, span, radius):
    width = rounded.shape[1]
    prod_ref[...] = jnp.dot(bands, rounded, preferred_element_type=f32)
    total = prod_ref[radius * PART : (radius + 1) * PART, :]
    for j in range(span):
        if j != radius:
            piece = prod_ref[j * PART : (j + 1) * PART, :]
            total = total + pltpu.roll(piece, (radius - j) % width, 1)
    return total


def fold_side(side, reach):
    lane = iota((8, 128), 1)
    used = (lane < reach) | (lane >= 128 - reach)
    count = 128 // (2 * reach)
    blocks = []
    for first in range(0, PART // 8, count):
        folded = jnp.zeros((8, 128), f32)
        for n, g in enumerate(range(first, min(first + count, PART // 8))):
            piece = jnp.where(used, side[8 * g : 8 * g + 8], 0.0)
            folded = folded + pltpu.roll(piece, reach + 2 * reach * n, 1)
        blocks.append(folded)
    return blocks


def unfold_side(blocks, reach):
    lane = iota((8, 128), 1)
    used = (lane < reach) | (lane >= 128 - reach)
    count = 128 // (2 * reach)
    pieces = []
    for g in range(PART // 8):
        piece = pltpu.roll(blocks[g // count], 128 - reach - 2 * reach * (g % count), 1)
        pieces.append(jnp.where(used, piece, 0.0))
    return jnp.concatenate(pieces, axis=0)


def depth_message_rows(cells_y, reach):
    blocks = -(-(PART // 8) // (128 // (2 * reach)))
    return PART * (cells_y // 128) + 8 * (blocks - 1)


def fold_places(cells_y):
    blocks = cells_y // 128
    return [PART * (n % blocks) + (PART - 1) * (n // blocks) for n in range(8)]


def store_depth_message(out_ref, part, cells_y, reach):
    for start in range(0, cells_y, 128):
        row = PART * (start // 128)
        out_ref[row : row + PART, :] = part[:, start : start + 128]
    folded, *others = fold_side(part[:, cells_y:], reach)
    for n, row in enumerate(fold_places(cells_y)):
        out_ref[row : row + 1, :] = folded[n : n + 1]
    for n, block in enumerate(others):
        row = PART * (cells_y // 128) + 8 * n
        out_ref[row : row + 8, :] = block


def first_kernel(
    labels_hbm, background_hbm, contrasts_hbm, k_hbm,
    out_ref, edge_ref, density_edge_ref, density_ref, bands_ref,
    labels_ref, background_ref, contrasts_ref, k_ref, sems,
    taps_ref, base_ref, prod_ref,
):
    layers, cells_x, cells_y = labels_ref.shape
    span = k_ref.shape[1]
    copies = [
        pltpu.make_async_copy(source, target, sems.at[n])
        for n, (source, target) in enumerate(
            (
                (k_hbm, k_ref),
                (contrasts_hbm, contrasts_ref),
                (labels_hbm, labels_ref),
                (background_hbm, background_ref),
            )
        )
    ]
    for copy in copies:
        copy.start()
    copies[0].wait()
    base_ref[...] = kernel_rows(k_ref, taps_ref)
    build_bands(base_ref, bands_ref, span)
    for copy in copies[1:]:
        copy.wait()
    classes = contrasts_ref.shape[0]
    for l in range(layers):
        label = labels_ref[l]
        value = jnp.full(label.shape, contrasts_ref[0], f32)
        for c in range(1, classes):
            value = jnp.where(label == c, contrasts_ref[c], value)
        density = value + background_ref[l].astype(f32)
        rows = slice(l * cells_x, (l + 1) * cells_x)
        density_ref[rows, :] = density
        density_edge_ref[rows, :] = edge_columns(
            density[:, :128], density[:, cells_y - 128 :]
        )
    lanes = layers * cells_x
    radius = (span - 1) // 2
    width = cells_y + 128
    prod_ref[...] = jnp.dot(
        bands_ref[:, :lanes], density_ref[...].astype(bf16), preferred_element_type=f32
    )
    part = jnp.zeros((PART, width), f32)
    side = jnp.zeros((PART, 128), f32)
    for j in range(span):
        piece = jnp.concatenate([prod_ref[j * PART : (j + 1) * PART, :], side], axis=1)
        shift = (radius - j) % width
        part = part + (pltpu.roll(piece, shift, 1) if shift else piece)
    edge_ref[...] = edges_of(part)
    store_depth_message(out_ref, part, cells_y, NEAR)


def observed_kernel(
    density_edge_ref, observed_hbm, q_ref, edge_ref, observed_ref, obs_ref, sem
):
    cells_y = observed_ref.shape[2]
    copy = pltpu.make_async_copy(observed_hbm, observed_ref, sem)
    copy.start()
    edge_ref[PART:, :] = density_edge_ref[...]
    obs_ref[...] = jnp.zeros(obs_ref.shape, f32)
    copy.wait()
    for k in range(3):
        obs_ref[k, 8 : PART - 8, :cells_y] = observed_ref[k]
    q = adjoint_of(obs_ref[0], obs_ref[1], obs_ref[2])
    q_ref[...] = q
    edge_ref[:PART, :] = edges_of(q)


def transpose_kernel(bands_ref, out_ref):
    out_ref[...] = bands_ref[...].astype(f32).T.astype(bf16)


def rows_kernel(
    part_ref, other_ref, edge_ref, edge_other_ref, q_ref, q_edge_ref,
    sum_ref, up_ref, down_ref, q_out_ref,
    dense_ref, fold_ref,
):
    cells_y = sum_ref.shape[1] - 128
    dense_ref[...] = part_ref[...] + other_ref[...]
    zero = jnp.zeros((1, 128), f32)
    for n, row in enumerate(fold_places(cells_y)):
        fold_ref[n : n + 1, :] = dense_ref[row : row + 1, :]
    folded = [fold_ref[...]]
    for row in range(PART * (cells_y // 128), dense_ref.shape[0], 8):
        folded.append(dense_ref[row : row + 8, :])
    for row in fold_places(cells_y):
        dense_ref[row : row + 1, :] = zero
    for start in range(0, cells_y, 128):
        row = PART * (start // 128)
        sum_ref[:, start : start + 128] = dense_ref[row : row + PART, :]
    sum_ref[:, cells_y:] = unfold_side(folded, NEAR)
    if edge_ref is not None:
        sum_ref[...] = add_edges(sum_ref[...], edge_ref[...] + edge_other_ref[...])
    sub = iota((8, sum_ref.shape[1]), 0)
    up_ref[:8, :] = sum_ref[8:16, :]
    up_ref[8:16, :] = jnp.where(sub >= 1, sum_ref[:8, :], sum_ref[16:24, :])
    down_ref[:8, :] = sum_ref[32:40, :]
    down_ref[8:16, :] = jnp.where(sub < 7, sum_ref[40:48, :], sum_ref[24:32, :])
    if q_ref is not None:
        q_out_ref[...] = add_edges(q_ref[...], q_edge_ref[:PART, :])
        up_ref[16:24, :] = jnp.where(sub < 7, q_out_ref[8:16, :], q_out_ref[:8, :])
        down_ref[16:24, :] = jnp.where(sub >= 1, q_out_ref[32:40, :], q_out_ref[40:48, :])


def full_surface(total, above, below):
    shape = (8, total.shape[1])
    sub = iota(shape, 0)
    zero = jnp.zeros(shape, f32)
    return jnp.concatenate(
        [
            jnp.where(sub == 7, above[8:16], zero),
            total[:8] + above[:8],
            total[8:16] + jnp.where(sub < 7, above[8:16], zero),
            total[16:32],
            total[32:40] + jnp.where(sub >= 1, below[8:16], zero),
            total[40:48] + below[:8],
            jnp.where(sub == 0, below[8:16], zero),
        ],
        axis=0,
    )


def full_q(q, above, below):
    shape = (8, q.shape[1])
    sub = iota(shape, 0)
    zero = jnp.zeros(shape, f32)
    return jnp.concatenate(
        [
            q[:8] + jnp.where(sub >= 1, above[16:24], zero),
            q[8:16] + jnp.where(sub == 0, above[16:24], zero),
            q[16:32],
            q[32:40] + jnp.where(sub == 7, below[16:24], zero),
            q[40:48] + jnp.where(sub < 7, below[16:24], zero),
        ],
        axis=0,
    )


def stack_shifts(adjoint, stack_ref, columns, span, radius):
    for j in range(span):
        shift = (j - radius) % adjoint.shape[1]
        moved = pltpu.roll(adjoint, shift, 1) if shift else adjoint
        stack_ref[j * PART : (j + 1) * PART, columns] = moved[:, columns]


def rounded_adjoint(s, q):
    return (adjoint_square(s) - q).astype(bf16)


def middle_kernel(
    sum_ref, above_ref, below_ref, q_ref, density_ref, edge_ref, bands_ref, turned_ref,
    out_ref, q_out_ref,
    stack_ref, prod_ref, *, span,
):
    radius = (span - 1) // 2
    lanes, cells_y = density_ref.shape
    above, below = above_ref[...], below_ref[...]
    q = full_q(q_ref[...], above, below)
    q_out_ref[...] = q
    adjoint = rounded_adjoint(full_surface(sum_ref[...], above, below), q)
    stack_shifts(adjoint, stack_ref, slice(0, cells_y + 128), span, radius)
    gradient = jnp.dot(turned_ref[:lanes, :], stack_ref[...], preferred_element_type=f32)
    density = density_ref[...] - descent * gradient[:, :cells_y]
    message = edge_ref[PART:, :]
    lane = iota(message.shape, 1)
    outside = jnp.where(lane < 16, pltpu.roll(message, 96, 1), message)
    outside = outside - descent * gradient[:, cells_y:]
    outside = jnp.where((lane < 16) | (lane >= 112), outside, 0.0)
    rounded = jnp.concatenate([density.astype(bf16), outside.astype(bf16)], axis=1)
    part = scatter_surface(bands_ref[:, :lanes], rounded, prod_ref, span, radius)
    store_depth_message(out_ref, part, cells_y, NEAR)


def last_kernel(
    sum_ref, above_ref, below_ref, q_ref, turned_ref, observed_ref,
    residual_hbm, gradient_hbm,
    residual_ref, gradient_ref, sems, full_ref, stack_ref, misfit_ref, *, span,
):
    radius = (span - 1) // 2
    layers, cells_x, cells_y = gradient_ref.shape
    s = full_surface(sum_ref[...], above_ref[...], below_ref[...])
    full_ref[...] = s
    adjoint = rounded_adjoint(s, q_ref[...])
    turned = turned_ref[: layers * cells_x, :]
    half = cells_y // 2
    copies = []
    for n in range(2):
        columns = slice(n * half, (n + 1) * half)
        stack_shifts(adjoint, stack_ref, columns, span, radius)
        gradient = jnp.dot(turned, stack_ref[:, columns], preferred_element_type=f32)
        for l in range(layers):
            gradient_ref[l, :, columns] = gradient[l * cells_x : (l + 1) * cells_x, :]
    copies.append(pltpu.make_async_copy(gradient_ref, gradient_hbm, sems.at[0]))
    copies[-1].start()
    share = residual_ref.shape[1]
    if share % 8 == 0:
        start = pl.multiple_of(lax.axis_index("gz") * share, 8)
        fields = tensor_fields(full_ref[pl.ds(start + 8, share + 16), :])
        for k in range(3):
            residual_ref[k] = (
                fields[k][8 : 8 + share, :cells_y] - observed_ref[k, pl.ds(start, share), :]
            )
    else:
        fields = tensor_fields(full_ref[...])
        for k in range(3):
            misfit_ref[k] = fields[k][16 : 16 + cells_x, :cells_y] - observed_ref[k]
        for start in range(0, cells_x, share):

            @pl.when(lax.axis_index("gz") * share == start)
            def _():
                residual_ref[...] = misfit_ref[:, start : start + share, :]

    copies.append(pltpu.make_async_copy(residual_ref, residual_hbm, sems.at[2]))
    copies[-1].start()
    for copy in copies:
        copy.wait()


def call(kernel, outs, scratch=(), inputs=None, results=pltpu.VMEM):
    made = pl.BlockSpec(memory_space=results)

    def run(*operands):
        spaces = inputs or (pltpu.VMEM,) * len(operands)
        operands = [
            pltpu.with_memory_space_constraint(v, space) if space is pltpu.HBM else v
            for v, space in zip(operands, spaces)
        ]
        return pl.pallas_call(
            kernel,
            out_shape=outs,
            in_specs=[pl.BlockSpec(memory_space=space) for space in spaces],
            out_specs=jax.tree.map(lambda _: made, outs),
            scratch_shapes=[
                pltpu.VMEM(*item) if isinstance(item, tuple) else item for item in scratch
            ],
            compiler_params=pltpu.CompilerParams(vmem_limit_bytes=GRANT),
        )(*operands)

    return run


def shaped(shape, kind=f32):
    return jax.ShapeDtypeStruct(shape, kind)


def swap(value, axis, distance):
    peers = lax.axis_size(axis)
    return lax.ppermute(value, axis, [(i, i ^ distance) for i in range(peers)])


def body(labels, background, contrasts, kernels, observed):
    layers, cells_x, cells_y = labels.shape
    span = kernels.shape[1]
    lanes = layers * cells_x
    width = cells_y + 128
    depth_peers, row_peers = lax.axis_size("gz"), lax.axis_size("gx")
    assert cells_x == 32 and span == 15 and lanes <= 192 and cells_y == 512 and lax.axis_size("gy") == 2
    assert depth_peers & (depth_peers - 1) == 0
    share = cells_x // depth_peers
    upward = [(i, (i - 1) % row_peers) for i in range(row_peers)]
    downward = [(j, i) for i, j in upward]
    full = ((FULL, width), f32)
    prod = ((span * PART, cells_y), f32)
    field = shaped((PART, width))

    def kernel_of(body_of):
        return functools.partial(body_of, span=span)

    message = shaped((depth_message_rows(cells_y, NEAR), 128))
    part, edge, density_edge, density, bands = call(
        first_kernel,
        (
            message,
            shaped((PART, 128)),
            shaped((lanes, 128)),
            shaped((lanes, cells_y)),
            shaped((span * PART, WIDE), bf16),
        ),
        (
            (labels.shape, labels.dtype),
            (background.shape, background.dtype),
            pltpu.SMEM(contrasts.shape, contrasts.dtype),
            (kernels.shape, kernels.dtype),
            pltpu.SemaphoreType.DMA((4,)),
            ((16 * layers, 16), f32),
            ((16, WIDE), f32),
            prod,
        ),
        inputs=(pltpu.HBM,) * 4,
    )(labels, background, contrasts, kernels)
    turned = call(transpose_kernel, shaped((WIDE, span * PART), bf16))(bands)

    distances = [2 << bit for bit in range(depth_peers.bit_length() - 2)] + [1]
    for iteration in range(ITERS):
        scratch = ((part.shape, f32), ((8, 128), f32))
        if iteration == 0:
            other = swap(part, "gz", distances[0])
            edge = swap(edge, "gy", 1)
            edge, density_edge = lax.optimization_barrier((edge, density_edge))
            edge_other = swap(edge, "gz", distances[0])
            q, q_edge, observed = call(
                observed_kernel,
                (field, shaped((PART + lanes, 128)), shaped(observed.shape)),
                (((3, PART, width), f32), pltpu.SemaphoreType.DMA),
                inputs=(pltpu.VMEM, pltpu.HBM),
            )(density_edge, observed)
            others = swap(q_edge, "gy", 1)
            for distance in distances[1:]:
                part, edge = part + other, edge + edge_other
                other = swap(part, "gz", distance)
                edge_other = swap(edge, "gz", distance)
        else:
            for distance in distances[:-1]:
                part = part + swap(part, "gz", distance)
            other = swap(part, "gz", 1)
        if iteration == 0:
            total, up, down, q = call(
                rows_kernel,
                (field, shaped((24, width)), shaped((24, width)), field),
                scratch,
            )(part, other, edge, edge_other, q, others)
        else:
            total, up, down = call(
                lambda a, b, c, d, e, f, g: rows_kernel(
                    a, b, None, None, None, None, c, d, e, None, f, g
                ),
                (field, shaped((16, width)), shaped((16, width))),
                scratch,
            )(part, other)
        below = lax.ppermute(up, "gx", upward)
        above = lax.ppermute(down, "gx", downward)
        if iteration == 0:
            part, q = call(
                kernel_of(middle_kernel),
                (shaped((depth_message_rows(cells_y, NEAR), 128)), field),
                (((span * PART, width), bf16), ((span * PART, width), f32)),
            )(total, above, below, q, density, others, bands, turned)
    return call(
        kernel_of(last_kernel),
        (shaped((3, share, cells_y)), shaped((layers, cells_x, cells_y))),
        (
            ((3, share, cells_y), f32),
            ((layers, cells_x, cells_y), f32),
            pltpu.SemaphoreType.DMA((3,)),
            full,
            ((span * PART, cells_y), bf16),
            ((3, cells_x, cells_y), f32),
        ),
        results=pltpu.HBM,
    )(total, above, below, q, turned, observed)


def solution(mesh):
    placed = (
        P(("runs", "gz"), "gx", "gy"),
        P(("runs", "gz"), "gx", "gy"),
        P("runs"),
        P(("runs", "gz"), None, None),
        P("runs", "gx", "gy"),
    )
    return jax.shard_map(
        body,
        mesh=mesh,
        in_specs=placed,
        out_specs=(P("runs", ("gx", "gz"), "gy"), P(("runs", "gz"), "gx", "gy")),
        check_vma=False,
    )
```
